32 devices in a mesh: subj: 4 (over y, x), slab: 8 (over z, core).
Axes of the slice: x: 2, y: 2, z: 4, core: 2. Of those that a mesh axis runs over, the one named last changes fastest.
Arguments:
- subjects_data: bfloat16 [16384, 16, 512], P('subj', 'slab'), may hold values from -6 to 6
- covariates: bfloat16 [3, 16384], P(None, 'subj'), may hold values from -5 to 5
- permutes: int32 [32, 16384], P(None, 'subj'), may hold values from 0 to 16383, as said below
- brain_mask: int32 [16, 512], P('slab'), may hold values 0 or 1
Outputs:
- smooth_t: float32 [16, 512], P('slab')
- p_values: float32 [16, 512], P('slab')
- perm_peaks: float32 [32], replicated
The draws below stay inside these ranges and needn't reach their ends.
Inputs may be any that keep to these rules, and one draw needn't show every extreme that they name: `permutes`: each row is a permutation of the subjects that maps every aligned block of 256 subjects onto itself.
All inputs are finite; a program needn't handle non-finite values. No bound on the sum of `brain_mask` on one device may be relied on, other than what follows from the above.
Results may differ from the reference program's by a relative error of at most 0.0003.
Values sent between devices are 32-bit elements; how exact they have to be, the bound alone decides.
A program may use at most 64 MiB of HBM per device.

```python
import math
import jax
import jax.numpy as jnp
from jax import lax

BLOCK = 256
PERMS = 32
PX = 16
PY = 32
S = 16384
NZ = 16
PLANE = 512


def draw_permutes(key, part):
    blocks = S // BLOCK
    count_all = PERMS * blocks
    key_list = jax.random.split(key, count_all)

    def shuffle_one(subkey):
        return jax.random.permutation(subkey, BLOCK).astype(jnp.int32)
    perm_rows = jax.vmap(shuffle_one)(key_list)
    offsets = jnp.arange(count_all, dtype=jnp.int32) % blocks * BLOCK
    return (perm_rows + offsets[:, None]).reshape(PERMS, S)


def shared_fields(key):
    base = jax.random.fold_in(key, 7)
    key_offset, key_noise = jax.random.split(base, 2)
    blocks = S // BLOCK
    block_offset = jax.random.uniform(key_offset, (blocks,), jnp.float32, -1.0, 1.0)
    subject_offset = jnp.repeat(block_offset, BLOCK)
    cov_noise = jax.random.normal(key_noise, (3, S), jnp.float32)
    zero_row = jnp.zeros((S,), jnp.float32)
    shifted = cov_noise + jnp.stack([zero_row, subject_offset, zero_row], axis=0)
    return (jnp.clip(shifted, -5.0, 5.0), subject_offset)


def draw_covariates(key, part):
    cov_values, subject_offset = shared_fields(key)
    return cov_values.astype(jnp.bfloat16)


def draw_subjects_data(key, part):
    cov_values, subject_offset = shared_fields(key)
    base = jax.random.fold_in(key, 11)
    key_mean, key_strength, key_region, key_noise = jax.random.split(base, 4)
    voxel_mean = jax.random.uniform(key_mean, (NZ, PLANE), jnp.float32, -0.3, 0.3)
    strength = jax.random.uniform(key_strength, (NZ, PLANE), jnp.float32, 0.0, 0.08)
    region = jax.random.bernoulli(key_region, 0.5, (NZ, PX, 1)).astype(jnp.float32)
    region = jnp.broadcast_to(region, (NZ, PX, PY)).reshape(NZ, PLANE)
    effect = strength * region
    noise = jax.random.normal(key_noise, (S, NZ, PLANE), jnp.float32)
    values = noise + voxel_mean[None] + cov_values[0][:, None, None] * effect[None] + 0.5 * subject_offset[:, None, None]
    return jnp.clip(values, -6.0, 6.0).astype(jnp.bfloat16)


def set_ends(array, key, low, top_value):
    extent = array.shape
    spot = [jax.random.randint(jax.random.fold_in(key, axis), (), 0, extent[axis]) for axis in range(len(extent))]
    array = array.at[tuple(spot)].set(low)
    longest = extent.index(max(extent))
    spot[longest] = (spot[longest] + 1) % extent[longest]
    return array.at[tuple(spot)].set(top_value)


def setup_inputs(seed: int = 0) -> dict:
    keys = jax.random.split(jax.random.key(seed), 5)
    subjects_data = draw_subjects_data(jax.random.fold_in(keys[4], 71), 0)
    covariates = draw_covariates(jax.random.fold_in(keys[4], 71), 0)
    permutes = draw_permutes(jax.random.fold_in(keys[4], 71), 0)
    brain_mask = set_ends((jax.random.randint(keys[3], (NZ, PLANE), 0, 4) < 3).astype(jnp.int32), jax.random.fold_in(keys[3], 1), 0, 1)
    return {"subjects_data": subjects_data, "covariates": covariates, "permutes": permutes, "brain_mask": brain_mask}


gauss_raw = tuple((math.exp(-0.5 * (offset - 2) ** 2) for offset in range(5)))
gauss_taps = tuple((value / sum(gauss_raw) for value in gauss_raw))

def band_weight(gap):
    total = jnp.zeros(gap.shape, jnp.float32)
    for position, weight in enumerate(gauss_taps):
        total = total + weight * (gap == position - 2).astype(jnp.float32)
    return total

def plane_kernel(rows_x, rows_y):
    cell_index = jnp.arange(rows_x * rows_y, dtype=jnp.int32)
    cell_row = cell_index // rows_y
    cell_col = cell_index % rows_y
    row_gap = cell_row[:, None] - cell_row[None, :]
    col_gap = cell_col[:, None] - cell_col[None, :]
    return band_weight(row_gap) * band_weight(col_gap)

def permute_design(permutes, design):
    copies = permutes.shape[0]
    subj_rows = design.shape[1]
    blocks = subj_rows // BLOCK
    local_idx = (permutes % BLOCK).reshape(copies, blocks, BLOCK).transpose(1, 0, 2)
    block_rows = design.reshape(4, blocks, BLOCK).transpose(1, 0, 2)

    def one_block(pair):
        local_part, design_part = pair
        onehot = (local_part[:, :, None] == jnp.arange(BLOCK, dtype=jnp.int32)[None, None, :]).astype(jnp.float32)
        return jnp.einsum('ci,pij->pcj', design_part.astype(jnp.float32), onehot).astype(jnp.bfloat16)
    shuffled = lax.map(one_block, (local_idx, block_rows))
    return shuffled.transpose(1, 2, 0, 3).reshape(copies * 4, subj_rows)

def t_statistics(products, squares, crossed, freedom):
    count_maps = crossed.shape[0] // 4
    width = products.shape[1]
    gram = crossed[0:4]
    chol_z = jnp.linalg.cholesky(gram[1:4, 1:4])
    gamma_fit = jax.scipy.linalg.cho_solve((chol_z, True), products[1:4])
    resid_sq = squares[0] - lax.optimization_barrier(jnp.sum(products[1:4] * gamma_fit, axis=0))
    cross_nuis = crossed.reshape(count_maps, 4, 4)[:, :, 1:4]
    projections = products.reshape(count_maps, 4, width) - jnp.einsum('pkm,mn->pkn', cross_nuis, gamma_fit, precision=lax.Precision.HIGHEST)
    chol_full = jnp.linalg.cholesky(gram)
    inverse = jax.scipy.linalg.cho_solve((chol_full, True), jnp.eye(4, dtype=gram.dtype))
    slope_est = jnp.einsum('k,pkn->pn', inverse[0], projections, precision=lax.Precision.HIGHEST)
    mixed_proj = jnp.einsum('kl,pln->pkn', inverse, projections, precision=lax.Precision.HIGHEST)
    quadratic = lax.optimization_barrier(jnp.sum(projections * mixed_proj, axis=1))
    return slope_est / jnp.sqrt((resid_sq - quadratic) / freedom * inverse[0, 0])

def reference(subjects_data, covariates, permutes, brain_mask):
    ones_row = jnp.ones((1, S), jnp.bfloat16)
    design = jnp.concatenate([covariates[0:1], ones_row, covariates[1:3]], axis=0)
    designs = jnp.concatenate([design, permute_design(permutes, design)], axis=0)
    crossed = jnp.dot(designs.astype(jnp.float32), design.T.astype(jnp.float32), preferred_element_type=jnp.float32)

    def slice_stats(slice_index):
        slice_data = lax.dynamic_index_in_dim(subjects_data, slice_index, 1, keepdims=False)
        products = jnp.dot(designs.astype(jnp.float32), slice_data.astype(jnp.float32), preferred_element_type=jnp.float32)
        squares = lax.optimization_barrier(jnp.sum(jnp.square(slice_data.astype(jnp.float32)), axis=0))[None]
        return t_statistics(products, squares, crossed, S - 4)
    tmaps = lax.map(slice_stats, jnp.arange(NZ, dtype=jnp.int32)).transpose(1, 0, 2)
    mask_float = brain_mask.astype(jnp.float32)
    masked = tmaps * mask_float[None]
    padded = jnp.pad(masked, ((0, 0), (2, 2), (0, 0)))
    depth_smooth = gauss_taps[0] * padded[:, 0:NZ]
    for position in range(1, 5):
        depth_smooth = depth_smooth + gauss_taps[position] * padded[:, position:position + NZ]
    kernel = plane_kernel(PX, PY)
    smoothed = jnp.dot(depth_smooth.reshape(-1, PLANE), kernel, precision=lax.Precision.HIGHEST).reshape(PERMS + 1, NZ, PLANE) * mask_float[None]
    smooth_t = smoothed[0]
    perm_peaks = lax.optimization_barrier(jnp.max(jnp.where(mask_float[None] > 0, smoothed[1:], -1e+30), axis=(1, 2)))
    p_values = mask_float * (1.0 + lax.optimization_barrier(jnp.sum(jax.nn.sigmoid((perm_peaks[:, None, None] - smooth_t[None]) / 0.2), axis=0))) / (PERMS + 1)
    return (smooth_t, p_values, perm_peaks)
```

```python
import functools
import math

import jax
import jax.numpy as jnp
from jax import lax
from jax.experimental import pallas as pl
from jax.experimental.pallas import tpu as pltpu
from jax.sharding import PartitionSpec as P

BLOCK = 256
HALF = 128
PX = 16
PY = 32
LANES = 128
MESH = pl.DeviceIdType.MESH

gauss_raw = tuple((math.exp(-0.5 * (offset - 2) ** 2) for offset in range(5)))
gauss_taps = tuple((value / sum(gauss_raw) for value in gauss_raw))

NT = (((1,), (1,)), ((), ()))


def cholesky(mat):
    size = len(mat)
    low = [[None] * size for _ in range(size)]
    for j in range(size):
        total = mat[j][j]
        for k in range(j):
            total = total - low[j][k] * low[j][k]
        low[j][j] = jnp.sqrt(total)
        for i in range(j + 1, size):
            total = mat[i][j]
            for k in range(j):
                total = total - low[i][k] * low[j][k]
            low[i][j] = total / low[j][j]
    return low


def cho_solve(low, inv_diag, rhs):
    size = len(low)
    half = []
    for i in range(size):
        total = rhs[i]
        for k in range(i):
            total = total - low[i][k] * half[k]
        half.append(total * inv_diag[i])
    out = [None] * size
    for i in reversed(range(size)):
        total = half[i]
        for k in range(i + 1, size):
            total = total - low[k][i] * out[k]
        out[i] = total * inv_diag[i]
    return out


def blur(cells, stride, coord, size):
    width = cells.shape[1]
    total = None
    for position in range(5):
        d = position - 2
        moved = cells if d == 0 else pltpu.roll(cells, (-d * stride) % width, 1)
        inside = (coord + d >= 0) & (coord + d < size)
        term = gauss_taps[position] * jnp.where(inside, moved, 0.0)
        total = term if total is None else total + term
    return total


def batcher(size):
    pairs = []
    p = 1
    while p < size:
        k = p
        while k >= 1:
            for j in range(k % p, size - k, 2 * k):
                for i in range(min(k, size - j - k)):
                    if (i + j) // (2 * p) == (i + j + k) // (2 * p):
                        pairs.append((i + j, i + j + k))
            k //= 2
        p *= 2
    return pairs

def exchange_all(held, step):
    for i in held:
        j = i ^ step
        if i < j:
            held[i], held[j] = jnp.minimum(held[i], held[j]), jnp.maximum(held[i], held[j])

def cosets(gens):
    left = set(range(HALF))
    out = []
    while left:
        group = {min(left)}
        for g in gens:
            group |= {i ^ g for i in group}
        out.append(sorted(group))
        left -= group
    return out

def sort_blocks(rank):
    def load(ids):
        return {i: rank[8 * i : 8 * i + 8, :] for i in ids}
    def save(held):
        for i, v in held.items():
            rank[8 * i : 8 * i + 8, :] = v
    net = batcher(32)
    for ids in cosets([1, 2, 4, 8, 16]):
        held = load(ids)
        for lo, hi in net:
            i, j = ids[lo], ids[hi]
            held[i], held[j] = jnp.minimum(held[i], held[j]), jnp.maximum(held[i], held[j])
        save(held)
    for steps in ([63, 16, 8, 4, 2], [1, 127, 32, 16, 8]):
        for ids in cosets(steps):
            held = load(ids)
            for step in steps:
                exchange_all(held, step)
            save(held)
    upper = lax.broadcasted_iota(jnp.int32, (8, LANES), 0) >= 4
    sign = jnp.where(upper, -1.0, 1.0)
    for ids in cosets([4, 2, 1, 64, 32]):
        held = load(ids)
        for step in (4, 2, 1):
            exchange_all(held, step)
        for i in ids:
            v = held[i]
            held[i] = jnp.minimum(v, -pltpu.roll(v, 4, 0)) * sign
        for step in (64, 32):
            exchange_all(held, step)
        save(held)
    for ids in cosets([16, 8, 4, 2, 1]):
        held = load(ids)
        for step in (16, 8, 4, 2, 1):
            exchange_all(held, step)
        save(held)

def take(table, index):
    return jnp.take_along_axis(table, index, axis=1, mode="promise_in_bounds")

def design_kernel(x_hbm, cov_hbm, perm_hbm, y_ref, des_ref, cross_ref, cov_ref, perm_ref, rank, flat_ref, xsem, csem):
    copies = [pltpu.make_async_copy(perm_hbm, perm_ref, csem.at[0]), pltpu.make_async_copy(cov_hbm, cov_ref, csem.at[1])]
    tiles = x_hbm.shape[1]
    loads = [pltpu.make_async_copy(x_hbm.at[:, c], y_ref.at[c], xsem.at[c]) for c in range(tiles)]
    for c in copies: c.start()
    blocks = perm_ref.shape[1] // BLOCK
    rows = perm_ref.shape[0]
    per = LANES // rows
    lane = lax.broadcasted_iota(jnp.int32, (rows, LANES), 1)
    with jax.named_scope("waitperm"):
        for c in copies: c.wait()
    for c in loads: c.start()
    sub8 = lax.broadcasted_iota(jnp.int32, (8, LANES), 0)
    first_obs = lax.broadcasted_iota(jnp.int32, (16, BLOCK), 0) < 4
    kind = sub8 % 4
    to = lax.broadcasted_iota(jnp.int32, (HALF, 512), 1)
    come = lax.broadcasted_iota(jnp.int32, (HALF, 512), 0)
    spread = jnp.where(to == 2 * come + (to >= 256) * 257, 1.0, 0.0).astype(jnp.bfloat16)
    nb = 4 * per

    def part(s, carry):
        base = s * nb
        with jax.named_scope("intrans"):
            def enter(g, c):
                half, hi = g // 4, g % 4
                got = []
                for bl in range(per):
                    at = (base + hi * per + bl) * BLOCK + half * HALF
                    local = perm_ref[:, pl.ds(pl.multiple_of(at, HALF), HALF)] & (BLOCK - 1)
                    value = (local * BLOCK + lane + half * HALF)
                    got.append(jnp.where(half == 0, value, -value).astype(jnp.float32))
                rank[pl.ds(g, HALF, stride=8), :] = jnp.concatenate(got, axis=0).T
                return c
            for g in range(8): enter(g, 0)
        with jax.named_scope("sort"):
            sort_blocks(rank)
        with jax.named_scope("gather"):
            def leave(hi, c):
                for half in range(2):
                    g = half * 4 + hi
                    turned = rank[pl.ds(g, HALF, stride=8), :].T.astype(jnp.int32)
                    tall = []
                    for bl in range(per):
                        at = (base + hi * per + bl) * BLOCK
                        cov = cov_ref[:, pl.ds(pl.multiple_of(at, BLOCK), BLOCK)].astype(jnp.float32)
                        table = [[jnp.broadcast_to(cov[k : k + 1, h * HALF : h * HALF + HALF], (8, LANES)) for h in range(2)] for k in range(3)]
                        values = []
                        for q in range(rows // 8):
                            r = bl * rows + q * 8
                            index = turned[r : r + 8] & (HALF - 1)
                            low = (turned[r : r + 8] & HALF) == 0
                            for k in range(3):
                                values.append(jnp.where(low, take(table[k][0], index), take(table[k][1], index)))
                        d = [table[k][half] for k in range(3)]
                        values.append(jnp.where(kind == 0, d[0], jnp.where(kind == 1, 1.0, jnp.where(kind == 2, d[1], d[2]))))
                        values.append(jnp.zeros((8, LANES), jnp.float32))
                        tile = jnp.concatenate(values, axis=0).astype(jnp.bfloat16)
                        flat_ref[:, pl.ds(pl.multiple_of(at + half * HALF, HALF), HALF)] = tile
                        tall.append(tile)
                    wide = jnp.dot(jnp.concatenate(tall, axis=0), spread, preferred_element_type=jnp.float32)
                    high = 3 * rows + 16
                    for bl in range(per):
                        at = (base + hi * per + bl) * BLOCK
                        out = pl.ds(pl.multiple_of(2 * at + half * 256, 256), 256)
                        piece = wide[bl * high : (bl + 1) * high]
                        des_ref[0 : 3 * rows, out] = piece[0 : 3 * rows, 0:256].astype(jnp.bfloat16)
                        des_ref[3 * rows : 6 * rows, out] = piece[0 : 3 * rows, 256:512].astype(jnp.bfloat16)
                        seen = jnp.where(first_obs, piece[3 * rows :, 0:256], piece[3 * rows :, 256:512])
                        des_ref[6 * rows :, out] = seen.astype(jnp.bfloat16)
                return c
            lax.fori_loop(0, 4, leave, 0)
        return carry
    if blocks == nb:
        part(0, 0)
    else:
        lax.fori_loop(0, blocks // nb, part, 0)
    with jax.named_scope("crossed"):
        cross_ref[...] = lax.dot_general(flat_ref[...], flat_ref[3 * rows : 3 * rows + 16, :], NT, preferred_element_type=jnp.float32)
    with jax.named_scope("waitx"):
        for c in loads: c.wait()

def maps_kernel(
    n, m, freedom,
    cells_ref, des_ref, cross_ref, mask_ref, smooth_ref, peak_ref,
    out_x, got_x, out_q, got_q, out, got, own, low, high, own_o, low_o, high_o, field, peak_out, peak_in,
    xsend, xrecv, qsend, qrecv, send, recv, hsend, hrecv, psend, precv,
):
    me = lax.axis_index("subj")
    slab = lax.axis_index("slab")
    plane = mask_ref.shape[1]
    rows = (des_ref.shape[0] - 16) // 6
    groups = rows // 8
    share = n // groups
    depth = des_ref.shape[1]
    half_plane = plane // 2
    top = 3 * rows

    barrier = pltpu.get_barrier_semaphore()
    for a in range(n):
        for o in range(m):
            if a + o:
                pl.semaphore_signal(
                    barrier, inc=1, device_id=(lax.rem(me + a, n), lax.rem(slab + o, m)), device_id_type=MESH)

    def source(s):
        return lax.rem(me - s + n, n)

    def exchange(src, dst, send_sem, recv_sem):
        made = []
        for o in range(1, n):
            to = lax.rem(me + o, n)
            made.append(pltpu.make_async_remote_copy(
                src_ref=src(to), dst_ref=dst(o), send_sem=send_sem(o), recv_sem=recv_sem(o),
                device_id=(to, slab), device_id_type=MESH))
            made[-1].start()
        return made

    out_x[...] = jnp.zeros_like(out_x)
    for g in range(n):
        q = g // share
        out_x[g, 0:24, 0:16] = cross_ref[24 * q : 24 * q + 24]
        out_x[g, 24:32, 0:16] = cross_ref[top : top + 8]
    got_x[0] = out_x[me]

    def multiply(h):
        total = None
        for k in range(2):
            at = k * (depth // 2)
            part = jnp.concatenate(
                [cells_ref[pl.ds((2 * h + c) * depth + at, depth // 2), :] for c in range(2)], axis=1)
            term = jnp.dot(
                des_ref[:, at : at + depth // 2], part, preferred_element_type=jnp.float32)
            total = term if total is None else total + term
        return total

    def spread_out(h, acc):
        for g in range(n):
            q = g // share
            out[h, g, 0:24] = acc[24 * q : 24 * q + 24]
            out[h, g, 24:48] = acc[top + 24 * q : top + 24 * q + 24]
            out[h, g, 48:56] = acc[2 * top : 2 * top + 8]
        got[h, 0] = out[h, me]
        return exchange(
            lambda g: out.at[h, g], lambda o: got.at[h, o], lambda o: send.at[h, o], lambda o: recv.at[h, o])

    with jax.named_scope("multiply_first"):
        acc = multiply(0)
    with jax.named_scope("entry_wait"):
        pl.semaphore_wait(barrier, n * m - 1)
    copies_x = exchange(
        lambda g: out_x.at[g], lambda o: got_x.at[o], lambda o: xsend.at[o], lambda o: xrecv.at[o])
    copies_t = [spread_out(0, acc)]

    with jax.named_scope("squares"):
        step = 256

        def square(k, totals):
            new = []
            for c in range(4):
                at = pl.ds(pl.multiple_of(c * depth + k * step, step), step)
                part = cells_ref[at, :].astype(jnp.float32)
                new.append(totals[c] + jnp.sum((part * part).reshape(step // 32, 4, 8, LANES), axis=0))
            return tuple(new)

        totals = lax.fori_loop(
            0, depth // step, square, tuple(jnp.zeros((4, 8, LANES), jnp.float32) for _ in range(4)))
        sub = lax.broadcasted_iota(jnp.int32, (8, LANES), 0)
        packed = jnp.zeros((8, LANES), jnp.float32)
        for c in range(4):
            total = jnp.sum(totals[c], axis=0)
            total = total + pltpu.roll(total, 4, 0)
            total = total + pltpu.roll(total, 2, 0)
            packed = jnp.where(sub // 2 == c, total, packed)
        out_q[...] = packed
        got_q[0] = packed
    copies_q = exchange(
        lambda g: out_q, lambda o: got_q.at[o], lambda o: qsend.at[o], lambda o: qrecv.at[o])
    with jax.named_scope("multiply_second"):
        copies_t.append(spread_out(1, multiply(1)))

    cells = mask_ref[...].astype(jnp.float32)

    with jax.named_scope("gram"):
        for copy in copies_x:
            copy.wait()
        total_x = got_x[source(0)]
        for s in range(1, n):
            total_x = total_x + got_x[source(s)]
        seen_x = total_x[24:32]
        gram = [[seen_x[i : i + 1, j : j + 1] for j in range(4)] for i in range(4)]
        low_z = cholesky([row[1:4] for row in gram[1:4]])
        inv_z = [1.0 / low_z[i][i] for i in range(3)]
        low_f = cholesky(gram)
        inv_diag = [1.0 / low_f[i][i] for i in range(4)]
        unit = [jnp.zeros((1, 1), jnp.float32), jnp.ones((1, 1), jnp.float32)]
        columns = [cho_solve(low_f, inv_diag, [unit[int(i == j)] for i in range(4)]) for j in range(4)]
        inverse = [[columns[j][i] for j in range(4)] for i in range(4)]

    up = (me, lax.rem(slab + 1, m))
    down = (me, lax.rem(slab + m - 1, m))

    def halo(src, dst, h, k, to):
        return pltpu.make_async_remote_copy(
            src_ref=src.at[h], dst_ref=dst.at[h], send_sem=hsend.at[h, k], recv_sem=hrecv.at[h, k],
            device_id=to, device_id_type=MESH)

    rise = [halo(own, low, h, 0, up) for h in range(2)] + [halo(own_o, low_o, h, 1, up) for h in range(2)]
    fall = [halo(own, high, h, 2, down) for h in range(2)] + [halo(own_o, high_o, h, 3, down) for h in range(2)]

    @pl.when(slab == 0)
    def _():
        low[...] = jnp.zeros_like(low)
        low_o[...] = jnp.zeros_like(low_o)

    @pl.when(slab == m - 1)
    def _():
        high[...] = jnp.zeros_like(high)
        high_o[...] = jnp.zeros_like(high_o)

    field[...] = jnp.zeros_like(field)

    for h in range(2):
        with jax.named_scope("take_in"):
            for copy in copies_t[h]:
                copy.wait()
            if h == 0:
                for copy in copies_q:
                    copy.wait()
                total_q = got_q[source(0)]
                for s in range(1, n):
                    total_q = total_q + got_q[source(s)]
        with jax.named_scope("statistic"):
            total = got[h, source(0)]
            for s in range(1, n):
                total = total + got[h, source(s)]
            for z in range(2):
                obs = total[48 + 4 * z : 52 + 4 * z]
                prod = [obs[k : k + 1] for k in range(4)]
                squares = jnp.concatenate(
                    [total_q[4 * h + 2 * c + z : 4 * h + 2 * c + z + 1] for c in range(2)], axis=1)
                fit = cho_solve(low_z, inv_z, prod[1:4])
                resid = squares - (prod[1] * fit[0] + prod[2] * fit[1] + prod[3] * fit[2])

                def statistic(proj):
                    slope = sum(inverse[0][k] * proj[k] for k in range(4))
                    quad = sum(proj[k] * sum(inverse[k][l] * proj[l] for l in range(4)) for k in range(4))
                    return slope / jnp.sqrt((resid - quad) / freedom * inverse[0][0])

                seen = [prod[k] - sum(gram[k][1 + i] * fit[i] for i in range(3)) for k in range(4)]
                mask_row = cells[z : z + 1, h * half_plane : (h + 1) * half_plane]
                cols = slice(z * half_plane, (z + 1) * half_plane)
                own_o[h, :, cols] = statistic(seen) * mask_row
                proj = []
                for c in range(3):
                    first = 24 * z + 8 * c
                    proj.append(total[first : first + 8] - sum(
                        total_x[8 * c : 8 * c + 8, 1 + i : 2 + i] * fit[i] for i in range(3)))
                own[h, :, cols] = statistic([proj[0], seen[1], proj[1], proj[2]]) * mask_row

        @pl.when(slab < m - 1)
        def _():
            rise[h].start()
            rise[2 + h].start()

        @pl.when(slab > 0)
        def _():
            fall[h].start()
            fall[2 + h].start()

    with jax.named_scope("halo_wait"):
        @pl.when(slab > 0)
        def _():
            for copy in rise:
                copy.wait_recv()

        @pl.when(slab < m - 1)
        def _():
            for copy in fall:
                copy.wait_recv()

    with jax.named_scope("blur"):
        def deep(lower, mine, upper):
            slices = []
            for ref in (lower, mine, upper):
                for z in range(2):
                    cols = slice(z * half_plane, (z + 1) * half_plane)
                    slices.append(jnp.concatenate([ref[0, :, cols], ref[1, :, cols]], axis=1))
            return [
                sum(gauss_taps[position] * slices[position + z] for position in range(5))
                for z in range(2)
            ]

        first, second = deep(low, own, high)
        field[0:8, :] = first
        field[8:16, :] = second
        first, second = deep(low_o, own_o, high_o)
        field[16:17, :] = first
        field[17:18, :] = second

        cell = lax.broadcasted_iota(jnp.int32, (24, plane), 1)
        smooth = blur(field[...], PY, cell // PY, PX)
        smooth = blur(smooth, 1, cell % PY, PY)

        peaks = jnp.maximum(
            jnp.max(jnp.where(cells[0:1] > 0, smooth[0:8] * cells[0:1], -1e30), axis=1, keepdims=True),
            jnp.max(jnp.where(cells[1:2] > 0, smooth[8:16] * cells[1:2], -1e30), axis=1, keepdims=True),
        )
        lane = lax.broadcasted_iota(jnp.int32, (8, LANES), 1)
        line = jnp.sum(jnp.where(lane == sub, peaks, 0.0), axis=0, keepdims=True)
        peak_out[...] = line
        peak_in[0, 0] = line
    copies_p = []
    for a in range(n):
        for o in range(m):
            if a + o:
                copies_p.append(pltpu.make_async_remote_copy(
                    src_ref=peak_out, dst_ref=peak_in.at[a, o],
                    send_sem=psend.at[a, o], recv_sem=precv.at[a, o],
                    device_id=(lax.rem(me + a, n), lax.rem(slab + o, m)), device_id_type=MESH))
                copies_p[-1].start()
    seen_t = [smooth[16 + z : 17 + z] * cells[z : z + 1] for z in range(2)]
    smooth_ref[...] = jnp.concatenate(seen_t, axis=0)

    with jax.named_scope("peak_wait"):
        for copy in copies_p:
            copy.wait_recv()
    for a in range(n):
        best = peak_in[a, 0]
        for o in range(1, m):
            best = jnp.maximum(best, peak_in[a, o])
        peak_ref[lax.rem(me - a + n, n)] = best

    with jax.named_scope("send_wait"):
        for copy in copies_p:
            copy.wait_send()

        @pl.when(slab < m - 1)
        def _():
            for copy in rise:
                copy.wait_send()

        @pl.when(slab > 0)
        def _():
            for copy in fall:
                copy.wait_send()


def p_kernel(smooth_ref, peaks_ref, mask_ref, t_ref, pval_ref, line_ref):
    n = peaks_ref.shape[0]
    copies = line_ref.shape[1]
    groups = copies // 8
    share = n // groups
    cells = mask_ref[...].astype(jnp.float32)
    values = smooth_ref[...]
    t_ref[...] = values
    sub = lax.broadcasted_iota(jnp.int32, (8, LANES), 0)
    lane = lax.broadcasted_iota(jnp.int32, (8, LANES), 1)
    line = jnp.zeros((8, LANES), jnp.float32)
    counts = [jnp.zeros((8, values.shape[1]), jnp.float32) for _ in range(2)]
    for q in range(groups):
        best = peaks_ref[q * share]
        for s in range(1, share):
            best = jnp.maximum(best, peaks_ref[q * share + s])
        value = jnp.sum(jnp.where(lane == sub, best, 0.0), axis=1, keepdims=True)
        line = jnp.where(lane == sub + 8 * q, value, line)
        for z in range(2):
            counts[z] = counts[z] + jax.nn.sigmoid((value - values[z : z + 1]) / 0.2)
    total = [jnp.sum(count, axis=0, keepdims=True) for count in counts]
    pval_ref[...] = cells * (1.0 + jnp.concatenate(total, axis=0)) / (copies + 1)
    line_ref[...] = jnp.sum(line, axis=0, keepdims=True)[:, :copies]


def body(n, m, subjects_data, covariates, permutes, brain_mask):
    subj_rows, depth, plane = subjects_data.shape
    copies = permutes.shape[0]
    groups = copies // 8
    nest = 4 * LANES // copies * BLOCK
    assert depth == 2 and plane == PX * PY and n % groups == 0 and subj_rows % nest == 0
    lane_tiles = plane // LANES
    data = subjects_data.reshape(subj_rows, depth, lane_tiles, LANES).transpose(0, 2, 1, 3)
    f32 = jnp.float32
    bf16 = jnp.bfloat16
    vmem = pl.BlockSpec(memory_space=pltpu.VMEM)
    hbm = pl.BlockSpec(memory_space=pltpu.HBM)
    dma = pltpu.SemaphoreType.DMA
    tall = 3 * copies + 16
    cells, designs, crossed = pl.pallas_call(
        design_kernel,
        in_specs=[hbm] * 3,
        out_specs=[vmem] * 3,
        out_shape=[
            pltpu.VMEM((lane_tiles, subj_rows, depth, LANES), bf16),
            pltpu.VMEM((6 * copies + 16, 2 * subj_rows), bf16),
            pltpu.VMEM((tall, 16), f32),
        ],
        scratch_shapes=[
            pltpu.VMEM((3, subj_rows), bf16),
            pltpu.VMEM((copies, subj_rows), jnp.int32),
            pltpu.VMEM((8 * HALF, LANES), f32),
            pltpu.VMEM((tall, subj_rows), bf16),
            dma((lane_tiles,)), dma((2,)),
        ],
        compiler_params=pltpu.CompilerParams(vmem_limit_bytes=32 * 2**20),
        name="designs",
    )(*(pltpu.with_memory_space_constraint(x, pltpu.HBM) for x in (data, covariates, permutes)))
    smooth, peaks = pl.pallas_call(
        functools.partial(maps_kernel, n, m, float(n * subj_rows - 4)),
        in_specs=[vmem] * 4,
        out_specs=[vmem] * 2,
        out_shape=[pltpu.VMEM((depth, plane), f32), pltpu.VMEM((n, 1, LANES), f32)],
        scratch_shapes=[
            pltpu.VMEM((n, 32, LANES), f32),
            pltpu.VMEM((n, 32, LANES), f32),
            pltpu.VMEM((8, LANES), f32),
            pltpu.VMEM((n, 8, LANES), f32),
            pltpu.VMEM((2, n, 56, plane // 2), f32),
            pltpu.VMEM((2, n, 56, plane // 2), f32),
            pltpu.VMEM((2, 8, plane), f32),
            pltpu.VMEM((2, 8, plane), f32),
            pltpu.VMEM((2, 8, plane), f32),
            pltpu.VMEM((2, 1, plane), f32),
            pltpu.VMEM((2, 1, plane), f32),
            pltpu.VMEM((2, 1, plane), f32),
            pltpu.VMEM((24, plane), f32),
            pltpu.VMEM((1, LANES), f32),
            pltpu.VMEM((n, m, 1, LANES), f32),
            dma((n,)), dma((n,)), dma((n,)), dma((n,)), dma((2, n)), dma((2, n)),
            dma((2, 4)), dma((2, 4)), dma((n, m)), dma((n, m)),
        ],
        compiler_params=pltpu.CompilerParams(
            collective_id=0, has_side_effects=True, vmem_limit_bytes=32 * 2**20
        ),
        name="maps",
    )(cells.reshape(subj_rows * depth * lane_tiles, LANES), designs, crossed, brain_mask)
    smooth_t, p_values, line = pl.pallas_call(
        p_kernel,
        in_specs=[vmem] * 3,
        out_specs=[vmem] * 3,
        out_shape=[
            jax.ShapeDtypeStruct((depth, plane), f32),
            jax.ShapeDtypeStruct((depth, plane), f32),
            jax.ShapeDtypeStruct((1, copies), f32),
        ],
        compiler_params=pltpu.CompilerParams(vmem_limit_bytes=8 * 2**20),
        name="p_values",
    )(smooth, peaks, brain_mask)
    return smooth_t, p_values, line.reshape(copies)


def solution(mesh):
    return jax.shard_map(
        functools.partial(body, mesh.shape["subj"], mesh.shape["slab"]),
        mesh=mesh,
        in_specs=(P("subj", "slab", None), P(None, "subj"), P(None, "subj"), P("slab", None)),
        out_specs=(P("slab", None), P("slab", None), P()),
        check_vma=False,
    )
```

```python
import functools
import math

import jax
import jax.numpy as jnp
from jax import lax
from jax.experimental import pallas as pl
from jax.experimental.pallas import tpu as pltpu
from jax.sharding import PartitionSpec as P

BLOCK = 256
HALF = 128
PX = 16
PY = 32
LANES = 128
MESH = pl.DeviceIdType.MESH
NT = (((1,), (1,)), ((), ()))

gauss_raw = tuple((math.exp(-0.5 * (offset - 2) ** 2) for offset in range(5)))
gauss_taps = tuple((value / sum(gauss_raw) for value in gauss_raw))

def cholesky(mat):
    size = len(mat)
    low = [[None] * size for _ in range(size)]
    for j in range(size):
        total = mat[j][j]
        for k in range(j):
            total = total - low[j][k] * low[j][k]
        low[j][j] = jnp.sqrt(total)
        for i in range(j + 1, size):
            total = mat[i][j]
            for k in range(j):
                total = total - low[i][k] * low[j][k]
            low[i][j] = total / low[j][j]
    return low


def cho_solve(low, inv_diag, rhs):
    size = len(low)
    half = []
    for i in range(size):
        total = rhs[i]
        for k in range(i):
            total = total - low[i][k] * half[k]
        half.append(total * inv_diag[i])
    out = [None] * size
    for i in reversed(range(size)):
        total = half[i]
        for k in range(i + 1, size):
            total = total - low[k][i] * out[k]
        out[i] = total * inv_diag[i]
    return out


def blur(cells, stride, coord, size):
    width = cells.shape[1]
    total = None
    for position in range(5):
        d = position - 2
        moved = cells if d == 0 else pltpu.roll(cells, (-d * stride) % width, 1)
        inside = (coord + d >= 0) & (coord + d < size)
        term = gauss_taps[position] * jnp.where(inside, moved, 0.0)
        total = term if total is None else total + term
    return total


def batcher(size):
    pairs = []
    p = 1
    while p < size:
        k = p
        while k >= 1:
            for j in range(k % p, size - k, 2 * k):
                for i in range(min(k, size - j - k)):
                    if (i + j) // (2 * p) == (i + j + k) // (2 * p):
                        pairs.append((i + j, i + j + k))
            k //= 2
        p *= 2
    return pairs

def exchange_all(held, step):
    for i in held:
        j = i ^ step
        if i < j:
            held[i], held[j] = jnp.minimum(held[i], held[j]), jnp.maximum(held[i], held[j])

def cosets(gens):
    left = set(range(HALF))
    out = []
    while left:
        group = {min(left)}
        for g in gens:
            group |= {i ^ g for i in group}
        out.append(sorted(group))
        left -= group
    return out

def sort_blocks(rank):
    def load(ids):
        return {i: rank[8 * i : 8 * i + 8, :] for i in ids}
    def save(held):
        for i, v in held.items():
            rank[8 * i : 8 * i + 8, :] = v
    net = batcher(32)
    for ids in cosets([1, 2, 4, 8, 16]):
        held = load(ids)
        for lo, hi in net:
            i, j = ids[lo], ids[hi]
            held[i], held[j] = jnp.minimum(held[i], held[j]), jnp.maximum(held[i], held[j])
        save(held)
    for steps in ([63, 16, 8, 4, 2], [1, 127, 32, 16, 8]):
        for ids in cosets(steps):
            held = load(ids)
            for step in steps:
                exchange_all(held, step)
            save(held)
    upper = lax.broadcasted_iota(jnp.int32, (8, LANES), 0) >= 4
    sign = jnp.where(upper, -1.0, 1.0)
    for ids in cosets([4, 2, 1, 64, 32]):
        held = load(ids)
        for step in (4, 2, 1):
            exchange_all(held, step)
        for i in ids:
            v = held[i]
            held[i] = jnp.minimum(v, -pltpu.roll(v, 4, 0)) * sign
        for step in (64, 32):
            exchange_all(held, step)
        save(held)
    for ids in cosets([16, 8, 4, 2, 1]):
        held = load(ids)
        for step in (16, 8, 4, 2, 1):
            exchange_all(held, step)
        save(held)

def take(table, index):
    return jnp.take_along_axis(table, index, axis=1, mode="promise_in_bounds")

def design_kernel(x_hbm, cov_hbm, perm_hbm, y_ref, des_ref, cross_ref, cov_ref, perm_ref, rank, flat_ref, xsem, csem):
    pieces = perm_ref.shape[0] // 8
    copies = [
        pltpu.make_async_copy(perm_hbm.at[pl.ds(8 * i, 8)], perm_ref.at[pl.ds(8 * i, 8)], csem.at[i])
        for i in range(pieces)
    ] + [pltpu.make_async_copy(cov_hbm, cov_ref, csem.at[pieces])]
    tiles = x_hbm.shape[1]
    loads = [pltpu.make_async_copy(x_hbm.at[:, c], y_ref.at[c], xsem.at[c]) for c in range(tiles)]
    for c in copies + loads[:1]: c.start()
    blocks = perm_ref.shape[1] // BLOCK
    rows = perm_ref.shape[0]
    per = LANES // rows
    lane = lax.broadcasted_iota(jnp.int32, (rows, LANES), 1)
    with jax.named_scope("waitperm"):
        for c in copies: c.wait()
    for c in loads[1:]: c.start()
    sub8 = lax.broadcasted_iota(jnp.int32, (8, LANES), 0)
    first_obs = lax.broadcasted_iota(jnp.int32, (16, BLOCK), 0) < 4
    kind = sub8 % 4
    to = lax.broadcasted_iota(jnp.int32, (HALF, 512), 1)
    come = lax.broadcasted_iota(jnp.int32, (HALF, 512), 0)
    spread = jnp.where(to == 2 * come + (to >= 256) * 257, 1.0, 0.0).astype(jnp.bfloat16)
    nb = 4 * per

    def part(s, carry):
        base = s * nb
        with jax.named_scope("intrans"):
            def enter(g, c):
                half, hi = g // 4, g % 4
                got = []
                for bl in range(per):
                    at = (base + hi * per + bl) * BLOCK + half * HALF
                    local = perm_ref[:, pl.ds(pl.multiple_of(at, HALF), HALF)] & (BLOCK - 1)
                    value = (local * BLOCK + lane + half * HALF)
                    got.append(jnp.where(half == 0, value, -value).astype(jnp.float32))
                rank[pl.ds(g, HALF, stride=8), :] = jnp.concatenate(got, axis=0).T
                return c
            for g in range(8): enter(g, 0)
        with jax.named_scope("sort"):
            sort_blocks(rank)
        with jax.named_scope("gather"):
            def leave(hi, c):
                for half in range(2):
                    g = half * 4 + hi
                    turned = rank[pl.ds(g, HALF, stride=8), :].T.astype(jnp.int32)
                    tall = []
                    for bl in range(per):
                        at = (base + hi * per + bl) * BLOCK
                        cov = cov_ref[:, pl.ds(pl.multiple_of(at, BLOCK), BLOCK)].astype(jnp.float32)
                        table = [[jnp.broadcast_to(cov[k : k + 1, h * HALF : h * HALF + HALF], (8, LANES)) for h in range(2)] for k in range(3)]
                        values = []
                        for q in range(rows // 8):
                            r = bl * rows + q * 8
                            index = turned[r : r + 8] & (HALF - 1)
                            low = (turned[r : r + 8] & HALF) == 0
                            for k in range(3):
                                values.append(jnp.where(low, take(table[k][0], index), take(table[k][1], index)))
                        d = [table[k][half] for k in range(3)]
                        values.append(jnp.where(kind == 0, d[0], jnp.where(kind == 1, 1.0, jnp.where(kind == 2, d[1], d[2]))))
                        values.append(jnp.zeros((8, LANES), jnp.float32))
                        tile = jnp.concatenate(values, axis=0).astype(jnp.bfloat16)
                        flat_ref[:, pl.ds(pl.multiple_of(at + half * HALF, HALF), HALF)] = tile
                        tall.append(tile)
                    wide = jnp.dot(jnp.concatenate(tall, axis=0), spread, preferred_element_type=jnp.float32)
                    high = 3 * rows + 16
                    for bl in range(per):
                        at = (base + hi * per + bl) * BLOCK
                        out = pl.ds(pl.multiple_of(2 * at + half * 256, 256), 256)
                        piece = wide[bl * high : (bl + 1) * high]
                        des_ref[0 : 3 * rows, out] = piece[0 : 3 * rows, 0:256].astype(jnp.bfloat16)
                        des_ref[3 * rows : 6 * rows, out] = piece[0 : 3 * rows, 256:512].astype(jnp.bfloat16)
                        seen = jnp.where(first_obs, piece[3 * rows :, 0:256], piece[3 * rows :, 256:512])
                        des_ref[6 * rows :, out] = seen.astype(jnp.bfloat16)
                return c
            lax.fori_loop(0, 4, leave, 0)
        return carry
    if blocks == nb:
        part(0, 0)
    else:
        lax.fori_loop(0, blocks // nb, part, 0)
    with jax.named_scope("crossed"):
        cross_ref[...] = jnp.zeros_like(cross_ref)
        high = 3 * rows + 16
        deep = flat_ref.shape[1] // 2
        for k in range(2):
            cols = slice(k * deep, (k + 1) * deep)
            cross_ref[k, :, 0:high] = lax.dot_general(
                flat_ref[3 * rows : high, cols], flat_ref[:, cols], NT, preferred_element_type=jnp.float32)[0:8]
    with jax.named_scope("waitx"):
        for c in loads: c.wait()

def maps_kernel(
    n, m, freedom,
    cells_ref, des_ref, cross_ref, mask_ref, smooth_ref, peak_ref,
    out_x, got_x, out_q, got_q, out, got, own, low, high, own_o, low_o, high_o, parts, field, peak_out, peak_in, turned,
    xsend, xrecv, qsend, qrecv, send, recv, hsend, hrecv, psend, precv,
):
    me = lax.axis_index("subj")
    slab = lax.axis_index("slab")
    plane = mask_ref.shape[1]
    rows = (des_ref.shape[0] - 16) // 6
    groups = rows // 8
    share = n // groups
    depth = des_ref.shape[1]
    half_plane = plane // 2
    top = 3 * rows

    barrier = pltpu.get_barrier_semaphore()
    for a in range(n):
        for o in range(m):
            if a + o:
                pl.semaphore_signal(
                    barrier, inc=1, device_id=(lax.rem(me + a, n), lax.rem(slab + o, m)), device_id_type=MESH)

    def source(s):
        return lax.rem(me - s + n, n)

    def exchange(src, box, send_sem, recv_sem):
        for o in range(1, n):
            to = lax.rem(me + o, n)
            pltpu.make_async_remote_copy(
                src_ref=src(to), dst_ref=box.at[o], send_sem=send_sem, recv_sem=recv_sem,
                device_id=(to, slab), device_id_type=MESH).start()
        rest = box.at[pl.ds(1, n - 1)]
        return pltpu.make_async_remote_copy(
            src_ref=rest, dst_ref=rest, send_sem=send_sem, recv_sem=recv_sem,
            device_id=(lax.rem(me + 1, n), slab), device_id_type=MESH)

    def multiply(h):
        for k in range(2):
            at = k * (depth // 2)
            part = jnp.concatenate(
                [cells_ref[pl.ds((2 * h + c) * depth + at, depth // 2), :] for c in range(2)], axis=1)
            parts[k] = jnp.dot(
                des_ref[:, at : at + depth // 2], part, preferred_element_type=jnp.float32)

    def spread_out(h):
        def piece(first, count):
            return parts[0, first : first + count] + parts[1, first : first + count]

        for g in range(n):
            q = g // share
            out[h, g, 0:24] = piece(24 * q, 24)
            out[h, g, 24:48] = piece(top + 24 * q, 24)
            out[h, g, 48:56] = piece(2 * top, 8)
        got[h, 0] = out[h, me]
        return exchange(lambda g: out.at[h, g], got.at[h], send.at[h], recv.at[h])

    with jax.named_scope("multiply_first"):
        multiply(0)
    with jax.named_scope("entry_wait"):
        pl.semaphore_wait(barrier, n * m - 1)
    out_x[...] = cross_ref[0] + cross_ref[1]
    copies_x = exchange(lambda g: out_x, got_x, xsend.at[0], xrecv.at[0])
    copies_t = [spread_out(0)]
    got_x[0] = out_x[...]

    with jax.named_scope("squares"):
        step = 256

        def square(k, totals):
            new = []
            for c in range(4):
                at = pl.ds(pl.multiple_of(c * depth + k * step, step), step)
                part = cells_ref[at, :].astype(jnp.float32)
                new.append(totals[c] + jnp.sum((part * part).reshape(step // 32, 4, 8, LANES), axis=0))
            return tuple(new)

        totals = lax.fori_loop(
            0, depth // step, square, tuple(jnp.zeros((4, 8, LANES), jnp.float32) for _ in range(4)))
        sub = lax.broadcasted_iota(jnp.int32, (8, LANES), 0)
        packed = jnp.zeros((8, LANES), jnp.float32)
        for c in range(4):
            total = jnp.sum(totals[c], axis=0)
            total = total + pltpu.roll(total, 4, 0)
            total = total + pltpu.roll(total, 2, 0)
            packed = jnp.where(sub // 2 == c, total, packed)
        out_q[...] = packed
        got_q[0] = packed
    copies_q = exchange(lambda g: out_q, got_q, qsend.at[0], qrecv.at[0])
    with jax.named_scope("multiply_second"):
        multiply(1)
        copies_t.append(spread_out(1))

    cells = mask_ref[...].astype(jnp.float32)

    with jax.named_scope("gram"):
        copies_x.wait()
        total_x = got_x[source(0)]
        for s in range(1, n):
            total_x = total_x + got_x[source(s)]
        gram = [[total_x[j : j + 1, top + i : top + i + 1] for j in range(4)] for i in range(4)]
        turned[...] = total_x.T
        mine_x = turned[pl.ds(pl.multiple_of(24 * (me // share), 8), 24), :]
        low_z = cholesky([row[1:4] for row in gram[1:4]])
        inv_z = [1.0 / low_z[i][i] for i in range(3)]
        low_f = cholesky(gram)
        inv_diag = [1.0 / low_f[i][i] for i in range(4)]
        unit = [jnp.zeros((1, 1), jnp.float32), jnp.ones((1, 1), jnp.float32)]
        columns = [cho_solve(low_f, inv_diag, [unit[int(i == j)] for i in range(4)]) for j in range(4)]
        inverse = [[columns[j][i] for j in range(4)] for i in range(4)]

    up = (me, lax.rem(slab + 1, m))
    down = (me, lax.rem(slab + m - 1, m))

    def halo(src, dst, h, k, to):
        return pltpu.make_async_remote_copy(
            src_ref=src.at[h], dst_ref=dst.at[h], send_sem=hsend.at[h, k], recv_sem=hrecv.at[h, k],
            device_id=to, device_id_type=MESH)

    rise = [halo(own, low, h, 0, up) for h in range(2)] + [halo(own_o, low_o, h, 1, up) for h in range(2)]
    fall = [halo(own, high, h, 2, down) for h in range(2)] + [halo(own_o, high_o, h, 3, down) for h in range(2)]

    @pl.when(slab == 0)
    def _():
        low[...] = jnp.zeros_like(low)
        low_o[...] = jnp.zeros_like(low_o)

    @pl.when(slab == m - 1)
    def _():
        high[...] = jnp.zeros_like(high)
        high_o[...] = jnp.zeros_like(high_o)

    field[...] = jnp.zeros_like(field)

    for h in range(2):
        with jax.named_scope("take_in"):
            copies_t[h].wait()
            if h == 0:
                copies_q.wait()
                total_q = got_q[source(0)]
                for s in range(1, n):
                    total_q = total_q + got_q[source(s)]
        with jax.named_scope("statistic"):
            total = got[h, source(0)]
            for s in range(1, n):
                total = total + got[h, source(s)]
            for z in range(2):
                obs = total[48 + 4 * z : 52 + 4 * z]
                prod = [obs[k : k + 1] for k in range(4)]
                squares = jnp.concatenate(
                    [total_q[4 * h + 2 * c + z : 4 * h + 2 * c + z + 1] for c in range(2)], axis=1)
                fit = cho_solve(low_z, inv_z, prod[1:4])
                resid = squares - (prod[1] * fit[0] + prod[2] * fit[1] + prod[3] * fit[2])

                def statistic(proj):
                    slope = sum(inverse[0][k] * proj[k] for k in range(4))
                    quad = sum(proj[k] * sum(inverse[k][l] * proj[l] for l in range(4)) for k in range(4))
                    return slope / jnp.sqrt((resid - quad) / freedom * inverse[0][0])

                seen = [prod[k] - sum(gram[k][1 + i] * fit[i] for i in range(3)) for k in range(4)]
                mask_row = cells[z : z + 1, h * half_plane : (h + 1) * half_plane]
                cols = slice(z * half_plane, (z + 1) * half_plane)
                own_o[h, :, cols] = statistic(seen) * mask_row
                proj = []
                for c in range(3):
                    first = 24 * z + 8 * c
                    proj.append(total[first : first + 8] - sum(
                        mine_x[8 * c : 8 * c + 8, 1 + i : 2 + i] * fit[i] for i in range(3)))
                own[h, :, cols] = statistic([proj[0], seen[1], proj[1], proj[2]]) * mask_row

        @pl.when(slab < m - 1)
        def _():
            rise[h].start()
            rise[2 + h].start()

        @pl.when(slab > 0)
        def _():
            fall[h].start()
            fall[2 + h].start()

    with jax.named_scope("halo_wait"):
        @pl.when(slab > 0)
        def _():
            for copy in rise:
                copy.wait_recv()

        @pl.when(slab < m - 1)
        def _():
            for copy in fall:
                copy.wait_recv()

    with jax.named_scope("blur"):
        def deep(lower, mine, upper):
            slices = []
            for ref in (lower, mine, upper):
                for z in range(2):
                    cols = slice(z * half_plane, (z + 1) * half_plane)
                    slices.append(jnp.concatenate([ref[0, :, cols], ref[1, :, cols]], axis=1))
            return [
                sum(gauss_taps[position] * slices[position + z] for position in range(5))
                for z in range(2)
            ]

        first, second = deep(low, own, high)
        field[0:8, :] = first
        field[8:16, :] = second
        first, second = deep(low_o, own_o, high_o)
        field[16:17, :] = first
        field[17:18, :] = second

        cell = lax.broadcasted_iota(jnp.int32, (24, plane), 1)
        smooth = blur(field[...], PY, cell // PY, PX)
        smooth = blur(smooth, 1, cell % PY, PY)

        peaks = jnp.maximum(
            jnp.max(jnp.where(cells[0:1] > 0, smooth[0:8] * cells[0:1], -1e30), axis=1, keepdims=True),
            jnp.max(jnp.where(cells[1:2] > 0, smooth[8:16] * cells[1:2], -1e30), axis=1, keepdims=True),
        )
        lane = lax.broadcasted_iota(jnp.int32, (8, LANES), 1)
        line = jnp.sum(jnp.where(lane == sub, peaks, 0.0), axis=0, keepdims=True)
        peak_out[...] = line
        peak_in[0] = line
    for a in range(n):
        for o in range(m):
            if a + o:
                pltpu.make_async_remote_copy(
                    src_ref=peak_out, dst_ref=peak_in.at[a * m + o], send_sem=psend.at[0], recv_sem=precv.at[0],
                    device_id=(lax.rem(me + a, n), lax.rem(slab + o, m)), device_id_type=MESH).start()
    rest = peak_in.at[pl.ds(1, n * m - 1)]
    copies_p = pltpu.make_async_remote_copy(
        src_ref=rest, dst_ref=rest, send_sem=psend.at[0], recv_sem=precv.at[0],
        device_id=(lax.rem(me + 1, n), slab), device_id_type=MESH)
    seen_t = [smooth[16 + z : 17 + z] * cells[z : z + 1] for z in range(2)]
    smooth_ref[...] = jnp.concatenate(seen_t, axis=0)

    with jax.named_scope("peak_wait"):
        copies_p.wait_recv()
    for a in range(n):
        best = peak_in[a * m]
        for o in range(1, m):
            best = jnp.maximum(best, peak_in[a * m + o])
        peak_ref[lax.rem(me - a + n, n)] = best

    with jax.named_scope("send_wait"):
        copies_p.wait_send()

        @pl.when(slab < m - 1)
        def _():
            for copy in rise:
                copy.wait_send()

        @pl.when(slab > 0)
        def _():
            for copy in fall:
                copy.wait_send()


def p_kernel(smooth_ref, peaks_ref, mask_ref, t_ref, pval_ref, line_ref):
    n = peaks_ref.shape[0]
    copies = line_ref.shape[1]
    groups = copies // 8
    share = n // groups
    cells = mask_ref[...].astype(jnp.float32)
    values = smooth_ref[...]
    t_ref[...] = values
    sub = lax.broadcasted_iota(jnp.int32, (8, LANES), 0)
    lane = lax.broadcasted_iota(jnp.int32, (8, LANES), 1)
    line = jnp.zeros((8, LANES), jnp.float32)
    counts = [jnp.zeros((8, values.shape[1]), jnp.float32) for _ in range(2)]
    for q in range(groups):
        best = peaks_ref[q * share]
        for s in range(1, share):
            best = jnp.maximum(best, peaks_ref[q * share + s])
        value = jnp.sum(jnp.where(lane == sub, best, 0.0), axis=1, keepdims=True)
        line = jnp.where(lane == sub + 8 * q, value, line)
        for z in range(2):
            counts[z] = counts[z] + jax.nn.sigmoid((value - values[z : z + 1]) / 0.2)
    total = [jnp.sum(count, axis=0, keepdims=True) for count in counts]
    pval_ref[...] = cells * (1.0 + jnp.concatenate(total, axis=0)) / (copies + 1)
    line_ref[...] = jnp.sum(line, axis=0, keepdims=True)[:, :copies]


def body(n, m, subjects_data, covariates, permutes, brain_mask):
    subj_rows, depth, plane = subjects_data.shape
    copies = permutes.shape[0]
    groups = copies // 8
    nest = 4 * LANES // copies * BLOCK
    assert depth == 2 and plane == PX * PY and n % groups == 0 and subj_rows % nest == 0
    lane_tiles = plane // LANES
    data = subjects_data.reshape(subj_rows, depth, lane_tiles, LANES).transpose(0, 2, 1, 3)
    f32 = jnp.float32
    bf16 = jnp.bfloat16
    vmem = pl.BlockSpec(memory_space=pltpu.VMEM)
    hbm = pl.BlockSpec(memory_space=pltpu.HBM)
    dma = pltpu.SemaphoreType.DMA
    tall = 3 * copies + 16
    cells, designs, crossed = pl.pallas_call(
        design_kernel,
        in_specs=[hbm] * 3,
        out_specs=[vmem] * 3,
        out_shape=[
            pltpu.VMEM((lane_tiles, subj_rows, depth, LANES), bf16),
            pltpu.VMEM((6 * copies + 16, 2 * subj_rows), bf16),
            pltpu.VMEM((2, 8, LANES), f32),
        ],
        scratch_shapes=[
            pltpu.VMEM((3, subj_rows), bf16),
            pltpu.VMEM((copies, subj_rows), jnp.int32),
            pltpu.VMEM((8 * HALF, LANES), f32),
            pltpu.VMEM((tall, subj_rows), bf16),
            dma((lane_tiles,)), dma((groups + 1,)),
        ],
        compiler_params=pltpu.CompilerParams(vmem_limit_bytes=32 * 2**20),
        name="designs",
    )(*(pltpu.with_memory_space_constraint(x, pltpu.HBM) for x in (data, covariates, permutes)))
    smooth, peaks = pl.pallas_call(
        functools.partial(maps_kernel, n, m, float(n * subj_rows - 4)),
        in_specs=[vmem] * 4,
        out_specs=[vmem] * 2,
        out_shape=[pltpu.VMEM((depth, plane), f32), pltpu.VMEM((n, 1, LANES), f32)],
        scratch_shapes=[
            pltpu.VMEM((8, LANES), f32),
            pltpu.VMEM((n, 8, LANES), f32),
            pltpu.VMEM((8, LANES), f32),
            pltpu.VMEM((n, 8, LANES), f32),
            pltpu.VMEM((2, n, 56, plane // 2), f32),
            pltpu.VMEM((2, n, 56, plane // 2), f32),
            pltpu.VMEM((2, 8, plane), f32),
            pltpu.VMEM((2, 8, plane), f32),
            pltpu.VMEM((2, 8, plane), f32),
            pltpu.VMEM((2, 1, plane), f32),
            pltpu.VMEM((2, 1, plane), f32),
            pltpu.VMEM((2, 1, plane), f32),
            pltpu.VMEM((2, 6 * copies + 16, plane // 2), f32),
            pltpu.VMEM((24, plane), f32),
            pltpu.VMEM((1, LANES), f32),
            pltpu.VMEM((n * m, 1, LANES), f32),
            pltpu.VMEM((LANES, 8), f32),
            dma((1,)), dma((1,)), dma((1,)), dma((1,)), dma((2,)), dma((2,)),
            dma((2, 4)), dma((2, 4)), dma((1,)), dma((1,)),
        ],
        compiler_params=pltpu.CompilerParams(
            collective_id=0, has_side_effects=True, vmem_limit_bytes=32 * 2**20
        ),
        name="maps",
    )(cells.reshape(subj_rows * depth * lane_tiles, LANES), designs, crossed, brain_mask)
    smooth_t, p_values, line = pl.pallas_call(
        p_kernel,
        in_specs=[vmem] * 3,
        out_specs=[vmem] * 3,
        out_shape=[
            jax.ShapeDtypeStruct((depth, plane), f32),
            jax.ShapeDtypeStruct((depth, plane), f32),
            jax.ShapeDtypeStruct((1, copies), f32),
        ],
        compiler_params=pltpu.CompilerParams(vmem_limit_bytes=8 * 2**20),
        name="p_values",
    )(smooth, peaks, brain_mask)
    return smooth_t, p_values, line.reshape(copies)


def solution(mesh):
    return jax.shard_map(
        functools.partial(body, mesh.shape["subj"], mesh.shape["slab"]),
        mesh=mesh,
        in_specs=(P("subj", "slab", None), P(None, "subj"), P(None, "subj"), P("slab", None)),
        out_specs=(P("slab", None), P("slab", None), P()),
        check_vma=False,
    )
```

```python
import functools
import math

import jax
import jax.numpy as jnp
from jax import lax
from jax.experimental import pallas as pl
from jax.experimental.pallas import tpu as pltpu
from jax.sharding import PartitionSpec as P

BLOCK = 256
HALF = 128
PX = 16
PY = 32
LANES = 128
MESH = pl.DeviceIdType.MESH
NT = (((1,), (1,)), ((), ()))

gauss_raw = tuple((math.exp(-0.5 * (offset - 2) ** 2) for offset in range(5)))
gauss_taps = tuple((value / sum(gauss_raw) for value in gauss_raw))

def cholesky(mat):
    size = len(mat)
    low = [[None] * size for _ in range(size)]
    for j in range(size):
        total = mat[j][j]
        for k in range(j):
            total = total - low[j][k] * low[j][k]
        low[j][j] = jnp.sqrt(total)
        for i in range(j + 1, size):
            total = mat[i][j]
            for k in range(j):
                total = total - low[i][k] * low[j][k]
            low[i][j] = total / low[j][j]
    return low


def cho_solve(low, inv_diag, rhs):
    size = len(low)
    half = []
    for i in range(size):
        total = rhs[i]
        for k in range(i):
            total = total - low[i][k] * half[k]
        half.append(total * inv_diag[i])
    out = [None] * size
    for i in reversed(range(size)):
        total = half[i]
        for k in range(i + 1, size):
            total = total - low[k][i] * out[k]
        out[i] = total * inv_diag[i]
    return out


def blur(cells, stride, coord, size):
    width = cells.shape[1]
    total = None
    for position in range(5):
        d = position - 2
        moved = cells if d == 0 else pltpu.roll(cells, (-d * stride) % width, 1)
        inside = (coord + d >= 0) & (coord + d < size)
        term = gauss_taps[position] * jnp.where(inside, moved, 0.0)
        total = term if total is None else total + term
    return total


def batcher(size):
    pairs = []
    p = 1
    while p < size:
        k = p
        while k >= 1:
            for j in range(k % p, size - k, 2 * k):
                for i in range(min(k, size - j - k)):
                    if (i + j) // (2 * p) == (i + j + k) // (2 * p):
                        pairs.append((i + j, i + j + k))
            k //= 2
        p *= 2
    return pairs

def exchange_all(held, step):
    for i in held:
        j = i ^ step
        if i < j:
            held[i], held[j] = jnp.minimum(held[i], held[j]), jnp.maximum(held[i], held[j])

def cosets(gens):
    left = set(range(HALF))
    out = []
    while left:
        group = {min(left)}
        for g in gens:
            group |= {i ^ g for i in group}
        out.append(sorted(group))
        left -= group
    return out

def sort_blocks(rank):
    def load(ids):
        return {i: rank[8 * i : 8 * i + 8, :] for i in ids}
    def save(held):
        for i, v in held.items():
            rank[8 * i : 8 * i + 8, :] = v
    net = batcher(32)
    for ids in cosets([1, 2, 4, 8, 16]):
        held = load(ids)
        for lo, hi in net:
            i, j = ids[lo], ids[hi]
            held[i], held[j] = jnp.minimum(held[i], held[j]), jnp.maximum(held[i], held[j])
        save(held)
    for steps in ([63, 16, 8, 4, 2], [1, 127, 32, 16, 8]):
        for ids in cosets(steps):
            held = load(ids)
            for step in steps:
                exchange_all(held, step)
            save(held)
    upper = lax.broadcasted_iota(jnp.int32, (8, LANES), 0) >= 4
    sign = jnp.where(upper, -1.0, 1.0)
    for ids in cosets([4, 2, 1, 64, 32]):
        held = load(ids)
        for step in (4, 2, 1):
            exchange_all(held, step)
        for i in ids:
            v = held[i]
            held[i] = jnp.minimum(v, -pltpu.roll(v, 4, 0)) * sign
        for step in (64, 32):
            exchange_all(held, step)
        save(held)
    for ids in cosets([16, 8, 4, 2, 1]):
        held = load(ids)
        for step in (16, 8, 4, 2, 1):
            exchange_all(held, step)
        save(held)

def take(table, index):
    return jnp.take_along_axis(table, index, axis=1, mode="promise_in_bounds")

def sort_permutations(perm_ref, rank_ref):
    rows = perm_ref.shape[0]
    per = LANES // rows
    lane = lax.broadcasted_iota(jnp.int32, (rows, LANES), 1)
    for s in range(rank_ref.shape[0]):
        rank = rank_ref.at[s]
        with jax.named_scope("turn_in"):
            for g in range(8):
                half, hi = g // 4, g % 4
                got = []
                for bl in range(per):
                    at = ((4 * s + hi) * per + bl) * BLOCK + half * HALF
                    local = perm_ref[:, at : at + HALF] & (BLOCK - 1)
                    value = local * BLOCK + lane + half * HALF
                    got.append((-value if half else value).astype(jnp.float32))
                rank[pl.ds(g, HALF, stride=8), :] = jnp.concatenate(got, axis=0).T
        with jax.named_scope("sort"):
            sort_blocks(rank)


def spread_designs(rank_ref, cov_ref, des_ref, flat_ref):
    rows = (des_ref.shape[0] - 16) // 6
    per = LANES // rows
    high = flat_ref.shape[0]
    sub8 = lax.broadcasted_iota(jnp.int32, (8, LANES), 0)
    first_obs = lax.broadcasted_iota(jnp.int32, (16, BLOCK), 0) < 4
    kind = sub8 % 4
    to = lax.broadcasted_iota(jnp.int32, (HALF, 2 * BLOCK), 1)
    come = lax.broadcasted_iota(jnp.int32, (HALF, 2 * BLOCK), 0)
    spread = jnp.where(to == 2 * come + (to >= BLOCK) * (BLOCK + 1), 1.0, 0.0).astype(jnp.bfloat16)

    def leave(step, carry):
        for half in range(2):
            turned = rank_ref[step // 4, pl.ds(half * 4 + step % 4, HALF, stride=8), :].T.astype(jnp.int32)
            tall = []
            for bl in range(per):
                at = (step * per + bl) * BLOCK
                cov = cov_ref[:, pl.ds(pl.multiple_of(at, BLOCK), BLOCK)].astype(jnp.float32)
                table = [
                    [jnp.broadcast_to(cov[k : k + 1, h * HALF : h * HALF + HALF], (8, LANES)) for h in range(2)]
                    for k in range(3)
                ]
                values = []
                for q in range(rows // 8):
                    r = bl * rows + q * 8
                    index = turned[r : r + 8] & (HALF - 1)
                    low = (turned[r : r + 8] & HALF) == 0
                    for k in range(3):
                        values.append(jnp.where(low, take(table[k][0], index), take(table[k][1], index)))
                d = [table[k][half] for k in range(3)]
                values.append(jnp.where(kind == 0, d[0], jnp.where(kind == 1, 1.0, jnp.where(kind == 2, d[1], d[2]))))
                values.append(jnp.zeros((8, LANES), jnp.float32))
                tile = jnp.concatenate(values, axis=0).astype(jnp.bfloat16)
                flat_ref[:, pl.ds(pl.multiple_of(at + half * HALF, HALF), HALF)] = tile
                tall.append(tile)
            wide = jnp.dot(jnp.concatenate(tall, axis=0), spread, preferred_element_type=jnp.float32)
            for bl in range(per):
                at = (step * per + bl) * BLOCK
                out = pl.ds(pl.multiple_of(2 * at + half * BLOCK, BLOCK), BLOCK)
                piece = wide[bl * high : (bl + 1) * high]
                des_ref[0 : 3 * rows, out] = piece[0 : 3 * rows, 0:BLOCK].astype(jnp.bfloat16)
                des_ref[3 * rows : 6 * rows, out] = piece[0 : 3 * rows, BLOCK:].astype(jnp.bfloat16)
                seen = jnp.where(first_obs, piece[3 * rows :, 0:BLOCK], piece[3 * rows :, BLOCK:])
                des_ref[6 * rows :, out] = seen.astype(jnp.bfloat16)
        return carry

    with jax.named_scope("gather"):
        lax.fori_loop(0, 4 * rank_ref.shape[0], leave, 0)


def cross_design(flat_ref, cross_ref):
    high = flat_ref.shape[0]
    with jax.named_scope("crossed"):
        cross_ref[...] = jnp.zeros_like(cross_ref)
        deep = flat_ref.shape[1] // 2
        for k in range(2):
            cols = slice(k * deep, (k + 1) * deep)
            cross_ref[k, :, 0:high] = lax.dot_general(
                flat_ref[high - 16 : high, cols], flat_ref[:, cols], NT, preferred_element_type=jnp.float32)[0:8]


def maps_kernel(
    n, m, freedom,
    x_hbm, cov_hbm, perm_hbm, mask_hbm, smooth_ref, peak_ref,
    mask_ref, staged, cells_ref, cov_ref, perm_ref, rank_ref, des_ref, flat_ref, cross_ref,
    out_x, got_x, out_q, got_q, out, got, own, low, high, own_o, low_o, high_o, parts, field, peak_out, peak_in, turned,
    lsem, csem, psem, xsend, xrecv, qsend, qrecv, send, recv, hsend, hrecv, psend, precv,
):
    me = lax.axis_index("subj")
    slab = lax.axis_index("slab")
    plane = mask_ref.shape[1]
    rows = (des_ref.shape[0] - 16) // 6
    groups = rows // 8
    share = n // groups
    depth = des_ref.shape[1]
    half_plane = plane // 2
    top = 3 * rows

    groups_of_rows = perm_ref.shape[0] // 8
    small = [
        pltpu.make_async_copy(perm_hbm.at[pl.ds(8 * i, 8)], perm_ref.at[pl.ds(8 * i, 8)], csem.at[i])
        for i in range(groups_of_rows)
    ] + [
        pltpu.make_async_copy(cov_hbm, cov_ref, csem.at[groups_of_rows]),
        pltpu.make_async_copy(mask_hbm, mask_ref, csem.at[groups_of_rows + 1]),
    ]
    loads = [pltpu.make_async_copy(x_hbm.at[:, c], staged.at[c], lsem.at[c]) for c in range(4)]
    plain = staged.reshape(cells_ref.shape)
    moves = [
        pltpu.make_async_copy(
            plain.at[pl.ds(c * depth, depth)], cells_ref.at[pl.ds(c * depth, depth)], psem.at[c])
        for c in range(4)
    ]
    for copy in small + loads[:1]:
        copy.start()

    barrier = pltpu.get_barrier_semaphore()
    for a in range(n):
        for o in range(m):
            if a + o:
                pl.semaphore_signal(
                    barrier, inc=1, device_id=(lax.rem(me + a, n), lax.rem(slab + o, m)), device_id_type=MESH)

    with jax.named_scope("perm_wait"):
        for copy in small:
            copy.wait()
    loads[1].start()
    sort_permutations(perm_ref, rank_ref)
    for copy in loads[2:]:
        copy.start()
    spread_designs(rank_ref, cov_ref, des_ref, flat_ref)
    with jax.named_scope("first_load_wait"):
        for c in range(2):
            loads[c].wait()
            moves[c].start()
    cross_design(flat_ref, cross_ref)
    with jax.named_scope("first_move_wait"):
        for c in range(2):
            moves[c].wait()

    def source(s):
        return lax.rem(me - s + n, n)

    def exchange(src, box, send_sem, recv_sem):
        for o in range(1, n):
            to = lax.rem(me + o, n)
            pltpu.make_async_remote_copy(
                src_ref=src(to), dst_ref=box.at[o], send_sem=send_sem, recv_sem=recv_sem,
                device_id=(to, slab), device_id_type=MESH).start()
        rest = box.at[pl.ds(1, n - 1)]
        return pltpu.make_async_remote_copy(
            src_ref=rest, dst_ref=rest, send_sem=send_sem, recv_sem=recv_sem,
            device_id=(lax.rem(me + 1, n), slab), device_id_type=MESH)

    def multiply(h):
        for k in range(2):
            at = k * (depth // 2)
            part = jnp.concatenate(
                [cells_ref[pl.ds((2 * h + c) * depth + at, depth // 2), :] for c in range(2)], axis=1)
            parts[k] = jnp.dot(
                des_ref[:, at : at + depth // 2], part, preferred_element_type=jnp.float32)

    def spread_out(h):
        def piece(first, count):
            return parts[0, first : first + count] + parts[1, first : first + count]

        for g in range(n):
            q = g // share
            out[h, g, 0:24] = piece(24 * q, 24)
            out[h, g, 24:48] = piece(top + 24 * q, 24)
            out[h, g, 48:56] = piece(2 * top, 8)
        got[h, 0] = out[h, me]
        return exchange(lambda g: out.at[h, g], got.at[h], send.at[h], recv.at[h])

    with jax.named_scope("multiply_first"):
        multiply(0)
    with jax.named_scope("entry_wait"):
        pl.semaphore_wait(barrier, n * m - 1)
    out_x[...] = cross_ref[0] + cross_ref[1]
    copies_x = exchange(lambda g: out_x, got_x, xsend.at[0], xrecv.at[0])
    copies_t = [spread_out(0)]
    got_x[0] = out_x[...]

    with jax.named_scope("second_load_wait"):
        for c in range(2, 4):
            loads[c].wait()
            moves[c].start()
        for c in range(2, 4):
            moves[c].wait()
    with jax.named_scope("squares"):
        step = 256

        def square(k, totals):
            new = []
            for c in range(4):
                at = pl.ds(pl.multiple_of(c * depth + k * step, step), step)
                part = cells_ref[at, :].astype(jnp.float32)
                new.append(totals[c] + jnp.sum((part * part).reshape(step // 32, 4, 8, LANES), axis=0))
            return tuple(new)

        totals = lax.fori_loop(
            0, depth // step, square, tuple(jnp.zeros((4, 8, LANES), jnp.float32) for _ in range(4)))
        sub = lax.broadcasted_iota(jnp.int32, (8, LANES), 0)
        packed = jnp.zeros((8, LANES), jnp.float32)
        for c in range(4):
            total = jnp.sum(totals[c], axis=0)
            total = total + pltpu.roll(total, 4, 0)
            total = total + pltpu.roll(total, 2, 0)
            packed = jnp.where(sub // 2 == c, total, packed)
        out_q[...] = packed
        got_q[0] = packed
    copies_q = exchange(lambda g: out_q, got_q, qsend.at[0], qrecv.at[0])
    with jax.named_scope("multiply_second"):
        multiply(1)
        copies_t.append(spread_out(1))

    cells = mask_ref[...].astype(jnp.float32)

    with jax.named_scope("gram"):
        copies_x.wait()
        total_x = got_x[source(0)]
        for s in range(1, n):
            total_x = total_x + got_x[source(s)]
        gram = [[total_x[j : j + 1, top + i : top + i + 1] for j in range(4)] for i in range(4)]
        turned[...] = total_x.T
        mine_x = turned[pl.ds(pl.multiple_of(24 * (me // share), 8), 24), :]
        low_z = cholesky([row[1:4] for row in gram[1:4]])
        inv_z = [1.0 / low_z[i][i] for i in range(3)]
        low_f = cholesky(gram)
        inv_diag = [1.0 / low_f[i][i] for i in range(4)]
        unit = [jnp.zeros((1, 1), jnp.float32), jnp.ones((1, 1), jnp.float32)]
        columns = [cho_solve(low_f, inv_diag, [unit[int(i == j)] for i in range(4)]) for j in range(4)]
        inverse = [[columns[j][i] for j in range(4)] for i in range(4)]

    up = (me, lax.rem(slab + 1, m))
    down = (me, lax.rem(slab + m - 1, m))

    def halo(src, dst, h, k, to):
        return pltpu.make_async_remote_copy(
            src_ref=src.at[h], dst_ref=dst.at[h], send_sem=hsend.at[h, k], recv_sem=hrecv.at[h, k],
            device_id=to, device_id_type=MESH)

    rise = [halo(own, low, h, 0, up) for h in range(2)] + [halo(own_o, low_o, h, 1, up) for h in range(2)]
    fall = [halo(own, high, h, 2, down) for h in range(2)] + [halo(own_o, high_o, h, 3, down) for h in range(2)]

    @pl.when(slab == 0)
    def _():
        low[...] = jnp.zeros_like(low)
        low_o[...] = jnp.zeros_like(low_o)

    @pl.when(slab == m - 1)
    def _():
        high[...] = jnp.zeros_like(high)
        high_o[...] = jnp.zeros_like(high_o)

    field[...] = jnp.zeros_like(field)

    for h in range(2):
        with jax.named_scope("take_in"):
            copies_t[h].wait()
            if h == 0:
                copies_q.wait()
                total_q = got_q[source(0)]
                for s in range(1, n):
                    total_q = total_q + got_q[source(s)]
        with jax.named_scope("statistic"):
            total = got[h, source(0)]
            for s in range(1, n):
                total = total + got[h, source(s)]
            for z in range(2):
                obs = total[48 + 4 * z : 52 + 4 * z]
                prod = [obs[k : k + 1] for k in range(4)]
                squares = jnp.concatenate(
                    [total_q[4 * h + 2 * c + z : 4 * h + 2 * c + z + 1] for c in range(2)], axis=1)
                fit = cho_solve(low_z, inv_z, prod[1:4])
                resid = squares - (prod[1] * fit[0] + prod[2] * fit[1] + prod[3] * fit[2])

                def statistic(proj):
                    slope = sum(inverse[0][k] * proj[k] for k in range(4))
                    quad = sum(proj[k] * sum(inverse[k][l] * proj[l] for l in range(4)) for k in range(4))
                    return slope / jnp.sqrt((resid - quad) / freedom * inverse[0][0])

                seen = [prod[k] - sum(gram[k][1 + i] * fit[i] for i in range(3)) for k in range(4)]
                mask_row = cells[z : z + 1, h * half_plane : (h + 1) * half_plane]
                cols = slice(z * half_plane, (z + 1) * half_plane)
                own_o[h, :, cols] = statistic(seen) * mask_row
                proj = []
                for c in range(3):
                    first = 24 * z + 8 * c
                    proj.append(total[first : first + 8] - sum(
                        mine_x[8 * c : 8 * c + 8, 1 + i : 2 + i] * fit[i] for i in range(3)))
                own[h, :, cols] = statistic([proj[0], seen[1], proj[1], proj[2]]) * mask_row

        @pl.when(slab < m - 1)
        def _():
            rise[h].start()
            rise[2 + h].start()

        @pl.when(slab > 0)
        def _():
            fall[h].start()
            fall[2 + h].start()

    with jax.named_scope("halo_wait"):
        @pl.when(slab > 0)
        def _():
            for copy in rise:
                copy.wait_recv()

        @pl.when(slab < m - 1)
        def _():
            for copy in fall:
                copy.wait_recv()

    with jax.named_scope("blur"):
        def deep(lower, mine, upper):
            slices = []
            for ref in (lower, mine, upper):
                for z in range(2):
                    cols = slice(z * half_plane, (z + 1) * half_plane)
                    slices.append(jnp.concatenate([ref[0, :, cols], ref[1, :, cols]], axis=1))
            return [
                sum(gauss_taps[position] * slices[position + z] for position in range(5))
                for z in range(2)
            ]

        first, second = deep(low, own, high)
        field[0:8, :] = first
        field[8:16, :] = second
        first, second = deep(low_o, own_o, high_o)
        field[16:17, :] = first
        field[17:18, :] = second

        cell = lax.broadcasted_iota(jnp.int32, (24, plane), 1)
        smooth = blur(field[...], PY, cell // PY, PX)
        smooth = blur(smooth, 1, cell % PY, PY)

        peaks = jnp.maximum(
            jnp.max(jnp.where(cells[0:1] > 0, smooth[0:8] * cells[0:1], -1e30), axis=1, keepdims=True),
            jnp.max(jnp.where(cells[1:2] > 0, smooth[8:16] * cells[1:2], -1e30), axis=1, keepdims=True),
        )
        lane = lax.broadcasted_iota(jnp.int32, (8, LANES), 1)
        line = jnp.sum(jnp.where(lane == sub, peaks, 0.0), axis=0, keepdims=True)
        peak_out[...] = line
        peak_in[0] = line
    for a in range(n):
        for o in range(m):
            if a + o:
                pltpu.make_async_remote_copy(
                    src_ref=peak_out, dst_ref=peak_in.at[a * m + o], send_sem=psend.at[0], recv_sem=precv.at[0],
                    device_id=(lax.rem(me + a, n), lax.rem(slab + o, m)), device_id_type=MESH).start()
    rest = peak_in.at[pl.ds(1, n * m - 1)]
    copies_p = pltpu.make_async_remote_copy(
        src_ref=rest, dst_ref=rest, send_sem=psend.at[0], recv_sem=precv.at[0],
        device_id=(lax.rem(me + 1, n), slab), device_id_type=MESH)
    seen_t = [smooth[16 + z : 17 + z] * cells[z : z + 1] for z in range(2)]
    smooth_ref[...] = jnp.concatenate(seen_t, axis=0)

    with jax.named_scope("peak_wait"):
        copies_p.wait_recv()
    for a in range(n):
        best = peak_in[a * m]
        for o in range(1, m):
            best = jnp.maximum(best, peak_in[a * m + o])
        peak_ref[lax.rem(me - a + n, n)] = best

    with jax.named_scope("send_wait"):
        copies_p.wait_send()

        @pl.when(slab < m - 1)
        def _():
            for copy in rise:
                copy.wait_send()

        @pl.when(slab > 0)
        def _():
            for copy in fall:
                copy.wait_send()


def p_kernel(smooth_ref, peaks_ref, mask_ref, t_ref, pval_ref, line_ref):
    n = peaks_ref.shape[0]
    copies = line_ref.shape[1]
    groups = copies // 8
    share = n // groups
    cells = mask_ref[...].astype(jnp.float32)
    values = smooth_ref[...]
    t_ref[...] = values
    sub = lax.broadcasted_iota(jnp.int32, (8, LANES), 0)
    lane = lax.broadcasted_iota(jnp.int32, (8, LANES), 1)
    line = jnp.zeros((8, LANES), jnp.float32)
    counts = [jnp.zeros((8, values.shape[1]), jnp.float32) for _ in range(2)]
    for q in range(groups):
        best = peaks_ref[q * share]
        for s in range(1, share):
            best = jnp.maximum(best, peaks_ref[q * share + s])
        value = jnp.sum(jnp.where(lane == sub, best, 0.0), axis=1, keepdims=True)
        line = jnp.where(lane == sub + 8 * q, value, line)
        for z in range(2):
            counts[z] = counts[z] + jax.nn.sigmoid((value - values[z : z + 1]) / 0.2)
    total = [jnp.sum(count, axis=0, keepdims=True) for count in counts]
    pval_ref[...] = cells * (1.0 + jnp.concatenate(total, axis=0)) / (copies + 1)
    line_ref[...] = jnp.sum(line, axis=0, keepdims=True)[:, :copies]


def body(n, m, subjects_data, covariates, permutes, brain_mask):
    subj_rows, depth, plane = subjects_data.shape
    copies = permutes.shape[0]
    groups = copies // 8
    nest = 4 * LANES // copies * BLOCK
    assert depth == 2 and plane == PX * PY and n % groups == 0 and subj_rows % nest == 0
    lane_tiles = plane // LANES
    data = subjects_data.reshape(subj_rows, depth, lane_tiles, LANES).transpose(0, 2, 1, 3)
    f32 = jnp.float32
    bf16 = jnp.bfloat16
    vmem = pl.BlockSpec(memory_space=pltpu.VMEM)
    hbm = pl.BlockSpec(memory_space=pltpu.HBM)
    dma = pltpu.SemaphoreType.DMA
    tall = 3 * copies + 16
    data, covariates, permutes = (
        pltpu.with_memory_space_constraint(x, pltpu.HBM) for x in (data, covariates, permutes))
    smooth, peaks = pl.pallas_call(
        functools.partial(maps_kernel, n, m, float(n * subj_rows - 4)),
        in_specs=[hbm] * 4,
        out_specs=[vmem] * 2,
        out_shape=[pltpu.VMEM((depth, plane), f32), pltpu.VMEM((n, 1, LANES), f32)],
        scratch_shapes=[
            pltpu.VMEM((depth, plane), jnp.int32),
            pltpu.VMEM((lane_tiles, subj_rows, depth, LANES), bf16),
            pltpu.VMEM((lane_tiles * subj_rows * depth, LANES), bf16),
            pltpu.VMEM((3, subj_rows), bf16),
            pltpu.VMEM((copies, subj_rows), jnp.int32),
            pltpu.VMEM((subj_rows // nest, 8 * HALF, LANES), f32),
            pltpu.VMEM((6 * copies + 16, 2 * subj_rows), bf16),
            pltpu.VMEM((tall, subj_rows), bf16),
            pltpu.VMEM((2, 8, LANES), f32),
            pltpu.VMEM((8, LANES), f32),
            pltpu.VMEM((n, 8, LANES), f32),
            pltpu.VMEM((8, LANES), f32),
            pltpu.VMEM((n, 8, LANES), f32),
            pltpu.VMEM((2, n, 56, plane // 2), f32),
            pltpu.VMEM((2, n, 56, plane // 2), f32),
            pltpu.VMEM((2, 8, plane), f32),
            pltpu.VMEM((2, 8, plane), f32),
            pltpu.VMEM((2, 8, plane), f32),
            pltpu.VMEM((2, 1, plane), f32),
            pltpu.VMEM((2, 1, plane), f32),
            pltpu.VMEM((2, 1, plane), f32),
            pltpu.VMEM((2, 6 * copies + 16, plane // 2), f32),
            pltpu.VMEM((24, plane), f32),
            pltpu.VMEM((1, LANES), f32),
            pltpu.VMEM((n * m, 1, LANES), f32),
            pltpu.VMEM((LANES, 8), f32),
            dma((lane_tiles,)), dma((groups + 2,)), dma((lane_tiles,)),
            dma((1,)), dma((1,)), dma((1,)), dma((1,)), dma((2,)), dma((2,)),
            dma((2, 4)), dma((2, 4)), dma((1,)), dma((1,)),
        ],
        compiler_params=pltpu.CompilerParams(
            collective_id=0, has_side_effects=True, vmem_limit_bytes=48 * 2**20
        ),
        name="maps",
    )(data, covariates, permutes, pltpu.with_memory_space_constraint(brain_mask, pltpu.HBM))
    smooth_t, p_values, line = pl.pallas_call(
        p_kernel,
        in_specs=[vmem] * 3,
        out_specs=[vmem] * 3,
        out_shape=[
            jax.ShapeDtypeStruct((depth, plane), f32),
            jax.ShapeDtypeStruct((depth, plane), f32),
            jax.ShapeDtypeStruct((1, copies), f32),
        ],
        compiler_params=pltpu.CompilerParams(vmem_limit_bytes=8 * 2**20),
        name="p_values",
    )(smooth, peaks, brain_mask)
    return smooth_t, p_values, line.reshape(copies)


def solution(mesh):
    return jax.shard_map(
        functools.partial(body, mesh.shape["subj"], mesh.shape["slab"]),
        mesh=mesh,
        in_specs=(P("subj", "slab", None), P(None, "subj"), P(None, "subj"), P("slab", None)),
        out_specs=(P("slab", None), P("slab", None), P()),
        check_vma=False,
    )
```

```python
import functools
import math

import jax
import jax.numpy as jnp
from jax import lax
from jax.experimental import pallas as pl
from jax.experimental.pallas import tpu as pltpu
from jax.sharding import PartitionSpec as P

BLOCK = 256
HALF = 128
PX = 16
PY = 32
LANES = 128
MESH = pl.DeviceIdType.MESH
NT = (((1,), (1,)), ((), ()))

gauss_raw = tuple((math.exp(-0.5 * (offset - 2) ** 2) for offset in range(5)))
gauss_taps = tuple((value / sum(gauss_raw) for value in gauss_raw))

def cholesky(mat):
    size = len(mat)
    low = [[None] * size for _ in range(size)]
    for j in range(size):
        total = mat[j][j]
        for k in range(j):
            total = total - low[j][k] * low[j][k]
        low[j][j] = jnp.sqrt(total)
        for i in range(j + 1, size):
            total = mat[i][j]
            for k in range(j):
                total = total - low[i][k] * low[j][k]
            low[i][j] = total / low[j][j]
    return low


def cho_solve(low, inv_diag, rhs):
    size = len(low)
    half = []
    for i in range(size):
        total = rhs[i]
        for k in range(i):
            total = total - low[i][k] * half[k]
        half.append(total * inv_diag[i])
    out = [None] * size
    for i in reversed(range(size)):
        total = half[i]
        for k in range(i + 1, size):
            total = total - low[k][i] * out[k]
        out[i] = total * inv_diag[i]
    return out


def blur(cells, stride, coord, size):
    width = cells.shape[1]
    total = None
    for position in range(5):
        d = position - 2
        moved = cells if d == 0 else pltpu.roll(cells, (-d * stride) % width, 1)
        inside = (coord + d >= 0) & (coord + d < size)
        term = gauss_taps[position] * jnp.where(inside, moved, 0.0)
        total = term if total is None else total + term
    return total


def batcher(size):
    pairs = []
    p = 1
    while p < size:
        k = p
        while k >= 1:
            for j in range(k % p, size - k, 2 * k):
                for i in range(min(k, size - j - k)):
                    if (i + j) // (2 * p) == (i + j + k) // (2 * p):
                        pairs.append((i + j, i + j + k))
            k //= 2
        p *= 2
    return pairs

def exchange_all(held, step):
    for i in held:
        j = i ^ step
        if i < j:
            held[i], held[j] = jnp.minimum(held[i], held[j]), jnp.maximum(held[i], held[j])

def cosets(gens):
    left = set(range(HALF))
    out = []
    while left:
        group = {min(left)}
        for g in gens:
            group |= {i ^ g for i in group}
        out.append(sorted(group))
        left -= group
    return out

def sort_blocks(rank):
    def load(ids):
        return {i: rank[8 * i : 8 * i + 8, :] for i in ids}
    def save(held):
        for i, v in held.items():
            rank[8 * i : 8 * i + 8, :] = v
    net = batcher(32)
    for ids in cosets([1, 2, 4, 8, 16]):
        held = load(ids)
        for lo, hi in net:
            i, j = ids[lo], ids[hi]
            held[i], held[j] = jnp.minimum(held[i], held[j]), jnp.maximum(held[i], held[j])
        save(held)
    for steps in ([63, 16, 8, 4, 2], [1, 127, 32, 16, 8]):
        for ids in cosets(steps):
            held = load(ids)
            for step in steps:
                exchange_all(held, step)
            save(held)
    upper = lax.broadcasted_iota(jnp.int32, (8, LANES), 0) >= 4
    sign = jnp.where(upper, -1.0, 1.0)
    for ids in cosets([4, 2, 1, 64, 32]):
        held = load(ids)
        for step in (4, 2, 1):
            exchange_all(held, step)
        for i in ids:
            v = held[i]
            held[i] = jnp.minimum(v, -pltpu.roll(v, 4, 0)) * sign
        for step in (64, 32):
            exchange_all(held, step)
        save(held)
    for ids in cosets([16, 8, 4, 2, 1]):
        held = load(ids)
        for step in (16, 8, 4, 2, 1):
            exchange_all(held, step)
        save(held)

def take(table, index):
    return jnp.take_along_axis(table, index, axis=1, mode="promise_in_bounds")

def sort_permutations(perm_ref, rank_ref):
    rows = perm_ref.shape[0]
    per = LANES // rows
    lane = lax.broadcasted_iota(jnp.int32, (rows, LANES), 1)
    for s in range(rank_ref.shape[0]):
        rank = rank_ref.at[s]
        with jax.named_scope("turn_in"):
            for g in range(8):
                half, hi = g // 4, g % 4
                got = []
                for bl in range(per):
                    at = ((4 * s + hi) * per + bl) * BLOCK + half * HALF
                    local = perm_ref[:, at : at + HALF] & (BLOCK - 1)
                    value = local * BLOCK + lane + half * HALF
                    got.append((-value if half else value).astype(jnp.float32))
                rank[pl.ds(g, HALF, stride=8), :] = jnp.concatenate(got, axis=0).T
        with jax.named_scope("sort"):
            sort_blocks(rank)


def spread_designs(rank_ref, cov_ref, des_ref, flat_ref, between):
    rows = (des_ref.shape[0] - 16) // 6
    per = LANES // rows
    high = flat_ref.shape[0]
    sub8 = lax.broadcasted_iota(jnp.int32, (8, LANES), 0)
    first_obs = lax.broadcasted_iota(jnp.int32, (16, BLOCK), 0) < 4
    kind = sub8 % 4
    to = lax.broadcasted_iota(jnp.int32, (HALF, 2 * BLOCK), 1)
    come = lax.broadcasted_iota(jnp.int32, (HALF, 2 * BLOCK), 0)
    spread = jnp.where(to == 2 * come + (to >= BLOCK) * (BLOCK + 1), 1.0, 0.0).astype(jnp.bfloat16)

    def leave(step):
        for half in range(2):
            turned = rank_ref[step // 4, pl.ds(half * 4 + step % 4, HALF, stride=8), :].T.astype(jnp.int32)
            tall = []
            for bl in range(per):
                at = (step * per + bl) * BLOCK
                cov = cov_ref[:, pl.ds(pl.multiple_of(at, BLOCK), BLOCK)].astype(jnp.float32)
                table = [
                    [jnp.broadcast_to(cov[k : k + 1, h * HALF : h * HALF + HALF], (8, LANES)) for h in range(2)]
                    for k in range(3)
                ]
                values = []
                for q in range(rows // 8):
                    r = bl * rows + q * 8
                    index = turned[r : r + 8] & (HALF - 1)
                    low = (turned[r : r + 8] & HALF) == 0
                    for k in range(3):
                        values.append(jnp.where(low, take(table[k][0], index), take(table[k][1], index)))
                d = [table[k][half] for k in range(3)]
                values.append(jnp.where(kind == 0, d[0], jnp.where(kind == 1, 1.0, jnp.where(kind == 2, d[1], d[2]))))
                values.append(jnp.zeros((8, LANES), jnp.float32))
                tile = jnp.concatenate(values, axis=0).astype(jnp.bfloat16)
                flat_ref[:, pl.ds(pl.multiple_of(at + half * HALF, HALF), HALF)] = tile
                tall.append(tile)
            wide = jnp.dot(jnp.concatenate(tall, axis=0), spread, preferred_element_type=jnp.float32)
            for bl in range(per):
                at = (step * per + bl) * BLOCK
                out = pl.ds(pl.multiple_of(2 * at + half * BLOCK, BLOCK), BLOCK)
                piece = wide[bl * high : (bl + 1) * high]
                des_ref[0 : 3 * rows, out] = piece[0 : 3 * rows, 0:BLOCK].astype(jnp.bfloat16)
                des_ref[3 * rows : 6 * rows, out] = piece[0 : 3 * rows, BLOCK:].astype(jnp.bfloat16)
                seen = jnp.where(first_obs, piece[3 * rows :, 0:BLOCK], piece[3 * rows :, BLOCK:])
                des_ref[6 * rows :, out] = seen.astype(jnp.bfloat16)

    for step in range(4 * rank_ref.shape[0]):
        leave(step)
        between(step)


def cross_design(flat_ref, cross_ref):
    high = flat_ref.shape[0]
    with jax.named_scope("crossed"):
        cross_ref[...] = jnp.zeros_like(cross_ref)
        deep = flat_ref.shape[1] // 2
        for k in range(2):
            cols = slice(k * deep, (k + 1) * deep)
            cross_ref[k, :, 0:high] = lax.dot_general(
                flat_ref[high - 16 : high, cols], flat_ref[:, cols], NT, preferred_element_type=jnp.float32)[0:8]


def maps_kernel(
    n, m, freedom,
    x_hbm, cov_hbm, perm_hbm, mask_hbm, smooth_ref, peak_ref,
    mask_ref, staged, cells_ref, cov_ref, perm_ref, rank_ref, des_ref, flat_ref, cross_ref,
    out_x, got_x, out_q, got_q, out, got, own, low, high, own_o, low_o, high_o, parts, field, peak_out, peak_in, turned,
    lsem, csem, psem, xsend, xrecv, qsend, qrecv, send, recv, hsend, hrecv, psend, precv,
):
    me = lax.axis_index("subj")
    slab = lax.axis_index("slab")
    plane = mask_ref.shape[1]
    rows = (des_ref.shape[0] - 16) // 6
    groups = rows // 8
    share = n // groups
    depth = des_ref.shape[1]
    half_plane = plane // 2
    top = 3 * rows

    groups_of_rows = perm_ref.shape[0] // 8
    small = [
        pltpu.make_async_copy(perm_hbm.at[pl.ds(8 * i, 8)], perm_ref.at[pl.ds(8 * i, 8)], csem.at[i])
        for i in range(groups_of_rows)
    ] + [
        pltpu.make_async_copy(cov_hbm, cov_ref, csem.at[groups_of_rows]),
        pltpu.make_async_copy(mask_hbm, mask_ref, csem.at[groups_of_rows + 1]),
    ]
    loads = [pltpu.make_async_copy(x_hbm.at[:, c], staged.at[c], lsem.at[c]) for c in range(4)]
    plain = staged.reshape(cells_ref.shape)
    moves = [
        pltpu.make_async_copy(
            plain.at[pl.ds(c * depth, depth)], cells_ref.at[pl.ds(c * depth, depth)], psem.at[c])
        for c in range(4)
    ]
    for copy in small + loads[:1]:
        copy.start()

    barrier = pltpu.get_barrier_semaphore()
    for a in range(n):
        for o in range(m):
            if a + o:
                pl.semaphore_signal(
                    barrier, inc=1, device_id=(lax.rem(me + a, n), lax.rem(slab + o, m)), device_id_type=MESH)

    with jax.named_scope("perm_wait"):
        for copy in small:
            copy.wait()
    loads[1].start()
    sort_permutations(perm_ref, rank_ref)
    for copy in loads[2:]:
        copy.start()
    chunks = 4 * rank_ref.shape[0]
    span = depth // chunks

    def add_product(h, chunk):
        for k in range(2):
            at = chunk * span + k * (span // 2)
            part = jnp.concatenate(
                [cells_ref[pl.ds((2 * h + c) * depth + at, span // 2), :] for c in range(2)], axis=1)
            term = jnp.dot(
                des_ref[:, at : at + span // 2], part, preferred_element_type=jnp.float32)
            parts[k] = parts[k] + term if chunk else term

    def between(step):
        if step:
            add_product(0, step - 1)
        else:
            for c in range(2):
                loads[c].wait()
                moves[c].start()
            for c in range(2):
                moves[c].wait()

    with jax.named_scope("gather"):
        spread_designs(rank_ref, cov_ref, des_ref, flat_ref, between)

    def source(s):
        return lax.rem(me - s + n, n)

    def exchange(src, box, send_sem, recv_sem):
        for o in range(1, n):
            to = lax.rem(me + o, n)
            pltpu.make_async_remote_copy(
                src_ref=src(to), dst_ref=box.at[o], send_sem=send_sem, recv_sem=recv_sem,
                device_id=(to, slab), device_id_type=MESH).start()
        rest = box.at[pl.ds(1, n - 1)]
        return pltpu.make_async_remote_copy(
            src_ref=rest, dst_ref=rest, send_sem=send_sem, recv_sem=recv_sem,
            device_id=(lax.rem(me + 1, n), slab), device_id_type=MESH)

    def multiply(h):
        for k in range(2):
            at = k * (depth // 2)
            part = jnp.concatenate(
                [cells_ref[pl.ds((2 * h + c) * depth + at, depth // 2), :] for c in range(2)], axis=1)
            parts[k] = jnp.dot(
                des_ref[:, at : at + depth // 2], part, preferred_element_type=jnp.float32)

    def spread_out(h):
        def piece(first, count):
            return parts[0, first : first + count] + parts[1, first : first + count]

        for g in range(n):
            q = g // share
            out[h, g, 0:24] = piece(24 * q, 24)
            out[h, g, 24:48] = piece(top + 24 * q, 24)
            out[h, g, 48:56] = piece(2 * top, 8)
        got[h, 0] = out[h, me]
        return exchange(lambda g: out.at[h, g], got.at[h], send.at[h], recv.at[h])

    with jax.named_scope("multiply_first"):
        add_product(0, chunks - 1)
    with jax.named_scope("entry_wait"):
        pl.semaphore_wait(barrier, n * m - 1)
    copies_t = [spread_out(0)]
    cross_design(flat_ref, cross_ref)
    out_x[...] = cross_ref[0] + cross_ref[1]
    copies_x = exchange(lambda g: out_x, got_x, xsend.at[0], xrecv.at[0])
    got_x[0] = out_x[...]

    with jax.named_scope("second_load_wait"):
        for c in range(2, 4):
            loads[c].wait()
            moves[c].start()
        for c in range(2, 4):
            moves[c].wait()
    with jax.named_scope("squares"):
        step = 256

        def square(k, totals):
            new = []
            for c in range(4):
                at = pl.ds(pl.multiple_of(c * depth + k * step, step), step)
                part = cells_ref[at, :].astype(jnp.float32)
                new.append(totals[c] + jnp.sum((part * part).reshape(step // 32, 4, 8, LANES), axis=0))
            return tuple(new)

        totals = lax.fori_loop(
            0, depth // step, square, tuple(jnp.zeros((4, 8, LANES), jnp.float32) for _ in range(4)))
        sub = lax.broadcasted_iota(jnp.int32, (8, LANES), 0)
        packed = jnp.zeros((8, LANES), jnp.float32)
        for c in range(4):
            total = jnp.sum(totals[c], axis=0)
            total = total + pltpu.roll(total, 4, 0)
            total = total + pltpu.roll(total, 2, 0)
            packed = jnp.where(sub // 2 == c, total, packed)
        out_q[...] = packed
        got_q[0] = packed
    copies_q = exchange(lambda g: out_q, got_q, qsend.at[0], qrecv.at[0])
    with jax.named_scope("multiply_second"):
        multiply(1)
        copies_t.append(spread_out(1))

    cells = mask_ref[...].astype(jnp.float32)

    with jax.named_scope("gram"):
        copies_x.wait()
        total_x = got_x[source(0)]
        for s in range(1, n):
            total_x = total_x + got_x[source(s)]
        gram = [[total_x[j : j + 1, top + i : top + i + 1] for j in range(4)] for i in range(4)]
        turned[...] = total_x.T
        mine_x = turned[pl.ds(pl.multiple_of(24 * (me // share), 8), 24), :]
        low_z = cholesky([row[1:4] for row in gram[1:4]])
        inv_z = [1.0 / low_z[i][i] for i in range(3)]
        low_f = cholesky(gram)
        inv_diag = [1.0 / low_f[i][i] for i in range(4)]
        unit = [jnp.zeros((1, 1), jnp.float32), jnp.ones((1, 1), jnp.float32)]
        columns = [cho_solve(low_f, inv_diag, [unit[int(i == j)] for i in range(4)]) for j in range(4)]
        inverse = [[columns[j][i] for j in range(4)] for i in range(4)]

    up = (me, lax.rem(slab + 1, m))
    down = (me, lax.rem(slab + m - 1, m))

    def halo(src, dst, h, k, to):
        return pltpu.make_async_remote_copy(
            src_ref=src.at[h], dst_ref=dst.at[h], send_sem=hsend.at[h, k], recv_sem=hrecv.at[h, k],
            device_id=to, device_id_type=MESH)

    rise = [halo(own, low, h, 0, up) for h in range(2)] + [halo(own_o, low_o, h, 1, up) for h in range(2)]
    fall = [halo(own, high, h, 2, down) for h in range(2)] + [halo(own_o, high_o, h, 3, down) for h in range(2)]

    @pl.when(slab == 0)
    def _():
        low[...] = jnp.zeros_like(low)
        low_o[...] = jnp.zeros_like(low_o)

    @pl.when(slab == m - 1)
    def _():
        high[...] = jnp.zeros_like(high)
        high_o[...] = jnp.zeros_like(high_o)

    field[...] = jnp.zeros_like(field)

    for h in range(2):
        with jax.named_scope("take_in"):
            copies_t[h].wait()
            if h == 0:
                copies_q.wait()
                total_q = got_q[source(0)]
                for s in range(1, n):
                    total_q = total_q + got_q[source(s)]
        with jax.named_scope("statistic"):
            total = got[h, source(0)]
            for s in range(1, n):
                total = total + got[h, source(s)]
            for z in range(2):
                obs = total[48 + 4 * z : 52 + 4 * z]
                prod = [obs[k : k + 1] for k in range(4)]
                squares = jnp.concatenate(
                    [total_q[4 * h + 2 * c + z : 4 * h + 2 * c + z + 1] for c in range(2)], axis=1)
                fit = cho_solve(low_z, inv_z, prod[1:4])
                resid = squares - (prod[1] * fit[0] + prod[2] * fit[1] + prod[3] * fit[2])

                def statistic(proj):
                    slope = sum(inverse[0][k] * proj[k] for k in range(4))
                    quad = sum(proj[k] * sum(inverse[k][l] * proj[l] for l in range(4)) for k in range(4))
                    return slope / jnp.sqrt((resid - quad) / freedom * inverse[0][0])

                seen = [prod[k] - sum(gram[k][1 + i] * fit[i] for i in range(3)) for k in range(4)]
                mask_row = cells[z : z + 1, h * half_plane : (h + 1) * half_plane]
                cols = slice(z * half_plane, (z + 1) * half_plane)
                own_o[h, :, cols] = statistic(seen) * mask_row
                proj = []
                for c in range(3):
                    first = 24 * z + 8 * c
                    proj.append(total[first : first + 8] - sum(
                        mine_x[8 * c : 8 * c + 8, 1 + i : 2 + i] * fit[i] for i in range(3)))
                own[h, :, cols] = statistic([proj[0], seen[1], proj[1], proj[2]]) * mask_row

        @pl.when(slab < m - 1)
        def _():
            rise[h].start()
            rise[2 + h].start()

        @pl.when(slab > 0)
        def _():
            fall[h].start()
            fall[2 + h].start()

    with jax.named_scope("halo_wait"):
        @pl.when(slab > 0)
        def _():
            for copy in rise:
                copy.wait_recv()

        @pl.when(slab < m - 1)
        def _():
            for copy in fall:
                copy.wait_recv()

    with jax.named_scope("blur"):
        def deep(lower, mine, upper):
            slices = []
            for ref in (lower, mine, upper):
                for z in range(2):
                    cols = slice(z * half_plane, (z + 1) * half_plane)
                    slices.append(jnp.concatenate([ref[0, :, cols], ref[1, :, cols]], axis=1))
            return [
                sum(gauss_taps[position] * slices[position + z] for position in range(5))
                for z in range(2)
            ]

        first, second = deep(low, own, high)
        field[0:8, :] = first
        field[8:16, :] = second
        first, second = deep(low_o, own_o, high_o)
        field[16:17, :] = first
        field[17:18, :] = second

        cell = lax.broadcasted_iota(jnp.int32, (24, plane), 1)
        smooth = blur(field[...], PY, cell // PY, PX)
        smooth = blur(smooth, 1, cell % PY, PY)

        peaks = jnp.maximum(
            jnp.max(jnp.where(cells[0:1] > 0, smooth[0:8] * cells[0:1], -1e30), axis=1, keepdims=True),
            jnp.max(jnp.where(cells[1:2] > 0, smooth[8:16] * cells[1:2], -1e30), axis=1, keepdims=True),
        )
        lane = lax.broadcasted_iota(jnp.int32, (8, LANES), 1)
        line = jnp.sum(jnp.where(lane == sub, peaks, 0.0), axis=0, keepdims=True)
        peak_out[...] = line
        peak_in[0] = line
    for a in range(n):
        for o in range(m):
            if a + o:
                pltpu.make_async_remote_copy(
                    src_ref=peak_out, dst_ref=peak_in.at[a * m + o], send_sem=psend.at[0], recv_sem=precv.at[0],
                    device_id=(lax.rem(me + a, n), lax.rem(slab + o, m)), device_id_type=MESH).start()
    rest = peak_in.at[pl.ds(1, n * m - 1)]
    copies_p = pltpu.make_async_remote_copy(
        src_ref=rest, dst_ref=rest, send_sem=psend.at[0], recv_sem=precv.at[0],
        device_id=(lax.rem(me + 1, n), slab), device_id_type=MESH)
    seen_t = [smooth[16 + z : 17 + z] * cells[z : z + 1] for z in range(2)]
    smooth_ref[...] = jnp.concatenate(seen_t, axis=0)

    with jax.named_scope("peak_wait"):
        copies_p.wait_recv()
    for a in range(n):
        best = peak_in[a * m]
        for o in range(1, m):
            best = jnp.maximum(best, peak_in[a * m + o])
        peak_ref[lax.rem(me - a + n, n)] = best

    with jax.named_scope("send_wait"):
        copies_p.wait_send()

        @pl.when(slab < m - 1)
        def _():
            for copy in rise:
                copy.wait_send()

        @pl.when(slab > 0)
        def _():
            for copy in fall:
                copy.wait_send()


def p_kernel(smooth_ref, peaks_ref, mask_ref, t_ref, pval_ref, line_ref):
    n = peaks_ref.shape[0]
    copies = line_ref.shape[1]
    groups = copies // 8
    share = n // groups
    cells = mask_ref[...].astype(jnp.float32)
    values = smooth_ref[...]
    t_ref[...] = values
    sub = lax.broadcasted_iota(jnp.int32, (8, LANES), 0)
    lane = lax.broadcasted_iota(jnp.int32, (8, LANES), 1)
    line = jnp.zeros((8, LANES), jnp.float32)
    counts = [jnp.zeros((8, values.shape[1]), jnp.float32) for _ in range(2)]
    for q in range(groups):
        best = peaks_ref[q * share]
        for s in range(1, share):
            best = jnp.maximum(best, peaks_ref[q * share + s])
        value = jnp.sum(jnp.where(lane == sub, best, 0.0), axis=1, keepdims=True)
        line = jnp.where(lane == sub + 8 * q, value, line)
        for z in range(2):
            counts[z] = counts[z] + jax.nn.sigmoid((value - values[z : z + 1]) / 0.2)
    total = [jnp.sum(count, axis=0, keepdims=True) for count in counts]
    pval_ref[...] = cells * (1.0 + jnp.concatenate(total, axis=0)) / (copies + 1)
    line_ref[...] = jnp.sum(line, axis=0, keepdims=True)[:, :copies]


def body(n, m, subjects_data, covariates, permutes, brain_mask):
    subj_rows, depth, plane = subjects_data.shape
    copies = permutes.shape[0]
    groups = copies // 8
    nest = 4 * LANES // copies * BLOCK
    assert depth == 2 and plane == PX * PY and n % groups == 0 and subj_rows % nest == 0
    lane_tiles = plane // LANES
    data = subjects_data.reshape(subj_rows, depth, lane_tiles, LANES).transpose(0, 2, 1, 3)
    f32 = jnp.float32
    bf16 = jnp.bfloat16
    vmem = pl.BlockSpec(memory_space=pltpu.VMEM)
    hbm = pl.BlockSpec(memory_space=pltpu.HBM)
    dma = pltpu.SemaphoreType.DMA
    tall = 3 * copies + 16
    data, covariates, permutes = (
        pltpu.with_memory_space_constraint(x, pltpu.HBM) for x in (data, covariates, permutes))
    smooth, peaks = pl.pallas_call(
        functools.partial(maps_kernel, n, m, float(n * subj_rows - 4)),
        in_specs=[hbm] * 4,
        out_specs=[vmem] * 2,
        out_shape=[pltpu.VMEM((depth, plane), f32), pltpu.VMEM((n, 1, LANES), f32)],
        scratch_shapes=[
            pltpu.VMEM((depth, plane), jnp.int32),
            pltpu.VMEM((lane_tiles, subj_rows, depth, LANES), bf16),
            pltpu.VMEM((lane_tiles * subj_rows * depth, LANES), bf16),
            pltpu.VMEM((3, subj_rows), bf16),
            pltpu.VMEM((copies, subj_rows), jnp.int32),
            pltpu.VMEM((subj_rows // nest, 8 * HALF, LANES), f32),
            pltpu.VMEM((6 * copies + 16, 2 * subj_rows), bf16),
            pltpu.VMEM((tall, subj_rows), bf16),
            pltpu.VMEM((2, 8, LANES), f32),
            pltpu.VMEM((8, LANES), f32),
            pltpu.VMEM((n, 8, LANES), f32),
            pltpu.VMEM((8, LANES), f32),
            pltpu.VMEM((n, 8, LANES), f32),
            pltpu.VMEM((2, n, 56, plane // 2), f32),
            pltpu.VMEM((2, n, 56, plane // 2), f32),
            pltpu.VMEM((2, 8, plane), f32),
            pltpu.VMEM((2, 8, plane), f32),
            pltpu.VMEM((2, 8, plane), f32),
            pltpu.VMEM((2, 1, plane), f32),
            pltpu.VMEM((2, 1, plane), f32),
            pltpu.VMEM((2, 1, plane), f32),
            pltpu.VMEM((2, 6 * copies + 16, plane // 2), f32),
            pltpu.VMEM((24, plane), f32),
            pltpu.VMEM((1, LANES), f32),
            pltpu.VMEM((n * m, 1, LANES), f32),
            pltpu.VMEM((LANES, 8), f32),
            dma((lane_tiles,)), dma((groups + 2,)), dma((lane_tiles,)),
            dma((1,)), dma((1,)), dma((1,)), dma((1,)), dma((2,)), dma((2,)),
            dma((2, 4)), dma((2, 4)), dma((1,)), dma((1,)),
        ],
        compiler_params=pltpu.CompilerParams(
            collective_id=0, has_side_effects=True, vmem_limit_bytes=48 * 2**20
        ),
        name="maps",
    )(data, covariates, permutes, pltpu.with_memory_space_constraint(brain_mask, pltpu.HBM))
    smooth_t, p_values, line = pl.pallas_call(
        p_kernel,
        in_specs=[vmem] * 3,
        out_specs=[vmem] * 3,
        out_shape=[
            jax.ShapeDtypeStruct((depth, plane), f32),
            jax.ShapeDtypeStruct((depth, plane), f32),
            jax.ShapeDtypeStruct((1, copies), f32),
        ],
        compiler_params=pltpu.CompilerParams(vmem_limit_bytes=8 * 2**20),
        name="p_values",
    )(smooth, peaks, brain_mask)
    return smooth_t, p_values, line.reshape(copies)


def solution(mesh):
    return jax.shard_map(
        functools.partial(body, mesh.shape["subj"], mesh.shape["slab"]),
        mesh=mesh,
        in_specs=(P("subj", "slab", None), P(None, "subj"), P(None, "subj"), P("slab", None)),
        out_specs=(P("slab", None), P("slab", None), P()),
        check_vma=False,
    )
```

```python
import functools
import math

import jax
import jax.numpy as jnp
from jax import lax
from jax.experimental import pallas as pl
from jax.experimental.pallas import tpu as pltpu
from jax.sharding import PartitionSpec as P

BLOCK = 256
HALF = 128
PX = 16
PY = 32
LANES = 128
MESH = pl.DeviceIdType.MESH
NT = (((1,), (1,)), ((), ()))

gauss_raw = tuple((math.exp(-0.5 * (offset - 2) ** 2) for offset in range(5)))
gauss_taps = tuple((value / sum(gauss_raw) for value in gauss_raw))

def cholesky(mat):
    size = len(mat)
    low = [[None] * size for _ in range(size)]
    for j in range(size):
        total = mat[j][j]
        for k in range(j):
            total = total - low[j][k] * low[j][k]
        low[j][j] = jnp.sqrt(total)
        for i in range(j + 1, size):
            total = mat[i][j]
            for k in range(j):
                total = total - low[i][k] * low[j][k]
            low[i][j] = total / low[j][j]
    return low


def cho_solve(low, inv_diag, rhs):
    size = len(low)
    half = []
    for i in range(size):
        total = rhs[i]
        for k in range(i):
            total = total - low[i][k] * half[k]
        half.append(total * inv_diag[i])
    out = [None] * size
    for i in reversed(range(size)):
        total = half[i]
        for k in range(i + 1, size):
            total = total - low[k][i] * out[k]
        out[i] = total * inv_diag[i]
    return out


def blur(cells, stride, coord, size):
    width = cells.shape[1]
    total = None
    for position in range(5):
        d = position - 2
        moved = cells if d == 0 else pltpu.roll(cells, (-d * stride) % width, 1)
        inside = (coord + d >= 0) & (coord + d < size)
        term = gauss_taps[position] * jnp.where(inside, moved, 0.0)
        total = term if total is None else total + term
    return total


def batcher(size):
    pairs = []
    p = 1
    while p < size:
        k = p
        while k >= 1:
            for j in range(k % p, size - k, 2 * k):
                for i in range(min(k, size - j - k)):
                    if (i + j) // (2 * p) == (i + j + k) // (2 * p):
                        pairs.append((i + j, i + j + k))
            k //= 2
        p *= 2
    return pairs

def exchange_all(held, step):
    for i in held:
        j = i ^ step
        if i < j:
            held[i], held[j] = jnp.minimum(held[i], held[j]), jnp.maximum(held[i], held[j])

def cosets(gens):
    left = set(range(HALF))
    out = []
    while left:
        group = {min(left)}
        for g in gens:
            group |= {i ^ g for i in group}
        out.append(sorted(group))
        left -= group
    return out

def sort_blocks(rank):
    def load(ids):
        return {i: rank[8 * i : 8 * i + 8, :] for i in ids}
    def save(held):
        for i, v in held.items():
            rank[8 * i : 8 * i + 8, :] = v
    net = batcher(32)
    for ids in cosets([1, 2, 4, 8, 16]):
        held = load(ids)
        for lo, hi in net:
            i, j = ids[lo], ids[hi]
            held[i], held[j] = jnp.minimum(held[i], held[j]), jnp.maximum(held[i], held[j])
        save(held)
    for steps in ([63, 16, 8, 4, 2], [1, 127, 32, 16, 8]):
        for ids in cosets(steps):
            held = load(ids)
            for step in steps:
                exchange_all(held, step)
            save(held)
    upper = lax.broadcasted_iota(jnp.int32, (8, LANES), 0) >= 4
    sign = jnp.where(upper, -1.0, 1.0)
    for ids in cosets([4, 2, 1, 64, 32]):
        held = load(ids)
        for step in (4, 2, 1):
            exchange_all(held, step)
        for i in ids:
            v = held[i]
            held[i] = jnp.minimum(v, -pltpu.roll(v, 4, 0)) * sign
        for step in (64, 32):
            exchange_all(held, step)
        save(held)
    for ids in cosets([16, 8, 4, 2, 1]):
        held = load(ids)
        for step in (16, 8, 4, 2, 1):
            exchange_all(held, step)
        save(held)

def take(table, index):
    return jnp.take_along_axis(table, index, axis=1, mode="promise_in_bounds")

def sort_permutations(perm_ref, rank_ref):
    rows = perm_ref.shape[0]
    per = LANES // rows
    lane = lax.broadcasted_iota(jnp.int32, (rows, LANES), 1)
    for s in range(rank_ref.shape[0]):
        rank = rank_ref.at[s]
        with jax.named_scope("turn_in"):
            for g in range(8):
                half, hi = g // 4, g % 4
                got = []
                for bl in range(per):
                    at = ((4 * s + hi) * per + bl) * BLOCK + half * HALF
                    local = perm_ref[:, at : at + HALF] & (BLOCK - 1)
                    value = local * BLOCK + lane + half * HALF
                    got.append((-value if half else value).astype(jnp.float32))
                rank[pl.ds(g, HALF, stride=8), :] = jnp.concatenate(got, axis=0).T
        with jax.named_scope("sort"):
            sort_blocks(rank)


def spread_designs(rank_ref, cov_ref, des_ref, flat_ref, turn_ref, between):
    rows = (des_ref.shape[0] - 16) // 6
    per = LANES // rows
    high = flat_ref.shape[0]
    sub8 = lax.broadcasted_iota(jnp.int32, (8, LANES), 0)
    kind = sub8 % 4
    to = lax.broadcasted_iota(jnp.int32, (HALF, BLOCK), 1)
    come = lax.broadcasted_iota(jnp.int32, (HALF, BLOCK), 0)
    double = jnp.where(to // 2 == come, 1.0, 0.0).astype(jnp.bfloat16)
    even = lax.broadcasted_iota(jnp.int32, (16, BLOCK), 1) % 2 == 0
    upper = lax.broadcasted_iota(jnp.int32, (16, BLOCK), 0) >= 4
    keep = [jnp.where(even == (z == 0), 1.0, 0.0).astype(jnp.bfloat16) for z in range(2)]
    keep_seen = jnp.where(even != upper, 1.0, 0.0).astype(jnp.bfloat16)
    for g in range(8 * rank_ref.shape[0]):
        turn_ref[g] = rank_ref[g // 8, pl.ds(g % 8, HALF, stride=8), :].T.astype(jnp.int32)

    def leave(step):
        for half in range(2):
            turned = turn_ref[step // 4 * 8 + half * 4 + step % 4]
            tall = []
            for bl in range(per):
                at = (step * per + bl) * BLOCK
                cov = cov_ref[:, pl.ds(pl.multiple_of(at, BLOCK), BLOCK)].astype(jnp.float32)
                table = [
                    [jnp.broadcast_to(cov[k : k + 1, h * HALF : h * HALF + HALF], (8, LANES)) for h in range(2)]
                    for k in range(3)
                ]
                values = []
                for q in range(rows // 8):
                    r = bl * rows + q * 8
                    index = turned[r : r + 8] & (HALF - 1)
                    low = (turned[r : r + 8] & HALF) == 0
                    for k in range(3):
                        values.append(jnp.where(low, take(table[k][0], index), take(table[k][1], index)))
                d = [table[k][half] for k in range(3)]
                values.append(jnp.where(kind == 0, d[0], jnp.where(kind == 1, 1.0, jnp.where(kind == 2, d[1], d[2]))))
                values.append(jnp.zeros((8, LANES), jnp.float32))
                tile = jnp.concatenate(values, axis=0).astype(jnp.bfloat16)
                flat_ref[:, pl.ds(pl.multiple_of(at + half * HALF, HALF), HALF)] = tile
                tall.append(tile)
            wide = jnp.dot(
                jnp.concatenate(tall, axis=0), double, preferred_element_type=jnp.float32).astype(jnp.bfloat16)
            for bl in range(per):
                at = (step * per + bl) * BLOCK
                out = pl.ds(2 * at + half * BLOCK, BLOCK)
                for r in range(0, high, 16):
                    piece = wide[bl * high + r : bl * high + r + 16]
                    if r < 3 * rows:
                        for z in range(2):
                            first = z * 3 * rows + r
                            des_ref[first : first + 16, out] = piece * keep[z]
                    else:
                        des_ref[6 * rows :, out] = piece * keep_seen

    for step in range(4 * rank_ref.shape[0]):
        leave(step)
        between(step)


def cross_design(flat_ref, cross_ref):
    high = flat_ref.shape[0]
    with jax.named_scope("crossed"):
        cross_ref[...] = jnp.zeros_like(cross_ref)
        deep = flat_ref.shape[1] // 2
        for k in range(2):
            cols = slice(k * deep, (k + 1) * deep)
            cross_ref[k, :, 0:high] = lax.dot_general(
                flat_ref[high - 16 : high, cols], flat_ref[:, cols], NT, preferred_element_type=jnp.float32)[0:8]


def maps_kernel(
    n, m, freedom,
    x_hbm, cov_hbm, perm_hbm, mask_hbm, smooth_ref, peak_ref,
    mask_ref, staged, cells_ref, cov_ref, perm_ref, rank_ref, turn_ref, des_ref, flat_ref, cross_ref,
    out_x, got_x, out_q, got_q, out, got, own, low, high, own_o, low_o, high_o, parts, field, peak_out, peak_in, turned,
    lsem, csem, psem, xsend, xrecv, qsend, qrecv, send, recv, hsend, hrecv, psend, precv,
):
    me = lax.axis_index("subj")
    slab = lax.axis_index("slab")
    plane = mask_ref.shape[1]
    rows = (des_ref.shape[0] - 16) // 6
    groups = rows // 8
    share = n // groups
    depth = des_ref.shape[1]
    half_plane = plane // 2
    top = 3 * rows

    groups_of_rows = perm_ref.shape[0] // 8
    small = [
        pltpu.make_async_copy(perm_hbm.at[pl.ds(8 * i, 8)], perm_ref.at[pl.ds(8 * i, 8)], csem.at[i])
        for i in range(groups_of_rows)
    ] + [
        pltpu.make_async_copy(cov_hbm, cov_ref, csem.at[groups_of_rows]),
        pltpu.make_async_copy(mask_hbm, mask_ref, csem.at[groups_of_rows + 1]),
    ]
    loads = [pltpu.make_async_copy(x_hbm.at[:, c], staged.at[c], lsem.at[c]) for c in range(4)]
    plain = staged.reshape(cells_ref.shape)
    moves = [
        pltpu.make_async_copy(
            plain.at[pl.ds(c * depth, depth)], cells_ref.at[pl.ds(c * depth, depth)], psem.at[c])
        for c in range(4)
    ]
    for copy in small + loads[:1]:
        copy.start()

    barrier = pltpu.get_barrier_semaphore()
    for a in range(n):
        for o in range(m):
            if a + o:
                pl.semaphore_signal(
                    barrier, inc=1, device_id=(lax.rem(me + a, n), lax.rem(slab + o, m)), device_id_type=MESH)

    with jax.named_scope("perm_wait"):
        for copy in small:
            copy.wait()
    loads[1].start()
    sort_permutations(perm_ref, rank_ref)
    for copy in loads[2:]:
        copy.start()
    chunks = 4 * rank_ref.shape[0]
    span = depth // chunks

    def add_product(h, chunk):
        for k in range(2):
            at = chunk * span + k * (span // 2)
            part = jnp.concatenate(
                [cells_ref[pl.ds((2 * h + c) * depth + at, span // 2), :] for c in range(2)], axis=1)
            term = jnp.dot(
                des_ref[:, at : at + span // 2], part, preferred_element_type=jnp.float32)
            parts[k] = parts[k] + term if chunk else term

    ready = 1
    left_over = list(range(chunks))

    def between(step):
        if step == ready:
            for c in range(2):
                loads[c].wait()
                moves[c].start()
            for c in range(2):
                moves[c].wait()
        if step > ready:
            for _ in range(2):
                if left_over[0] < step:
                    add_product(0, left_over.pop(0))

    with jax.named_scope("gather"):
        spread_designs(rank_ref, cov_ref, des_ref, flat_ref, turn_ref, between)

    def source(s):
        return lax.rem(me - s + n, n)

    def exchange(src, box, send_sem, recv_sem):
        for o in range(1, n):
            to = lax.rem(me + o, n)
            pltpu.make_async_remote_copy(
                src_ref=src(to), dst_ref=box.at[o], send_sem=send_sem, recv_sem=recv_sem,
                device_id=(to, slab), device_id_type=MESH).start()
        rest = box.at[pl.ds(1, n - 1)]
        return pltpu.make_async_remote_copy(
            src_ref=rest, dst_ref=rest, send_sem=send_sem, recv_sem=recv_sem,
            device_id=(lax.rem(me + 1, n), slab), device_id_type=MESH)

    def multiply(h):
        for k in range(2):
            at = k * (depth // 2)
            part = jnp.concatenate(
                [cells_ref[pl.ds((2 * h + c) * depth + at, depth // 2), :] for c in range(2)], axis=1)
            parts[k] = jnp.dot(
                des_ref[:, at : at + depth // 2], part, preferred_element_type=jnp.float32)

    def spread_out(h):
        def piece(first, count):
            return parts[0, first : first + count] + parts[1, first : first + count]

        for g in range(n):
            q = g // share
            out[h, g, 0:24] = piece(24 * q, 24)
            out[h, g, 24:48] = piece(top + 24 * q, 24)
            out[h, g, 48:56] = piece(2 * top, 8)
        got[h, 0] = out[h, me]
        return exchange(lambda g: out.at[h, g], got.at[h], send.at[h], recv.at[h])

    with jax.named_scope("multiply_first"):
        for chunk in left_over:
            add_product(0, chunk)
    with jax.named_scope("entry_wait"):
        pl.semaphore_wait(barrier, n * m - 1)
    copies_t = [spread_out(0)]
    cross_design(flat_ref, cross_ref)
    out_x[...] = cross_ref[0] + cross_ref[1]
    copies_x = exchange(lambda g: out_x, got_x, xsend.at[0], xrecv.at[0])
    got_x[0] = out_x[...]

    with jax.named_scope("second_load_wait"):
        for c in range(2, 4):
            loads[c].wait()
            moves[c].start()
        for c in range(2, 4):
            moves[c].wait()
    with jax.named_scope("squares"):
        step = 256

        def square(k, totals):
            new = []
            for c in range(4):
                at = pl.ds(pl.multiple_of(c * depth + k * step, step), step)
                part = cells_ref[at, :].astype(jnp.float32)
                new.append(totals[c] + jnp.sum((part * part).reshape(step // 32, 4, 8, LANES), axis=0))
            return tuple(new)

        totals = lax.fori_loop(
            0, depth // step, square, tuple(jnp.zeros((4, 8, LANES), jnp.float32) for _ in range(4)))
        sub = lax.broadcasted_iota(jnp.int32, (8, LANES), 0)
        packed = jnp.zeros((8, LANES), jnp.float32)
        for c in range(4):
            total = jnp.sum(totals[c], axis=0)
            total = total + pltpu.roll(total, 4, 0)
            total = total + pltpu.roll(total, 2, 0)
            packed = jnp.where(sub // 2 == c, total, packed)
        out_q[...] = packed
        got_q[0] = packed
    copies_q = exchange(lambda g: out_q, got_q, qsend.at[0], qrecv.at[0])
    with jax.named_scope("multiply_second"):
        multiply(1)
        copies_t.append(spread_out(1))

    cells = mask_ref[...].astype(jnp.float32)

    with jax.named_scope("gram"):
        copies_x.wait()
        total_x = got_x[source(0)]
        for s in range(1, n):
            total_x = total_x + got_x[source(s)]
        gram = [[total_x[j : j + 1, top + i : top + i + 1] for j in range(4)] for i in range(4)]
        turned[...] = total_x.T
        mine_x = turned[pl.ds(pl.multiple_of(24 * (me // share), 8), 24), :]
        low_z = cholesky([row[1:4] for row in gram[1:4]])
        inv_z = [1.0 / low_z[i][i] for i in range(3)]
        low_f = cholesky(gram)
        inv_diag = [1.0 / low_f[i][i] for i in range(4)]
        unit = [jnp.zeros((1, 1), jnp.float32), jnp.ones((1, 1), jnp.float32)]
        columns = [cho_solve(low_f, inv_diag, [unit[int(i == j)] for i in range(4)]) for j in range(4)]
        inverse = [[columns[j][i] for j in range(4)] for i in range(4)]

    up = (me, lax.rem(slab + 1, m))
    down = (me, lax.rem(slab + m - 1, m))

    def halo(src, dst, h, k, to):
        return pltpu.make_async_remote_copy(
            src_ref=src.at[h], dst_ref=dst.at[h], send_sem=hsend.at[h, k], recv_sem=hrecv.at[h, k],
            device_id=to, device_id_type=MESH)

    rise = [halo(own, low, h, 0, up) for h in range(2)] + [halo(own_o, low_o, h, 1, up) for h in range(2)]
    fall = [halo(own, high, h, 2, down) for h in range(2)] + [halo(own_o, high_o, h, 3, down) for h in range(2)]

    @pl.when(slab == 0)
    def _():
        low[...] = jnp.zeros_like(low)
        low_o[...] = jnp.zeros_like(low_o)

    @pl.when(slab == m - 1)
    def _():
        high[...] = jnp.zeros_like(high)
        high_o[...] = jnp.zeros_like(high_o)

    field[...] = jnp.zeros_like(field)

    for h in range(2):
        with jax.named_scope("take_in"):
            copies_t[h].wait()
            if h == 0:
                copies_q.wait()
                total_q = got_q[source(0)]
                for s in range(1, n):
                    total_q = total_q + got_q[source(s)]
        with jax.named_scope("statistic"):
            total = got[h, source(0)]
            for s in range(1, n):
                total = total + got[h, source(s)]
            for z in range(2):
                obs = total[48 + 4 * z : 52 + 4 * z]
                prod = [obs[k : k + 1] for k in range(4)]
                squares = jnp.concatenate(
                    [total_q[4 * h + 2 * c + z : 4 * h + 2 * c + z + 1] for c in range(2)], axis=1)
                fit = cho_solve(low_z, inv_z, prod[1:4])
                resid = squares - (prod[1] * fit[0] + prod[2] * fit[1] + prod[3] * fit[2])

                def statistic(proj):
                    slope = sum(inverse[0][k] * proj[k] for k in range(4))
                    quad = sum(proj[k] * sum(inverse[k][l] * proj[l] for l in range(4)) for k in range(4))
                    return slope / jnp.sqrt((resid - quad) / freedom * inverse[0][0])

                seen = [prod[k] - sum(gram[k][1 + i] * fit[i] for i in range(3)) for k in range(4)]
                mask_row = cells[z : z + 1, h * half_plane : (h + 1) * half_plane]
                cols = slice(z * half_plane, (z + 1) * half_plane)
                own_o[h, :, cols] = statistic(seen) * mask_row
                proj = []
                for c in range(3):
                    first = 24 * z + 8 * c
                    proj.append(total[first : first + 8] - sum(
                        mine_x[8 * c : 8 * c + 8, 1 + i : 2 + i] * fit[i] for i in range(3)))
                own[h, :, cols] = statistic([proj[0], seen[1], proj[1], proj[2]]) * mask_row

        @pl.when(slab < m - 1)
        def _():
            rise[h].start()
            rise[2 + h].start()

        @pl.when(slab > 0)
        def _():
            fall[h].start()
            fall[2 + h].start()

    with jax.named_scope("halo_wait"):
        @pl.when(slab > 0)
        def _():
            for copy in rise:
                copy.wait_recv()

        @pl.when(slab < m - 1)
        def _():
            for copy in fall:
                copy.wait_recv()

    with jax.named_scope("blur"):
        def deep(lower, mine, upper):
            slices = []
            for ref in (lower, mine, upper):
                for z in range(2):
                    cols = slice(z * half_plane, (z + 1) * half_plane)
                    slices.append(jnp.concatenate([ref[0, :, cols], ref[1, :, cols]], axis=1))
            return [
                sum(gauss_taps[position] * slices[position + z] for position in range(5))
                for z in range(2)
            ]

        first, second = deep(low, own, high)
        field[0:8, :] = first
        field[8:16, :] = second
        first, second = deep(low_o, own_o, high_o)
        field[16:17, :] = first
        field[17:18, :] = second

        cell = lax.broadcasted_iota(jnp.int32, (24, plane), 1)
        smooth = blur(field[...], PY, cell // PY, PX)
        smooth = blur(smooth, 1, cell % PY, PY)

        peaks = jnp.maximum(
            jnp.max(jnp.where(cells[0:1] > 0, smooth[0:8] * cells[0:1], -1e30), axis=1, keepdims=True),
            jnp.max(jnp.where(cells[1:2] > 0, smooth[8:16] * cells[1:2], -1e30), axis=1, keepdims=True),
        )
        lane = lax.broadcasted_iota(jnp.int32, (8, LANES), 1)
        line = jnp.sum(jnp.where(lane == sub, peaks, 0.0), axis=0, keepdims=True)
        peak_out[...] = line
        peak_in[0] = line
    for a in range(n):
        for o in range(m):
            if a + o:
                pltpu.make_async_remote_copy(
                    src_ref=peak_out, dst_ref=peak_in.at[a * m + o], send_sem=psend.at[0], recv_sem=precv.at[0],
                    device_id=(lax.rem(me + a, n), lax.rem(slab + o, m)), device_id_type=MESH).start()
    rest = peak_in.at[pl.ds(1, n * m - 1)]
    copies_p = pltpu.make_async_remote_copy(
        src_ref=rest, dst_ref=rest, send_sem=psend.at[0], recv_sem=precv.at[0],
        device_id=(lax.rem(me + 1, n), slab), device_id_type=MESH)
    seen_t = [smooth[16 + z : 17 + z] * cells[z : z + 1] for z in range(2)]
    smooth_ref[...] = jnp.concatenate(seen_t, axis=0)

    with jax.named_scope("peak_wait"):
        copies_p.wait_recv()
    for a in range(n):
        best = peak_in[a * m]
        for o in range(1, m):
            best = jnp.maximum(best, peak_in[a * m + o])
        peak_ref[lax.rem(me - a + n, n)] = best

    with jax.named_scope("send_wait"):
        copies_p.wait_send()

        @pl.when(slab < m - 1)
        def _():
            for copy in rise:
                copy.wait_send()

        @pl.when(slab > 0)
        def _():
            for copy in fall:
                copy.wait_send()


def p_kernel(smooth_ref, peaks_ref, mask_ref, t_ref, pval_ref, line_ref):
    n = peaks_ref.shape[0]
    copies = line_ref.shape[1]
    groups = copies // 8
    share = n // groups
    cells = mask_ref[...].astype(jnp.float32)
    values = smooth_ref[...]
    t_ref[...] = values
    sub = lax.broadcasted_iota(jnp.int32, (8, LANES), 0)
    lane = lax.broadcasted_iota(jnp.int32, (8, LANES), 1)
    line = jnp.zeros((8, LANES), jnp.float32)
    counts = [jnp.zeros((8, values.shape[1]), jnp.float32) for _ in range(2)]
    for q in range(groups):
        best = peaks_ref[q * share]
        for s in range(1, share):
            best = jnp.maximum(best, peaks_ref[q * share + s])
        value = jnp.sum(jnp.where(lane == sub, best, 0.0), axis=1, keepdims=True)
        line = jnp.where(lane == sub + 8 * q, value, line)
        for z in range(2):
            counts[z] = counts[z] + jax.nn.sigmoid((value - values[z : z + 1]) / 0.2)
    total = [jnp.sum(count, axis=0, keepdims=True) for count in counts]
    pval_ref[...] = cells * (1.0 + jnp.concatenate(total, axis=0)) / (copies + 1)
    line_ref[...] = jnp.sum(line, axis=0, keepdims=True)[:, :copies]


def body(n, m, subjects_data, covariates, permutes, brain_mask):
    subj_rows, depth, plane = subjects_data.shape
    copies = permutes.shape[0]
    groups = copies // 8
    nest = 4 * LANES // copies * BLOCK
    assert depth == 2 and plane == PX * PY and n % groups == 0 and subj_rows % nest == 0
    lane_tiles = plane // LANES
    data = subjects_data.reshape(subj_rows, depth, lane_tiles, LANES).transpose(0, 2, 1, 3)
    f32 = jnp.float32
    bf16 = jnp.bfloat16
    vmem = pl.BlockSpec(memory_space=pltpu.VMEM)
    hbm = pl.BlockSpec(memory_space=pltpu.HBM)
    dma = pltpu.SemaphoreType.DMA
    tall = 3 * copies + 16
    data, covariates, permutes = (
        pltpu.with_memory_space_constraint(x, pltpu.HBM) for x in (data, covariates, permutes))
    smooth, peaks = pl.pallas_call(
        functools.partial(maps_kernel, n, m, float(n * subj_rows - 4)),
        in_specs=[hbm] * 4,
        out_specs=[vmem] * 2,
        out_shape=[pltpu.VMEM((depth, plane), f32), pltpu.VMEM((n, 1, LANES), f32)],
        scratch_shapes=[
            pltpu.VMEM((depth, plane), jnp.int32),
            pltpu.VMEM((lane_tiles, subj_rows, depth, LANES), bf16),
            pltpu.VMEM((lane_tiles * subj_rows * depth, LANES), bf16),
            pltpu.VMEM((3, subj_rows), bf16),
            pltpu.VMEM((copies, subj_rows), jnp.int32),
            pltpu.VMEM((subj_rows // nest, 8 * HALF, LANES), f32),
            pltpu.VMEM((subj_rows // nest * 8, HALF, LANES), jnp.int32),
            pltpu.VMEM((6 * copies + 16, 2 * subj_rows), bf16),
            pltpu.VMEM((tall, subj_rows), bf16),
            pltpu.VMEM((2, 8, LANES), f32),
            pltpu.VMEM((8, LANES), f32),
            pltpu.VMEM((n, 8, LANES), f32),
            pltpu.VMEM((8, LANES), f32),
            pltpu.VMEM((n, 8, LANES), f32),
            pltpu.VMEM((2, n, 56, plane // 2), f32),
            pltpu.VMEM((2, n, 56, plane // 2), f32),
            pltpu.VMEM((2, 8, plane), f32),
            pltpu.VMEM((2, 8, plane), f32),
            pltpu.VMEM((2, 8, plane), f32),
            pltpu.VMEM((2, 1, plane), f32),
            pltpu.VMEM((2, 1, plane), f32),
            pltpu.VMEM((2, 1, plane), f32),
            pltpu.VMEM((2, 6 * copies + 16, plane // 2), f32),
            pltpu.VMEM((24, plane), f32),
            pltpu.VMEM((1, LANES), f32),
            pltpu.VMEM((n * m, 1, LANES), f32),
            pltpu.VMEM((LANES, 8), f32),
            dma((lane_tiles,)), dma((groups + 2,)), dma((lane_tiles,)),
            dma((1,)), dma((1,)), dma((1,)), dma((1,)), dma((2,)), dma((2,)),
            dma((2, 4)), dma((2, 4)), dma((1,)), dma((1,)),
        ],
        compiler_params=pltpu.CompilerParams(
            collective_id=0, has_side_effects=True, vmem_limit_bytes=48 * 2**20
        ),
        name="maps",
    )(data, covariates, permutes, pltpu.with_memory_space_constraint(brain_mask, pltpu.HBM))
    smooth_t, p_values, line = pl.pallas_call(
        p_kernel,
        in_specs=[vmem] * 3,
        out_specs=[vmem] * 3,
        out_shape=[
            jax.ShapeDtypeStruct((depth, plane), f32),
            jax.ShapeDtypeStruct((depth, plane), f32),
            jax.ShapeDtypeStruct((1, copies), f32),
        ],
        compiler_params=pltpu.CompilerParams(vmem_limit_bytes=8 * 2**20),
        name="p_values",
    )(smooth, peaks, brain_mask)
    return smooth_t, p_values, line.reshape(copies)


def solution(mesh):
    return jax.shard_map(
        functools.partial(body, mesh.shape["subj"], mesh.shape["slab"]),
        mesh=mesh,
        in_specs=(P("subj", "slab", None), P(None, "subj"), P(None, "subj"), P("slab", None)),
        out_specs=(P("slab", None), P("slab", None), P()),
        check_vma=False,
    )
```

```python
import functools
import math

import jax
import jax.numpy as jnp
from jax import lax
from jax.experimental import pallas as pl
from jax.experimental.pallas import tpu as pltpu
from jax.sharding import PartitionSpec as P

BLOCK = 256
HALF = 128
PX = 16
PY = 32
LANES = 128
MESH = pl.DeviceIdType.MESH
NT = (((1,), (1,)), ((), ()))

gauss_raw = tuple((math.exp(-0.5 * (offset - 2) ** 2) for offset in range(5)))
gauss_taps = tuple((value / sum(gauss_raw) for value in gauss_raw))

def cholesky(mat):
    size = len(mat)
    low = [[None] * size for _ in range(size)]
    for j in range(size):
        total = mat[j][j]
        for k in range(j):
            total = total - low[j][k] * low[j][k]
        low[j][j] = jnp.sqrt(total)
        for i in range(j + 1, size):
            total = mat[i][j]
            for k in range(j):
                total = total - low[i][k] * low[j][k]
            low[i][j] = total / low[j][j]
    return low


def cho_solve(low, inv_diag, rhs):
    size = len(low)
    half = []
    for i in range(size):
        total = rhs[i]
        for k in range(i):
            total = total - low[i][k] * half[k]
        half.append(total * inv_diag[i])
    out = [None] * size
    for i in reversed(range(size)):
        total = half[i]
        for k in range(i + 1, size):
            total = total - low[k][i] * out[k]
        out[i] = total * inv_diag[i]
    return out


def blur(cells, stride, coord, size):
    width = cells.shape[1]
    total = None
    for position in range(5):
        d = position - 2
        moved = cells if d == 0 else pltpu.roll(cells, (-d * stride) % width, 1)
        inside = (coord + d >= 0) & (coord + d < size)
        term = gauss_taps[position] * jnp.where(inside, moved, 0.0)
        total = term if total is None else total + term
    return total


def batcher(size):
    pairs = []
    p = 1
    while p < size:
        k = p
        while k >= 1:
            for j in range(k % p, size - k, 2 * k):
                for i in range(min(k, size - j - k)):
                    if (i + j) // (2 * p) == (i + j + k) // (2 * p):
                        pairs.append((i + j, i + j + k))
            k //= 2
        p *= 2
    return pairs

def exchange_all(held, step):
    for i in held:
        j = i ^ step
        if i < j:
            held[i], held[j] = jnp.minimum(held[i], held[j]), jnp.maximum(held[i], held[j])

def cosets(gens):
    left = set(range(HALF))
    out = []
    while left:
        group = {min(left)}
        for g in gens:
            group |= {i ^ g for i in group}
        out.append(sorted(group))
        left -= group
    return out

def sort_blocks(rank):
    def load(ids):
        return {i: rank[8 * i : 8 * i + 8, :] for i in ids}
    def save(held):
        for i, v in held.items():
            rank[8 * i : 8 * i + 8, :] = v
    net = batcher(32)
    for ids in cosets([1, 2, 4, 8, 16]):
        held = load(ids)
        for lo, hi in net:
            i, j = ids[lo], ids[hi]
            held[i], held[j] = jnp.minimum(held[i], held[j]), jnp.maximum(held[i], held[j])
        save(held)
    for steps in ([63, 16, 8, 4, 2], [1, 127, 32, 16, 8]):
        for ids in cosets(steps):
            held = load(ids)
            for step in steps:
                exchange_all(held, step)
            save(held)
    upper = lax.broadcasted_iota(jnp.int32, (8, LANES), 0) >= 4
    sign = jnp.where(upper, -1.0, 1.0)
    for ids in cosets([4, 2, 1, 64, 32]):
        held = load(ids)
        for step in (4, 2, 1):
            exchange_all(held, step)
        for i in ids:
            v = held[i]
            held[i] = jnp.minimum(v, -pltpu.roll(v, 4, 0)) * sign
        for step in (64, 32):
            exchange_all(held, step)
        save(held)
    for ids in cosets([16, 8, 4, 2, 1]):
        held = load(ids)
        for step in (16, 8, 4, 2, 1):
            exchange_all(held, step)
        save(held)

def take(table, index):
    return jnp.take_along_axis(table, index, axis=1, mode="promise_in_bounds")

def sort_permutations(perm_ref, rank_ref):
    rows = perm_ref.shape[0]
    per = LANES // rows
    lane = lax.broadcasted_iota(jnp.int32, (rows, LANES), 1)
    for s in range(rank_ref.shape[0]):
        rank = rank_ref.at[s]
        with jax.named_scope("turn_in"):
            for g in range(8):
                half, hi = g // 4, g % 4
                got = []
                for bl in range(per):
                    at = ((4 * s + hi) * per + bl) * BLOCK + half * HALF
                    local = perm_ref[:, at : at + HALF] & (BLOCK - 1)
                    value = local * BLOCK + lane + half * HALF
                    got.append((-value if half else value).astype(jnp.float32))
                rank[pl.ds(g, HALF, stride=8), :] = jnp.concatenate(got, axis=0).T
        with jax.named_scope("sort"):
            sort_blocks(rank)


def spread_designs(rank_ref, cov_ref, des_ref, flat_ref, turn_ref, between):
    rows = (des_ref.shape[0] - 16) // 6
    per = LANES // rows
    high = flat_ref.shape[0]
    sub8 = lax.broadcasted_iota(jnp.int32, (8, LANES), 0)
    kind = sub8 % 4
    to = lax.broadcasted_iota(jnp.int32, (HALF, BLOCK), 1)
    come = lax.broadcasted_iota(jnp.int32, (HALF, BLOCK), 0)
    double = jnp.where(to // 2 == come, 1.0, 0.0).astype(jnp.bfloat16)
    even = lax.broadcasted_iota(jnp.int32, (16, BLOCK), 1) % 2 == 0
    upper = lax.broadcasted_iota(jnp.int32, (16, BLOCK), 0) >= 4
    keep = [jnp.where(even == (z == 0), 1.0, 0.0).astype(jnp.bfloat16) for z in range(2)]
    keep_seen = jnp.where(even != upper, 1.0, 0.0).astype(jnp.bfloat16)
    for g in range(8 * rank_ref.shape[0]):
        turn_ref[g] = rank_ref[g // 8, pl.ds(g % 8, HALF, stride=8), :].T.astype(jnp.int32)

    def leave(step):
        for half in range(2):
            turned = turn_ref[step // 4 * 8 + half * 4 + step % 4]
            tall = []
            for bl in range(per):
                at = (step * per + bl) * BLOCK
                cov = cov_ref[:, pl.ds(pl.multiple_of(at, BLOCK), BLOCK)].astype(jnp.float32)
                table = [
                    [jnp.broadcast_to(cov[k : k + 1, h * HALF : h * HALF + HALF], (8, LANES)) for h in range(2)]
                    for k in range(3)
                ]
                values = []
                for q in range(rows // 8):
                    r = bl * rows + q * 8
                    index = turned[r : r + 8] & (HALF - 1)
                    low = (turned[r : r + 8] & HALF) == 0
                    for k in range(3):
                        values.append(jnp.where(low, take(table[k][0], index), take(table[k][1], index)))
                d = [table[k][half] for k in range(3)]
                values.append(jnp.where(kind == 0, d[0], jnp.where(kind == 1, 1.0, jnp.where(kind == 2, d[1], d[2]))))
                values.append(jnp.zeros((8, LANES), jnp.float32))
                tile = jnp.concatenate(values, axis=0).astype(jnp.bfloat16)
                flat_ref[:, pl.ds(pl.multiple_of(at + half * HALF, HALF), HALF)] = tile
                tall.append(tile)
            wide = jnp.dot(
                jnp.concatenate(tall, axis=0), double, preferred_element_type=jnp.float32).astype(jnp.bfloat16)
            for bl in range(per):
                at = (step * per + bl) * BLOCK
                out = pl.ds(2 * at + half * BLOCK, BLOCK)
                for r in range(0, high, 16):
                    piece = wide[bl * high + r : bl * high + r + 16]
                    if r < 3 * rows:
                        for z in range(2):
                            first = z * 3 * rows + r
                            des_ref[first : first + 16, out] = piece * keep[z]
                    else:
                        des_ref[6 * rows :, out] = piece * keep_seen

    for step in range(4 * rank_ref.shape[0]):
        leave(step)
        between(step)


def cross_design(flat_ref, cross_ref):
    high = flat_ref.shape[0]
    with jax.named_scope("crossed"):
        cross_ref[...] = jnp.zeros_like(cross_ref)
        deep = flat_ref.shape[1] // 2
        for k in range(2):
            cols = slice(k * deep, (k + 1) * deep)
            cross_ref[k, :, 0:high] = lax.dot_general(
                flat_ref[high - 16 : high, cols], flat_ref[:, cols], NT, preferred_element_type=jnp.float32)[0:8]


def maps_kernel(
    n, m, freedom,
    x_hbm, cov_hbm, perm_hbm, mask_hbm, smooth_ref, peak_ref,
    mask_ref, staged, cells_ref, cov_ref, perm_ref, rank_ref, turn_ref, des_ref, flat_ref, cross_ref,
    out_x, got_x, out_q, got_q, out, got, own, low, high, parts, field, peak_out, peak_in, turned,
    lsem, csem, psem, xsend, xrecv, qsend, qrecv, send, recv, hsend, hrecv, psend, precv,
):
    me = lax.axis_index("subj")
    slab = lax.axis_index("slab")
    plane = mask_ref.shape[1]
    rows = (des_ref.shape[0] - 16) // 6
    groups = rows // 8
    share = n // groups
    depth = des_ref.shape[1]
    half_plane = plane // 2
    top = 3 * rows

    groups_of_rows = perm_ref.shape[0] // 8
    small = [
        pltpu.make_async_copy(perm_hbm.at[pl.ds(8 * i, 8)], perm_ref.at[pl.ds(8 * i, 8)], csem.at[0])
        for i in range(groups_of_rows)
    ] + [
        pltpu.make_async_copy(cov_hbm, cov_ref, csem.at[1]),
        pltpu.make_async_copy(mask_hbm, mask_ref, csem.at[2]),
    ]
    arrivals = [pltpu.make_async_copy(perm_hbm, perm_ref, csem.at[0])] + small[groups_of_rows:]
    plain = staged.reshape(cells_ref.shape)

    def load(c):
        return pltpu.make_async_copy(x_hbm.at[:, c], staged.at[c], lsem.at[c // 2])

    def settle(h):
        held = staged.at[pl.ds(2 * h, 2)]
        pltpu.make_async_copy(held, held, lsem.at[h]).wait()
        for c in range(2):
            at = pl.ds((2 * h + c) * depth, depth)
            pltpu.make_async_copy(plain.at[at], cells_ref.at[at], psem.at[h]).start()
        at = pl.ds(2 * h * depth, 2 * depth)
        pltpu.make_async_copy(plain.at[at], cells_ref.at[at], psem.at[h]).wait()

    for copy in small + [load(0)]:
        copy.start()

    barrier = pltpu.get_barrier_semaphore()
    for a in range(n):
        for o in range(m):
            if a + o:
                pl.semaphore_signal(
                    barrier, inc=1, device_id=(lax.rem(me + a, n), lax.rem(slab + o, m)), device_id_type=MESH)

    with jax.named_scope("perm_wait"):
        for copy in arrivals:
            copy.wait()
    load(1).start()
    sort_permutations(perm_ref, rank_ref)
    for c in range(2, 4):
        load(c).start()
    chunks = 4 * rank_ref.shape[0]
    span = depth // chunks

    def add_product(h, chunk):
        for k in range(2):
            at = chunk * span + k * (span // 2)
            part = jnp.concatenate(
                [cells_ref[pl.ds((2 * h + c) * depth + at, span // 2), :] for c in range(2)], axis=1)
            term = jnp.dot(
                des_ref[:, at : at + span // 2], part, preferred_element_type=jnp.float32)
            parts[k] = parts[k] + term if chunk else term

    left_over = list(range(chunks))

    def between(step):
        if step == 1:
            settle(0)
            add_product(0, left_over.pop(0))
        if step > 1:
            add_product(0, left_over.pop(0))

    with jax.named_scope("gather"):
        spread_designs(rank_ref, cov_ref, des_ref, flat_ref, turn_ref, between)

    def source(s):
        return lax.rem(me - s + n, n)

    def exchange(src, box, send_sem, recv_sem):
        for o in range(1, n):
            to = lax.rem(me + o, n)
            pltpu.make_async_remote_copy(
                src_ref=src(to), dst_ref=box.at[o], send_sem=send_sem, recv_sem=recv_sem,
                device_id=(to, slab), device_id_type=MESH).start()
        rest = box.at[pl.ds(1, n - 1)]
        return pltpu.make_async_remote_copy(
            src_ref=rest, dst_ref=rest, send_sem=send_sem, recv_sem=recv_sem,
            device_id=(lax.rem(me + 1, n), slab), device_id_type=MESH)

    def multiply(h):
        for k in range(2):
            at = k * (depth // 2)
            part = jnp.concatenate(
                [cells_ref[pl.ds((2 * h + c) * depth + at, depth // 2), :] for c in range(2)], axis=1)
            parts[k] = jnp.dot(
                des_ref[:, at : at + depth // 2], part, preferred_element_type=jnp.float32)

    def spread_out(h):
        def piece(first, count):
            return parts[0, first : first + count] + parts[1, first : first + count]

        for g in range(n):
            q = g // share
            out[h, g, 0:24] = piece(24 * q, 24)
            out[h, g, 24:48] = piece(top + 24 * q, 24)
            out[h, g, 48:56] = piece(2 * top, 8)
        got[h, 0] = out[h, me]
        return exchange(lambda g: out.at[h, g], got.at[h], send.at[h], recv.at[h])

    with jax.named_scope("multiply_first"):
        for chunk in left_over:
            add_product(0, chunk)
    with jax.named_scope("entry_wait"):
        pl.semaphore_wait(barrier, n * m - 1)
    copies_t = [spread_out(0)]
    cross_design(flat_ref, cross_ref)
    out_x[...] = cross_ref[0] + cross_ref[1]
    copies_x = exchange(lambda g: out_x, got_x, xsend.at[0], xrecv.at[0])
    got_x[0] = out_x[...]

    with jax.named_scope("second_load_wait"):
        settle(1)
    with jax.named_scope("squares"):
        step = 256

        def square(k, totals):
            new = []
            for c in range(4):
                at = pl.ds(pl.multiple_of(c * depth + k * step, step), step)
                part = cells_ref[at, :].astype(jnp.float32)
                new.append(totals[c] + jnp.sum((part * part).reshape(step // 32, 4, 8, LANES), axis=0))
            return tuple(new)

        totals = lax.fori_loop(
            0, depth // step, square, tuple(jnp.zeros((4, 8, LANES), jnp.float32) for _ in range(4)))
        sub = lax.broadcasted_iota(jnp.int32, (8, LANES), 0)
        packed = jnp.zeros((8, LANES), jnp.float32)
        for c in range(4):
            total = jnp.sum(totals[c], axis=0)
            total = total + pltpu.roll(total, 4, 0)
            total = total + pltpu.roll(total, 2, 0)
            packed = jnp.where(sub // 2 == c, total, packed)
        out_q[...] = packed
        got_q[0] = packed
    copies_q = exchange(lambda g: out_q, got_q, qsend.at[0], qrecv.at[0])
    with jax.named_scope("multiply_second"):
        multiply(1)
        copies_t.append(spread_out(1))

    cells = mask_ref[...].astype(jnp.float32)

    with jax.named_scope("gram"):
        copies_x.wait()
        total_x = got_x[source(0)]
        for s in range(1, n):
            total_x = total_x + got_x[source(s)]
        gram = [[total_x[j : j + 1, top + i : top + i + 1] for j in range(4)] for i in range(4)]
        turned[...] = total_x.T
        mine_x = turned[pl.ds(pl.multiple_of(24 * (me // share), 8), 24), :]
        low_z = cholesky([row[1:4] for row in gram[1:4]])
        inv_z = [1.0 / low_z[i][i] for i in range(3)]
        low_f = cholesky(gram)
        inv_diag = [1.0 / low_f[i][i] for i in range(4)]
        unit = [jnp.zeros((1, 1), jnp.float32), jnp.ones((1, 1), jnp.float32)]
        columns = [cho_solve(low_f, inv_diag, [unit[int(i == j)] for i in range(4)]) for j in range(4)]
        inverse = [[columns[j][i] for j in range(4)] for i in range(4)]

    up = (me, lax.rem(slab + 1, m))
    down = (me, lax.rem(slab + m - 1, m))

    def halo(src, dst, h, k, to):
        return pltpu.make_async_remote_copy(
            src_ref=src.at[h], dst_ref=dst.at[h], send_sem=hsend.at[h, k], recv_sem=hrecv.at[h, k],
            device_id=to, device_id_type=MESH)

    rise = [halo(own, low, h, 0, up) for h in range(2)]
    fall = [halo(own, high, h, 1, down) for h in range(2)]

    @pl.when(slab == 0)
    def _():
        low[...] = jnp.zeros_like(low)

    @pl.when(slab == m - 1)
    def _():
        high[...] = jnp.zeros_like(high)

    own[...] = jnp.zeros_like(own)
    field[...] = jnp.zeros_like(field)

    for h in range(2):
        with jax.named_scope("take_in"):
            copies_t[h].wait()
            if h == 0:
                copies_q.wait()
                total_q = got_q[source(0)]
                for s in range(1, n):
                    total_q = total_q + got_q[source(s)]
        with jax.named_scope("statistic"):
            total = got[h, source(0)]
            for s in range(1, n):
                total = total + got[h, source(s)]
            for z in range(2):
                obs = total[48 + 4 * z : 52 + 4 * z]
                prod = [obs[k : k + 1] for k in range(4)]
                squares = jnp.concatenate(
                    [total_q[4 * h + 2 * c + z : 4 * h + 2 * c + z + 1] for c in range(2)], axis=1)
                fit = cho_solve(low_z, inv_z, prod[1:4])
                resid = squares - (prod[1] * fit[0] + prod[2] * fit[1] + prod[3] * fit[2])

                def statistic(proj):
                    slope = sum(inverse[0][k] * proj[k] for k in range(4))
                    quad = sum(proj[k] * sum(inverse[k][l] * proj[l] for l in range(4)) for k in range(4))
                    return slope / jnp.sqrt((resid - quad) / freedom * inverse[0][0])

                seen = [prod[k] - sum(gram[k][1 + i] * fit[i] for i in range(3)) for k in range(4)]
                mask_row = cells[z : z + 1, h * half_plane : (h + 1) * half_plane]
                line = statistic(seen) * mask_row
                for c in range(2):
                    own[h, 4, 2 * z + c : 2 * z + c + 1] = line[:, c * LANES : (c + 1) * LANES]
                proj = []
                for c in range(3):
                    first = 24 * z + 8 * c
                    proj.append(total[first : first + 8] - sum(
                        mine_x[8 * c : 8 * c + 8, 1 + i : 2 + i] * fit[i] for i in range(3)))
                block = statistic([proj[0], seen[1], proj[1], proj[2]]) * mask_row
                for c in range(2):
                    own[h, 2 * z + c] = block[:, c * LANES : (c + 1) * LANES]

        @pl.when(slab < m - 1)
        def _():
            rise[h].start()

        @pl.when(slab > 0)
        def _():
            fall[h].start()

    with jax.named_scope("halo_wait"):
        @pl.when(slab > 0)
        def _():
            for copy in rise:
                copy.wait_recv()

        @pl.when(slab < m - 1)
        def _():
            for copy in fall:
                copy.wait_recv()

    with jax.named_scope("blur"):
        def deep(pick):
            slices = []
            for ref in (low, own, high):
                for z in range(2):
                    slices.append(jnp.concatenate(
                        [pick(ref, h, 2 * z + c) for h in range(2) for c in range(2)], axis=1))
            return [
                sum(gauss_taps[position] * slices[position + z] for position in range(5))
                for z in range(2)
            ]

        first, second = deep(lambda ref, h, k: ref[h, k])
        field[0:8, :] = first
        field[8:16, :] = second
        first, second = deep(lambda ref, h, k: ref[h, 4, k : k + 1])
        field[16:17, :] = first
        field[17:18, :] = second

        cell = lax.broadcasted_iota(jnp.int32, (24, plane), 1)
        smooth = blur(field[...], PY, cell // PY, PX)
        smooth = blur(smooth, 1, cell % PY, PY)

        peaks = jnp.maximum(
            jnp.max(jnp.where(cells[0:1] > 0, smooth[0:8] * cells[0:1], -1e30), axis=1, keepdims=True),
            jnp.max(jnp.where(cells[1:2] > 0, smooth[8:16] * cells[1:2], -1e30), axis=1, keepdims=True),
        )
        lane = lax.broadcasted_iota(jnp.int32, (8, LANES), 1)
        line = jnp.sum(jnp.where(lane == sub, peaks, 0.0), axis=0, keepdims=True)
        peak_out[...] = line
        peak_in[0] = line
    for a in range(n):
        for o in range(m):
            if a + o:
                pltpu.make_async_remote_copy(
                    src_ref=peak_out, dst_ref=peak_in.at[a * m + o], send_sem=psend.at[0], recv_sem=precv.at[0],
                    device_id=(lax.rem(me + a, n), lax.rem(slab + o, m)), device_id_type=MESH).start()
    rest = peak_in.at[pl.ds(1, n * m - 1)]
    copies_p = pltpu.make_async_remote_copy(
        src_ref=rest, dst_ref=rest, send_sem=psend.at[0], recv_sem=precv.at[0],
        device_id=(lax.rem(me + 1, n), slab), device_id_type=MESH)
    seen_t = [smooth[16 + z : 17 + z] * cells[z : z + 1] for z in range(2)]
    smooth_ref[...] = jnp.concatenate(seen_t, axis=0)

    with jax.named_scope("peak_wait"):
        copies_p.wait_recv()
    for a in range(n):
        best = peak_in[a * m]
        for o in range(1, m):
            best = jnp.maximum(best, peak_in[a * m + o])
        peak_ref[lax.rem(me - a + n, n)] = best

    with jax.named_scope("send_wait"):
        copies_p.wait_send()

        @pl.when(slab < m - 1)
        def _():
            for copy in rise:
                copy.wait_send()

        @pl.when(slab > 0)
        def _():
            for copy in fall:
                copy.wait_send()


def p_kernel(smooth_ref, peaks_ref, mask_ref, t_ref, pval_ref, line_ref):
    n = peaks_ref.shape[0]
    copies = line_ref.shape[1]
    groups = copies // 8
    share = n // groups
    cells = mask_ref[...].astype(jnp.float32)
    values = smooth_ref[...]
    t_ref[...] = values
    sub = lax.broadcasted_iota(jnp.int32, (8, LANES), 0)
    lane = lax.broadcasted_iota(jnp.int32, (8, LANES), 1)
    line = jnp.zeros((8, LANES), jnp.float32)
    counts = [jnp.zeros((8, values.shape[1]), jnp.float32) for _ in range(2)]
    for q in range(groups):
        best = peaks_ref[q * share]
        for s in range(1, share):
            best = jnp.maximum(best, peaks_ref[q * share + s])
        value = jnp.sum(jnp.where(lane == sub, best, 0.0), axis=1, keepdims=True)
        line = jnp.where(lane == sub + 8 * q, value, line)
        for z in range(2):
            counts[z] = counts[z] + jax.nn.sigmoid((value - values[z : z + 1]) / 0.2)
    total = [jnp.sum(count, axis=0, keepdims=True) for count in counts]
    pval_ref[...] = cells * (1.0 + jnp.concatenate(total, axis=0)) / (copies + 1)
    line_ref[...] = jnp.sum(line, axis=0, keepdims=True)[:, :copies]


def body(n, m, subjects_data, covariates, permutes, brain_mask):
    subj_rows, depth, plane = subjects_data.shape
    copies = permutes.shape[0]
    groups = copies // 8
    nest = 4 * LANES // copies * BLOCK
    assert depth == 2 and plane == PX * PY and n % groups == 0 and subj_rows % nest == 0
    lane_tiles = plane // LANES
    data = subjects_data.reshape(subj_rows, depth, lane_tiles, LANES).transpose(0, 2, 1, 3)
    f32 = jnp.float32
    bf16 = jnp.bfloat16
    vmem = pl.BlockSpec(memory_space=pltpu.VMEM)
    hbm = pl.BlockSpec(memory_space=pltpu.HBM)
    dma = pltpu.SemaphoreType.DMA
    tall = 3 * copies + 16
    data, covariates, permutes = (
        pltpu.with_memory_space_constraint(x, pltpu.HBM) for x in (data, covariates, permutes))
    smooth, peaks = pl.pallas_call(
        functools.partial(maps_kernel, n, m, float(n * subj_rows - 4)),
        in_specs=[hbm] * 4,
        out_specs=[vmem] * 2,
        out_shape=[pltpu.VMEM((depth, plane), f32), pltpu.VMEM((n, 1, LANES), f32)],
        scratch_shapes=[
            pltpu.VMEM((depth, plane), jnp.int32),
            pltpu.VMEM((lane_tiles, subj_rows, depth, LANES), bf16),
            pltpu.VMEM((lane_tiles * subj_rows * depth, LANES), bf16),
            pltpu.VMEM((3, subj_rows), bf16),
            pltpu.VMEM((copies, subj_rows), jnp.int32),
            pltpu.VMEM((subj_rows // nest, 8 * HALF, LANES), f32),
            pltpu.VMEM((subj_rows // nest * 8, HALF, LANES), jnp.int32),
            pltpu.VMEM((6 * copies + 16, 2 * subj_rows), bf16),
            pltpu.VMEM((tall, subj_rows), bf16),
            pltpu.VMEM((2, 8, LANES), f32),
            pltpu.VMEM((8, LANES), f32),
            pltpu.VMEM((n, 8, LANES), f32),
            pltpu.VMEM((8, LANES), f32),
            pltpu.VMEM((n, 8, LANES), f32),
            pltpu.VMEM((2, n, 56, plane // 2), f32),
            pltpu.VMEM((2, n, 56, plane // 2), f32),
            pltpu.VMEM((2, lane_tiles + 1, 8, LANES), f32),
            pltpu.VMEM((2, lane_tiles + 1, 8, LANES), f32),
            pltpu.VMEM((2, lane_tiles + 1, 8, LANES), f32),
            pltpu.VMEM((2, 6 * copies + 16, plane // 2), f32),
            pltpu.VMEM((24, plane), f32),
            pltpu.VMEM((1, LANES), f32),
            pltpu.VMEM((n * m, 1, LANES), f32),
            pltpu.VMEM((LANES, 8), f32),
            dma((2,)), dma((3,)), dma((2,)),
            dma((1,)), dma((1,)), dma((1,)), dma((1,)), dma((2,)), dma((2,)),
            dma((2, 2)), dma((2, 2)), dma((1,)), dma((1,)),
        ],
        compiler_params=pltpu.CompilerParams(
            collective_id=0, has_side_effects=True, vmem_limit_bytes=48 * 2**20
        ),
        name="maps",
    )(data, covariates, permutes, pltpu.with_memory_space_constraint(brain_mask, pltpu.HBM))
    smooth_t, p_values, line = pl.pallas_call(
        p_kernel,
        in_specs=[vmem] * 3,
        out_specs=[vmem] * 3,
        out_shape=[
            jax.ShapeDtypeStruct((depth, plane), f32),
            jax.ShapeDtypeStruct((depth, plane), f32),
            jax.ShapeDtypeStruct((1, copies), f32),
        ],
        compiler_params=pltpu.CompilerParams(vmem_limit_bytes=8 * 2**20),
        name="p_values",
    )(smooth, peaks, brain_mask)
    return smooth_t, p_values, line.reshape(copies)


def solution(mesh):
    return jax.shard_map(
        functools.partial(body, mesh.shape["subj"], mesh.shape["slab"]),
        mesh=mesh,
        in_specs=(P("subj", "slab", None), P(None, "subj"), P(None, "subj"), P("slab", None)),
        out_specs=(P("slab", None), P("slab", None), P()),
        check_vma=False,
    )
```

```python
import functools
import math

import jax
import jax.numpy as jnp
from jax import lax
from jax.experimental import pallas as pl
from jax.experimental.pallas import tpu as pltpu
from jax.sharding import PartitionSpec as P

BLOCK = 256
HALF = 128
PX = 16
PY = 32
LANES = 128
MESH = pl.DeviceIdType.MESH
NT = (((1,), (1,)), ((), ()))

gauss_raw = tuple((math.exp(-0.5 * (offset - 2) ** 2) for offset in range(5)))
gauss_taps = tuple((value / sum(gauss_raw) for value in gauss_raw))

def cholesky(mat):
    size = len(mat)
    low = [[None] * size for _ in range(size)]
    for j in range(size):
        total = mat[j][j]
        for k in range(j):
            total = total - low[j][k] * low[j][k]
        low[j][j] = jnp.sqrt(total)
        for i in range(j + 1, size):
            total = mat[i][j]
            for k in range(j):
                total = total - low[i][k] * low[j][k]
            low[i][j] = total / low[j][j]
    return low


def cho_solve(low, inv_diag, rhs):
    size = len(low)
    half = []
    for i in range(size):
        total = rhs[i]
        for k in range(i):
            total = total - low[i][k] * half[k]
        half.append(total * inv_diag[i])
    out = [None] * size
    for i in reversed(range(size)):
        total = half[i]
        for k in range(i + 1, size):
            total = total - low[k][i] * out[k]
        out[i] = total * inv_diag[i]
    return out


def blur(cells, stride, coord, size):
    width = cells.shape[1]
    total = None
    for position in range(5):
        d = position - 2
        moved = cells if d == 0 else pltpu.roll(cells, (-d * stride) % width, 1)
        inside = (coord + d >= 0) & (coord + d < size)
        term = gauss_taps[position] * jnp.where(inside, moved, 0.0)
        total = term if total is None else total + term
    return total


def batcher(size):
    pairs = []
    p = 1
    while p < size:
        k = p
        while k >= 1:
            for j in range(k % p, size - k, 2 * k):
                for i in range(min(k, size - j - k)):
                    if (i + j) // (2 * p) == (i + j + k) // (2 * p):
                        pairs.append((i + j, i + j + k))
            k //= 2
        p *= 2
    return pairs

def exchange_all(held, step):
    for i in held:
        j = i ^ step
        if i < j:
            held[i], held[j] = jnp.minimum(held[i], held[j]), jnp.maximum(held[i], held[j])

def cosets(gens):
    left = set(range(HALF))
    out = []
    while left:
        group = {min(left)}
        for g in gens:
            group |= {i ^ g for i in group}
        out.append(sorted(group))
        left -= group
    return out

def sort_blocks(rank):
    def load(ids):
        return {i: rank[8 * i : 8 * i + 8, :] for i in ids}
    def save(held):
        for i, v in held.items():
            rank[8 * i : 8 * i + 8, :] = v
    net = batcher(32)
    for ids in cosets([1, 2, 4, 8, 16]):
        held = load(ids)
        for lo, hi in net:
            i, j = ids[lo], ids[hi]
            held[i], held[j] = jnp.minimum(held[i], held[j]), jnp.maximum(held[i], held[j])
        save(held)
    for steps in ([63, 16, 8, 4, 2], [1, 127, 32, 16, 8]):
        for ids in cosets(steps):
            held = load(ids)
            for step in steps:
                exchange_all(held, step)
            save(held)
    upper = lax.broadcasted_iota(jnp.int32, (8, LANES), 0) >= 4
    sign = jnp.where(upper, -1.0, 1.0)
    for ids in cosets([4, 2, 1, 64, 32]):
        held = load(ids)
        for step in (4, 2, 1):
            exchange_all(held, step)
        for i in ids:
            v = held[i]
            held[i] = jnp.minimum(v, -pltpu.roll(v, 4, 0)) * sign
        for step in (64, 32):
            exchange_all(held, step)
        save(held)
    for ids in cosets([16, 8, 4, 2, 1]):
        held = load(ids)
        for step in (16, 8, 4, 2, 1):
            exchange_all(held, step)
        save(held)

def take(table, index):
    return jnp.take_along_axis(table, index, axis=1, mode="promise_in_bounds")

def sort_permutations(perm_ref, rank_ref):
    rows = perm_ref.shape[0]
    per = LANES // rows
    lane = lax.broadcasted_iota(jnp.int32, (rows, LANES), 1)
    for s in range(rank_ref.shape[0]):
        rank = rank_ref.at[s]
        with jax.named_scope("turn_in"):
            for g in range(8):
                half, hi = g // 4, g % 4
                got = []
                for bl in range(per):
                    at = ((4 * s + hi) * per + bl) * BLOCK + half * HALF
                    local = perm_ref[:, at : at + HALF] & (BLOCK - 1)
                    value = local * BLOCK + lane + half * HALF
                    got.append((-value if half else value).astype(jnp.float32))
                rank[pl.ds(g, HALF, stride=8), :] = jnp.concatenate(got, axis=0).T
        with jax.named_scope("sort"):
            sort_blocks(rank)


def spread_designs(rank_ref, cov_ref, des_ref, flat_ref, turn_ref, between):
    rows = (des_ref.shape[0] - 16) // 6
    per = LANES // rows
    high = flat_ref.shape[0]
    sub8 = lax.broadcasted_iota(jnp.int32, (8, LANES), 0)
    kind = sub8 % 4
    to = lax.broadcasted_iota(jnp.int32, (HALF, BLOCK), 1)
    come = lax.broadcasted_iota(jnp.int32, (HALF, BLOCK), 0)
    double = jnp.where(to // 2 == come, 1.0, 0.0).astype(jnp.bfloat16)
    even = lax.broadcasted_iota(jnp.int32, (16, BLOCK), 1) % 2 == 0
    upper = lax.broadcasted_iota(jnp.int32, (16, BLOCK), 0) >= 4
    keep = [jnp.where(even == (z == 0), 1.0, 0.0).astype(jnp.bfloat16) for z in range(2)]
    keep_seen = jnp.where(even != upper, 1.0, 0.0).astype(jnp.bfloat16)
    for g in range(8 * rank_ref.shape[0]):
        turn_ref[g] = rank_ref[g // 8, pl.ds(g % 8, HALF, stride=8), :].T.astype(jnp.int32)

    def leave(step):
        for half in range(2):
            turned = turn_ref[step // 4 * 8 + half * 4 + step % 4]
            tall = []
            for bl in range(per):
                at = (step * per + bl) * BLOCK
                cov = cov_ref[:, pl.ds(pl.multiple_of(at, BLOCK), BLOCK)].astype(jnp.float32)
                table = [
                    [jnp.broadcast_to(cov[k : k + 1, h * HALF : h * HALF + HALF], (8, LANES)) for h in range(2)]
                    for k in range(3)
                ]
                values = []
                for q in range(rows // 8):
                    r = bl * rows + q * 8
                    index = turned[r : r + 8] & (HALF - 1)
                    low = (turned[r : r + 8] & HALF) == 0
                    for k in range(3):
                        values.append(jnp.where(low, take(table[k][0], index), take(table[k][1], index)))
                d = [table[k][half] for k in range(3)]
                values.append(jnp.where(kind == 0, d[0], jnp.where(kind == 1, 1.0, jnp.where(kind == 2, d[1], d[2]))))
                values.append(jnp.zeros((8, LANES), jnp.float32))
                tile = jnp.concatenate(values, axis=0).astype(jnp.bfloat16)
                flat_ref[:, pl.ds(pl.multiple_of(at + half * HALF, HALF), HALF)] = tile
                tall.append(tile)
            wide = jnp.dot(
                jnp.concatenate(tall, axis=0), double, preferred_element_type=jnp.float32).astype(jnp.bfloat16)
            for bl in range(per):
                at = (step * per + bl) * BLOCK
                out = pl.ds(2 * at + half * BLOCK, BLOCK)
                for r in range(0, high, 16):
                    piece = wide[bl * high + r : bl * high + r + 16]
                    if r < 3 * rows:
                        for z in range(2):
                            first = z * 3 * rows + r
                            des_ref[first : first + 16, out] = piece * keep[z]
                    else:
                        des_ref[6 * rows :, out] = piece * keep_seen

    for step in range(4 * rank_ref.shape[0]):
        leave(step)
        between(step)


def cross_design(flat_ref, cross_ref):
    high = flat_ref.shape[0]
    with jax.named_scope("crossed"):
        cross_ref[...] = jnp.zeros_like(cross_ref)
        deep = flat_ref.shape[1] // 2
        for k in range(2):
            cols = slice(k * deep, (k + 1) * deep)
            cross_ref[k, :, 0:high] = lax.dot_general(
                flat_ref[high - 16 : high, cols], flat_ref[:, cols], NT, preferred_element_type=jnp.float32)[0:8]


def maps_kernel(
    n, m, freedom,
    x_hbm, cov_hbm, perm_hbm, mask_hbm, smooth_ref, peak_ref,
    mask_ref, staged, cells_ref, cov_ref, perm_ref, rank_ref, turn_ref, des_ref, flat_ref, cross_ref,
    out_x, got_x, out_q, got_q, out, got, own, low, high, parts, field, peak_out, peak_in, turned,
    lsem, csem, psem, xsend, xrecv, qsend, qrecv, send, recv, hsend, hrecv, psend, precv,
):
    me = lax.axis_index("subj")
    slab = lax.axis_index("slab")
    plane = mask_ref.shape[1]
    rows = (des_ref.shape[0] - 16) // 6
    groups = rows // 8
    share = n // groups
    depth = des_ref.shape[1]
    half_plane = plane // 2
    top = 3 * rows

    groups_of_rows = perm_ref.shape[0] // 8
    small = [
        pltpu.make_async_copy(perm_hbm.at[pl.ds(8 * i, 8), at], perm_ref.at[pl.ds(8 * i, 8), at], csem.at[0])
        for i in range(groups_of_rows)
        for at in (pl.ds(0, depth // 4), pl.ds(depth // 4, depth // 4))
    ] + [
        pltpu.make_async_copy(cov_hbm, cov_ref, csem.at[1]),
        pltpu.make_async_copy(mask_hbm, mask_ref, csem.at[2]),
    ]
    arrivals = [pltpu.make_async_copy(perm_hbm, perm_ref, csem.at[0])] + small[2 * groups_of_rows:]
    plain = staged.reshape(cells_ref.shape)

    def load(c):
        return pltpu.make_async_copy(x_hbm.at[:, c], staged.at[c], lsem.at[c // 2])

    def settle(h):
        held = staged.at[pl.ds(2 * h, 2)]
        pltpu.make_async_copy(held, held, lsem.at[h]).wait()
        for c in range(2):
            at = pl.ds((2 * h + c) * depth, depth)
            pltpu.make_async_copy(plain.at[at], cells_ref.at[at], psem.at[h]).start()
        at = pl.ds(2 * h * depth, 2 * depth)
        pltpu.make_async_copy(plain.at[at], cells_ref.at[at], psem.at[h]).wait()

    for copy in small + [load(0)]:
        copy.start()

    barrier = pltpu.get_barrier_semaphore()
    for a in range(n):
        for o in range(m):
            if a + o:
                pl.semaphore_signal(
                    barrier, inc=1, device_id=(lax.rem(me + a, n), lax.rem(slab + o, m)), device_id_type=MESH)

    with jax.named_scope("perm_wait"):
        for copy in arrivals:
            copy.wait()
    load(1).start()
    sort_permutations(perm_ref, rank_ref)
    for c in range(2, 4):
        load(c).start()
    chunks = 4 * rank_ref.shape[0]
    span = depth // chunks

    def add_product(h, chunk):
        for k in range(2):
            at = chunk * span + k * (span // 2)
            part = jnp.concatenate(
                [cells_ref[pl.ds((2 * h + c) * depth + at, span // 2), :] for c in range(2)], axis=1)
            term = jnp.dot(
                des_ref[:, at : at + span // 2], part, preferred_element_type=jnp.float32)
            parts[k] = parts[k] + term if chunk else term

    left_over = list(range(chunks))

    def between(step):
        if step == 1:
            settle(0)
            add_product(0, left_over.pop(0))
        if step > 1:
            add_product(0, left_over.pop(0))

    with jax.named_scope("gather"):
        spread_designs(rank_ref, cov_ref, des_ref, flat_ref, turn_ref, between)

    def source(s):
        return lax.rem(me - s + n, n)

    odd = lax.rem(me, 2)
    far_first = [n - 1 - (n - 2) * odd, *range(2, n - 1), 1 + (n - 2) * odd]

    def exchange(src, box, send_sem, recv_sem):
        for o in far_first:
            to = lax.rem(me + o, n)
            pltpu.make_async_remote_copy(
                src_ref=src(to), dst_ref=box.at[o], send_sem=send_sem, recv_sem=recv_sem,
                device_id=(to, slab), device_id_type=MESH).start()
        rest = box.at[pl.ds(1, n - 1)]
        return pltpu.make_async_remote_copy(
            src_ref=rest, dst_ref=rest, send_sem=send_sem, recv_sem=recv_sem,
            device_id=(lax.rem(me + 1, n), slab), device_id_type=MESH)

    def multiply(h):
        for k in range(2):
            at = k * (depth // 2)
            part = jnp.concatenate(
                [cells_ref[pl.ds((2 * h + c) * depth + at, depth // 2), :] for c in range(2)], axis=1)
            parts[k] = jnp.dot(
                des_ref[:, at : at + depth // 2], part, preferred_element_type=jnp.float32)

    def spread_out(h):
        def piece(first, count):
            return parts[0, first : first + count] + parts[1, first : first + count]

        for g in range(n):
            q = g // share
            out[h, g, 0:24] = piece(24 * q, 24)
            out[h, g, 24:48] = piece(top + 24 * q, 24)
            out[h, g, 48:56] = piece(2 * top, 8)
        got[h, 0] = out[h, me]
        return exchange(lambda g: out.at[h, g], got.at[h], send.at[h], recv.at[h])

    with jax.named_scope("multiply_first"):
        for chunk in left_over:
            add_product(0, chunk)
    with jax.named_scope("entry_wait"):
        pl.semaphore_wait(barrier, n * m - 1)
    copies_t = [spread_out(0)]
    cross_design(flat_ref, cross_ref)
    out_x[...] = cross_ref[0] + cross_ref[1]
    copies_x = exchange(lambda g: out_x, got_x, xsend.at[0], xrecv.at[0])
    got_x[0] = out_x[...]

    with jax.named_scope("second_load_wait"):
        settle(1)
    with jax.named_scope("squares"):
        step = 256

        def square(k, totals):
            new = []
            for c in range(4):
                at = pl.ds(pl.multiple_of(c * depth + k * step, step), step)
                part = cells_ref[at, :].astype(jnp.float32)
                new.append(totals[c] + jnp.sum((part * part).reshape(step // 32, 4, 8, LANES), axis=0))
            return tuple(new)

        totals = lax.fori_loop(
            0, depth // step, square, tuple(jnp.zeros((4, 8, LANES), jnp.float32) for _ in range(4)))
        sub = lax.broadcasted_iota(jnp.int32, (8, LANES), 0)
        packed = jnp.zeros((8, LANES), jnp.float32)
        for c in range(4):
            total = jnp.sum(totals[c], axis=0)
            total = total + pltpu.roll(total, 4, 0)
            total = total + pltpu.roll(total, 2, 0)
            packed = jnp.where(sub // 2 == c, total, packed)
        out_q[...] = packed
        got_q[0] = packed
    copies_q = exchange(lambda g: out_q, got_q, qsend.at[0], qrecv.at[0])
    with jax.named_scope("multiply_second"):
        multiply(1)
        copies_t.append(spread_out(1))

    cells = mask_ref[...].astype(jnp.float32)

    with jax.named_scope("gram"):
        copies_x.wait()
        total_x = got_x[source(0)]
        for s in range(1, n):
            total_x = total_x + got_x[source(s)]
        gram = [[total_x[j : j + 1, top + i : top + i + 1] for j in range(4)] for i in range(4)]
        turned[...] = total_x.T
        mine_x = turned[pl.ds(pl.multiple_of(24 * (me // share), 8), 24), :]
        low_z = cholesky([row[1:4] for row in gram[1:4]])
        inv_z = [1.0 / low_z[i][i] for i in range(3)]
        low_f = cholesky(gram)
        inv_diag = [1.0 / low_f[i][i] for i in range(4)]
        unit = [jnp.zeros((1, 1), jnp.float32), jnp.ones((1, 1), jnp.float32)]
        columns = [cho_solve(low_f, inv_diag, [unit[int(i == j)] for i in range(4)]) for j in range(4)]
        inverse = [[columns[j][i] for j in range(4)] for i in range(4)]

    up = (me, lax.rem(slab + 1, m))
    down = (me, lax.rem(slab + m - 1, m))

    def halo(src, dst, h, k, to):
        return pltpu.make_async_remote_copy(
            src_ref=src.at[h], dst_ref=dst.at[h], send_sem=hsend.at[h, k], recv_sem=hrecv.at[h, k],
            device_id=to, device_id_type=MESH)

    rise = [halo(own, low, h, 0, up) for h in range(2)]
    fall = [halo(own, high, h, 1, down) for h in range(2)]

    @pl.when(slab == 0)
    def _():
        low[...] = jnp.zeros_like(low)

    @pl.when(slab == m - 1)
    def _():
        high[...] = jnp.zeros_like(high)

    own[...] = jnp.zeros_like(own)
    field[...] = jnp.zeros_like(field)

    for h in range(2):
        with jax.named_scope("take_in"):
            copies_t[h].wait()
            if h == 0:
                copies_q.wait()
                total_q = got_q[source(0)]
                for s in range(1, n):
                    total_q = total_q + got_q[source(s)]
        with jax.named_scope("statistic"):
            total = got[h, source(0)]
            for s in range(1, n):
                total = total + got[h, source(s)]
            for z in range(2):
                obs = total[48 + 4 * z : 52 + 4 * z]
                prod = [obs[k : k + 1] for k in range(4)]
                squares = jnp.concatenate(
                    [total_q[4 * h + 2 * c + z : 4 * h + 2 * c + z + 1] for c in range(2)], axis=1)
                fit = cho_solve(low_z, inv_z, prod[1:4])
                resid = squares - (prod[1] * fit[0] + prod[2] * fit[1] + prod[3] * fit[2])

                def statistic(proj):
                    slope = sum(inverse[0][k] * proj[k] for k in range(4))
                    quad = sum(proj[k] * sum(inverse[k][l] * proj[l] for l in range(4)) for k in range(4))
                    return slope / jnp.sqrt((resid - quad) / freedom * inverse[0][0])

                seen = [prod[k] - sum(gram[k][1 + i] * fit[i] for i in range(3)) for k in range(4)]
                mask_row = cells[z : z + 1, h * half_plane : (h + 1) * half_plane]
                line = statistic(seen) * mask_row
                for c in range(2):
                    own[h, 4, 2 * z + c : 2 * z + c + 1] = line[:, c * LANES : (c + 1) * LANES]
                proj = []
                for c in range(3):
                    first = 24 * z + 8 * c
                    proj.append(total[first : first + 8] - sum(
                        mine_x[8 * c : 8 * c + 8, 1 + i : 2 + i] * fit[i] for i in range(3)))
                block = statistic([proj[0], seen[1], proj[1], proj[2]]) * mask_row
                for c in range(2):
                    own[h, 2 * z + c] = block[:, c * LANES : (c + 1) * LANES]

        @pl.when(slab < m - 1)
        def _():
            rise[h].start()

        @pl.when(slab > 0)
        def _():
            fall[h].start()

    with jax.named_scope("halo_wait"):
        @pl.when(slab > 0)
        def _():
            for copy in rise:
                copy.wait_recv()

        @pl.when(slab < m - 1)
        def _():
            for copy in fall:
                copy.wait_recv()

    with jax.named_scope("blur"):
        def deep(pick):
            slices = []
            for ref in (low, own, high):
                for z in range(2):
                    slices.append(jnp.concatenate(
                        [pick(ref, h, 2 * z + c) for h in range(2) for c in range(2)], axis=1))
            return [
                sum(gauss_taps[position] * slices[position + z] for position in range(5))
                for z in range(2)
            ]

        first, second = deep(lambda ref, h, k: ref[h, k])
        field[0:8, :] = first
        field[8:16, :] = second
        first, second = deep(lambda ref, h, k: ref[h, 4, k : k + 1])
        field[16:17, :] = first
        field[17:18, :] = second

        cell = lax.broadcasted_iota(jnp.int32, (24, plane), 1)
        smooth = blur(field[...], PY, cell // PY, PX)
        smooth = blur(smooth, 1, cell % PY, PY)

        peaks = jnp.maximum(
            jnp.max(jnp.where(cells[0:1] > 0, smooth[0:8] * cells[0:1], -1e30), axis=1, keepdims=True),
            jnp.max(jnp.where(cells[1:2] > 0, smooth[8:16] * cells[1:2], -1e30), axis=1, keepdims=True),
        )
        lane = lax.broadcasted_iota(jnp.int32, (8, LANES), 1)
        line = jnp.sum(jnp.where(lane == sub, peaks, 0.0), axis=0, keepdims=True)
        peak_out[...] = line
        peak_in[0] = line
    side = 2 * slab // m
    targets = []
    for j in range(m):
        line_slab = side * j + (1 - side) * (m - 1 - j)
        targets += [(a, line_slab, lax.rem(line_slab - slab + m, m)) for a in range(n - 1, 0, -1)]
    targets += [(0, lax.rem(slab + o, m), o) for o in range(1, m)]
    for a, line_slab, o in targets:
        pltpu.make_async_remote_copy(
            src_ref=peak_out, dst_ref=peak_in.at[a * m + o], send_sem=psend.at[0], recv_sem=precv.at[0],
            device_id=(lax.rem(me + a, n), line_slab), device_id_type=MESH).start()
    rest = peak_in.at[pl.ds(1, n * m - 1)]
    copies_p = pltpu.make_async_remote_copy(
        src_ref=rest, dst_ref=rest, send_sem=psend.at[0], recv_sem=precv.at[0],
        device_id=(lax.rem(me + 1, n), slab), device_id_type=MESH)
    seen_t = [smooth[16 + z : 17 + z] * cells[z : z + 1] for z in range(2)]
    smooth_ref[...] = jnp.concatenate(seen_t, axis=0)

    with jax.named_scope("peak_wait"):
        copies_p.wait_recv()
    for a in range(n):
        best = peak_in[a * m]
        for o in range(1, m):
            best = jnp.maximum(best, peak_in[a * m + o])
        peak_ref[lax.rem(me - a + n, n)] = best

    with jax.named_scope("send_wait"):
        copies_p.wait_send()

        @pl.when(slab < m - 1)
        def _():
            for copy in rise:
                copy.wait_send()

        @pl.when(slab > 0)
        def _():
            for copy in fall:
                copy.wait_send()


def p_kernel(smooth_ref, peaks_ref, mask_ref, t_ref, pval_ref, line_ref):
    n = peaks_ref.shape[0]
    copies = line_ref.shape[1]
    groups = copies // 8
    share = n // groups
    cells = mask_ref[...].astype(jnp.float32)
    values = smooth_ref[...]
    t_ref[...] = values
    sub = lax.broadcasted_iota(jnp.int32, (8, LANES), 0)
    lane = lax.broadcasted_iota(jnp.int32, (8, LANES), 1)
    line = jnp.zeros((8, LANES), jnp.float32)
    counts = [jnp.zeros((8, values.shape[1]), jnp.float32) for _ in range(2)]
    for q in range(groups):
        best = peaks_ref[q * share]
        for s in range(1, share):
            best = jnp.maximum(best, peaks_ref[q * share + s])
        value = jnp.sum(jnp.where(lane == sub, best, 0.0), axis=1, keepdims=True)
        line = jnp.where(lane == sub + 8 * q, value, line)
        for z in range(2):
            counts[z] = counts[z] + jax.nn.sigmoid((value - values[z : z + 1]) / 0.2)
    total = [jnp.sum(count, axis=0, keepdims=True) for count in counts]
    pval_ref[...] = cells * (1.0 + jnp.concatenate(total, axis=0)) / (copies + 1)
    line_ref[...] = jnp.sum(line, axis=0, keepdims=True)[:, :copies]


def body(n, m, subjects_data, covariates, permutes, brain_mask):
    subj_rows, depth, plane = subjects_data.shape
    copies = permutes.shape[0]
    groups = copies // 8
    nest = 4 * LANES // copies * BLOCK
    assert depth == 2 and plane == PX * PY and n % groups == 0 and subj_rows % nest == 0
    lane_tiles = plane // LANES
    data = subjects_data.reshape(subj_rows, depth, lane_tiles, LANES).transpose(0, 2, 1, 3)
    f32 = jnp.float32
    bf16 = jnp.bfloat16
    vmem = pl.BlockSpec(memory_space=pltpu.VMEM)
    hbm = pl.BlockSpec(memory_space=pltpu.HBM)
    dma = pltpu.SemaphoreType.DMA
    tall = 3 * copies + 16
    data, covariates, permutes = (
        pltpu.with_memory_space_constraint(x, pltpu.HBM) for x in (data, covariates, permutes))
    smooth, peaks = pl.pallas_call(
        functools.partial(maps_kernel, n, m, float(n * subj_rows - 4)),
        in_specs=[hbm] * 4,
        out_specs=[vmem] * 2,
        out_shape=[pltpu.VMEM((depth, plane), f32), pltpu.VMEM((n, 1, LANES), f32)],
        scratch_shapes=[
            pltpu.VMEM((depth, plane), jnp.int32),
            pltpu.VMEM((lane_tiles, subj_rows, depth, LANES), bf16),
            pltpu.VMEM((lane_tiles * subj_rows * depth, LANES), bf16),
            pltpu.VMEM((3, subj_rows), bf16),
            pltpu.VMEM((copies, subj_rows), jnp.int32),
            pltpu.VMEM((subj_rows // nest, 8 * HALF, LANES), f32),
            pltpu.VMEM((subj_rows // nest * 8, HALF, LANES), jnp.int32),
            pltpu.VMEM((6 * copies + 16, 2 * subj_rows), bf16),
            pltpu.VMEM((tall, subj_rows), bf16),
            pltpu.VMEM((2, 8, LANES), f32),
            pltpu.VMEM((8, LANES), f32),
            pltpu.VMEM((n, 8, LANES), f32),
            pltpu.VMEM((8, LANES), f32),
            pltpu.VMEM((n, 8, LANES), f32),
            pltpu.VMEM((2, n, 56, plane // 2), f32),
            pltpu.VMEM((2, n, 56, plane // 2), f32),
            pltpu.VMEM((2, lane_tiles + 1, 8, LANES), f32),
            pltpu.VMEM((2, lane_tiles + 1, 8, LANES), f32),
            pltpu.VMEM((2, lane_tiles + 1, 8, LANES), f32),
            pltpu.VMEM((2, 6 * copies + 16, plane // 2), f32),
            pltpu.VMEM((24, plane), f32),
            pltpu.VMEM((1, LANES), f32),
            pltpu.VMEM((n * m, 1, LANES), f32),
            pltpu.VMEM((LANES, 8), f32),
            dma((2,)), dma((3,)), dma((2,)),
            dma((1,)), dma((1,)), dma((1,)), dma((1,)), dma((2,)), dma((2,)),
            dma((2, 2)), dma((2, 2)), dma((1,)), dma((1,)),
        ],
        compiler_params=pltpu.CompilerParams(
            collective_id=0, has_side_effects=True, vmem_limit_bytes=48 * 2**20
        ),
        name="maps",
    )(data, covariates, permutes, pltpu.with_memory_space_constraint(brain_mask, pltpu.HBM))
    smooth_t, p_values, line = pl.pallas_call(
        p_kernel,
        in_specs=[vmem] * 3,
        out_specs=[vmem] * 3,
        out_shape=[
            jax.ShapeDtypeStruct((depth, plane), f32),
            jax.ShapeDtypeStruct((depth, plane), f32),
            jax.ShapeDtypeStruct((1, copies), f32),
        ],
        compiler_params=pltpu.CompilerParams(vmem_limit_bytes=8 * 2**20),
        name="p_values",
    )(smooth, peaks, brain_mask)
    return smooth_t, p_values, line.reshape(copies)


def solution(mesh):
    return jax.shard_map(
        functools.partial(body, mesh.shape["subj"], mesh.shape["slab"]),
        mesh=mesh,
        in_specs=(P("subj", "slab", None), P(None, "subj"), P(None, "subj"), P("slab", None)),
        out_specs=(P("slab", None), P("slab", None), P()),
        check_vma=False,
    )
```

```python
import functools
import math

import jax
import jax.numpy as jnp
from jax import lax
from jax.experimental import pallas as pl
from jax.experimental.pallas import tpu as pltpu
from jax.sharding import PartitionSpec as P

BLOCK = 256
HALF = 128
PX = 16
PY = 32
LANES = 128
MESH = pl.DeviceIdType.MESH
NT = (((1,), (1,)), ((), ()))

gauss_raw = tuple((math.exp(-0.5 * (offset - 2) ** 2) for offset in range(5)))
gauss_taps = tuple((value / sum(gauss_raw) for value in gauss_raw))

def cholesky(mat):
    size = len(mat)
    low = [[None] * size for _ in range(size)]
    for j in range(size):
        total = mat[j][j]
        for k in range(j):
            total = total - low[j][k] * low[j][k]
        low[j][j] = jnp.sqrt(total)
        for i in range(j + 1, size):
            total = mat[i][j]
            for k in range(j):
                total = total - low[i][k] * low[j][k]
            low[i][j] = total / low[j][j]
    return low


def cho_solve(low, inv_diag, rhs):
    size = len(low)
    half = []
    for i in range(size):
        total = rhs[i]
        for k in range(i):
            total = total - low[i][k] * half[k]
        half.append(total * inv_diag[i])
    out = [None] * size
    for i in reversed(range(size)):
        total = half[i]
        for k in range(i + 1, size):
            total = total - low[k][i] * out[k]
        out[i] = total * inv_diag[i]
    return out


def blur(cells, stride, coord, size):
    width = cells.shape[1]
    total = None
    for position in range(5):
        d = position - 2
        moved = cells if d == 0 else pltpu.roll(cells, (-d * stride) % width, 1)
        inside = (coord + d >= 0) & (coord + d < size)
        term = gauss_taps[position] * jnp.where(inside, moved, 0.0)
        total = term if total is None else total + term
    return total


def batcher(size):
    pairs = []
    p = 1
    while p < size:
        k = p
        while k >= 1:
            for j in range(k % p, size - k, 2 * k):
                for i in range(min(k, size - j - k)):
                    if (i + j) // (2 * p) == (i + j + k) // (2 * p):
                        pairs.append((i + j, i + j + k))
            k //= 2
        p *= 2
    return pairs

def exchange_all(held, step):
    for i in held:
        j = i ^ step
        if i < j:
            held[i], held[j] = jnp.minimum(held[i], held[j]), jnp.maximum(held[i], held[j])

def cosets(gens):
    left = set(range(HALF))
    out = []
    while left:
        group = {min(left)}
        for g in gens:
            group |= {i ^ g for i in group}
        out.append(sorted(group))
        left -= group
    return out

def sort_blocks(rank):
    def load(ids):
        return {i: rank[8 * i : 8 * i + 8, :] for i in ids}
    def save(held):
        for i, v in held.items():
            rank[8 * i : 8 * i + 8, :] = v
    net = batcher(32)
    for ids in cosets([1, 2, 4, 8, 16]):
        held = load(ids)
        for lo, hi in net:
            i, j = ids[lo], ids[hi]
            held[i], held[j] = jnp.minimum(held[i], held[j]), jnp.maximum(held[i], held[j])
        save(held)
    for steps in ([63, 16, 8, 4, 2], [1, 127, 32, 16, 8]):
        for ids in cosets(steps):
            held = load(ids)
            for step in steps:
                exchange_all(held, step)
            save(held)
    upper = lax.broadcasted_iota(jnp.int32, (8, LANES), 0) >= 4
    sign = jnp.where(upper, -1.0, 1.0)
    for ids in cosets([4, 2, 1, 64, 32]):
        held = load(ids)
        for step in (4, 2, 1):
            exchange_all(held, step)
        for i in ids:
            v = held[i]
            held[i] = jnp.minimum(v, -pltpu.roll(v, 4, 0)) * sign
        for step in (64, 32):
            exchange_all(held, step)
        save(held)
    for ids in cosets([16, 8, 4, 2, 1]):
        held = load(ids)
        for step in (16, 8, 4, 2, 1):
            exchange_all(held, step)
        save(held)

def take(table, index):
    return jnp.take_along_axis(table, index, axis=1, mode="promise_in_bounds")

def sort_permutations(perm_ref, rank_ref):
    rows = perm_ref.shape[0]
    per = LANES // rows
    lane = lax.broadcasted_iota(jnp.int32, (rows, LANES), 1)
    for s in range(rank_ref.shape[0]):
        rank = rank_ref.at[s]
        with jax.named_scope("turn_in"):
            for g in range(8):
                half, hi = g // 4, g % 4
                got = []
                for bl in range(per):
                    at = ((4 * s + hi) * per + bl) * BLOCK + half * HALF
                    local = perm_ref[:, at : at + HALF] & (BLOCK - 1)
                    value = local * BLOCK + lane + half * HALF
                    got.append((-value if half else value).astype(jnp.float32))
                rank[pl.ds(g, HALF, stride=8), :] = jnp.concatenate(got, axis=0).T
        with jax.named_scope("sort"):
            sort_blocks(rank)


def spread_designs(rank_ref, cov_ref, des_ref, flat_ref, turn_ref, between):
    rows = (des_ref.shape[0] - 16) // 6
    per = LANES // rows
    high = flat_ref.shape[0]
    sub8 = lax.broadcasted_iota(jnp.int32, (8, LANES), 0)
    kind = sub8 % 4
    to = lax.broadcasted_iota(jnp.int32, (HALF, BLOCK), 1)
    come = lax.broadcasted_iota(jnp.int32, (HALF, BLOCK), 0)
    double = jnp.where(to // 2 == come, 1.0, 0.0).astype(jnp.bfloat16)
    even = lax.broadcasted_iota(jnp.int32, (16, BLOCK), 1) % 2 == 0
    upper = lax.broadcasted_iota(jnp.int32, (16, BLOCK), 0) >= 4
    keep = [jnp.where(even == (z == 0), 1.0, 0.0).astype(jnp.bfloat16) for z in range(2)]
    keep_seen = jnp.where(even != upper, 1.0, 0.0).astype(jnp.bfloat16)
    for g in range(8 * rank_ref.shape[0]):
        turn_ref[g] = rank_ref[g // 8, pl.ds(g % 8, HALF, stride=8), :].T.astype(jnp.int32)

    def leave(step):
        for half in range(2):
            turned = turn_ref[step // 4 * 8 + half * 4 + step % 4]
            tall = []
            for bl in range(per):
                at = (step * per + bl) * BLOCK
                cov = cov_ref[:, pl.ds(pl.multiple_of(at, BLOCK), BLOCK)].astype(jnp.float32)
                table = [
                    [jnp.broadcast_to(cov[k : k + 1, h * HALF : h * HALF + HALF], (8, LANES)) for h in range(2)]
                    for k in range(3)
                ]
                values = []
                for q in range(rows // 8):
                    r = bl * rows + q * 8
                    index = turned[r : r + 8] & (HALF - 1)
                    low = (turned[r : r + 8] & HALF) == 0
                    for k in range(3):
                        values.append(jnp.where(low, take(table[k][0], index), take(table[k][1], index)))
                d = [table[k][half] for k in range(3)]
                values.append(jnp.where(kind == 0, d[0], jnp.where(kind == 1, 1.0, jnp.where(kind == 2, d[1], d[2]))))
                values.append(jnp.zeros((8, LANES), jnp.float32))
                tile = jnp.concatenate(values, axis=0).astype(jnp.bfloat16)
                flat_ref[:, pl.ds(pl.multiple_of(at + half * HALF, HALF), HALF)] = tile
                tall.append(tile)
            wide = jnp.dot(
                jnp.concatenate(tall, axis=0), double, preferred_element_type=jnp.float32).astype(jnp.bfloat16)
            for bl in range(per):
                at = (step * per + bl) * BLOCK
                out = pl.ds(2 * at + half * BLOCK, BLOCK)
                for r in range(0, high, 16):
                    piece = wide[bl * high + r : bl * high + r + 16]
                    if r < 3 * rows:
                        for z in range(2):
                            first = z * 3 * rows + r
                            des_ref[first : first + 16, out] = piece * keep[z]
                    else:
                        des_ref[6 * rows :, out] = piece * keep_seen

    for step in range(4 * rank_ref.shape[0]):
        leave(step)
        between(step)


def cross_design(flat_ref, cross_ref):
    high = flat_ref.shape[0]
    with jax.named_scope("crossed"):
        cross_ref[...] = jnp.zeros_like(cross_ref)
        deep = flat_ref.shape[1] // 2
        for k in range(2):
            cols = slice(k * deep, (k + 1) * deep)
            cross_ref[k, :, 0:high] = lax.dot_general(
                flat_ref[high - 16 : high, cols], flat_ref[:, cols], NT, preferred_element_type=jnp.float32)[0:8]


def maps_kernel(
    n, m, freedom,
    x_hbm, cov_hbm, perm_hbm, mask_hbm, smooth_ref, peak_ref,
    mask_ref, staged, cells_ref, cov_ref, perm_ref, rank_ref, turn_ref, des_ref, flat_ref, cross_ref,
    out_x, got_x, out_q, got_q, out, got, own, low, high, parts, field, peak_out, peak_in, turned,
    lsem, csem, psem, xsend, xrecv, qsend, qrecv, send, recv, hsend, hrecv, psend, precv,
):
    me = lax.axis_index("subj")
    slab = lax.axis_index("slab")
    plane = mask_ref.shape[1]
    rows = (des_ref.shape[0] - 16) // 6
    groups = rows // 8
    share = n // groups
    depth = des_ref.shape[1]
    half_plane = plane // 2
    top = 3 * rows

    groups_of_rows = perm_ref.shape[0] // 8
    small = [
        pltpu.make_async_copy(perm_hbm.at[pl.ds(8 * i, 8), at], perm_ref.at[pl.ds(8 * i, 8), at], csem.at[0])
        for i in range(groups_of_rows)
        for at in (pl.ds(0, depth // 4), pl.ds(depth // 4, depth // 4))
    ] + [
        pltpu.make_async_copy(cov_hbm, cov_ref, csem.at[1]),
        pltpu.make_async_copy(mask_hbm, mask_ref, csem.at[2]),
    ]
    arrivals = [pltpu.make_async_copy(perm_hbm, perm_ref, csem.at[0])] + small[2 * groups_of_rows:]
    plain = staged.reshape(cells_ref.shape)

    def load(c):
        return pltpu.make_async_copy(x_hbm.at[:, c], staged.at[c], lsem.at[c // 2])

    def settle(h):
        held = staged.at[pl.ds(2 * h, 2)]
        pltpu.make_async_copy(held, held, lsem.at[h]).wait()
        for c in range(2):
            at = pl.ds((2 * h + c) * depth, depth)
            pltpu.make_async_copy(plain.at[at], cells_ref.at[at], psem.at[h]).start()
        at = pl.ds(2 * h * depth, 2 * depth)
        pltpu.make_async_copy(plain.at[at], cells_ref.at[at], psem.at[h]).wait()

    for copy in small + [load(0)]:
        copy.start()

    barrier = pltpu.get_barrier_semaphore()
    for a in range(n):
        for o in range(m):
            if a + o:
                pl.semaphore_signal(
                    barrier, inc=1, device_id=(lax.rem(me + a, n), lax.rem(slab + o, m)), device_id_type=MESH)

    with jax.named_scope("perm_wait"):
        for copy in arrivals:
            copy.wait()
    load(1).start()
    sort_permutations(perm_ref, rank_ref)
    for c in range(2, 4):
        load(c).start()
    chunks = 4 * rank_ref.shape[0]
    span = depth // chunks

    def add_product(h, chunk):
        for k in range(2):
            at = chunk * span + k * (span // 2)
            part = jnp.concatenate(
                [cells_ref[pl.ds((2 * h + c) * depth + at, span // 2), :] for c in range(2)], axis=1)
            term = jnp.dot(
                des_ref[:, at : at + span // 2], part, preferred_element_type=jnp.float32)
            parts[k] = parts[k] + term if chunk else term

    left_over = list(range(chunks))

    def between(step):
        if step == 1:
            settle(0)
            for _ in range(2):
                add_product(0, left_over.pop(0))
        if step > 1:
            add_product(0, left_over.pop(0))

    with jax.named_scope("gather"):
        spread_designs(rank_ref, cov_ref, des_ref, flat_ref, turn_ref, between)

    def source(s):
        return lax.rem(me - s + n, n)

    odd = lax.rem(me, 2)
    far_first = [n - 1 - (n - 2) * odd, *range(2, n - 1), 1 + (n - 2) * odd]

    def exchange(src, box, send_sem, recv_sem):
        for o in far_first:
            to = lax.rem(me + o, n)
            pltpu.make_async_remote_copy(
                src_ref=src(to), dst_ref=box.at[o], send_sem=send_sem, recv_sem=recv_sem,
                device_id=(to, slab), device_id_type=MESH).start()
        rest = box.at[pl.ds(1, n - 1)]
        return pltpu.make_async_remote_copy(
            src_ref=rest, dst_ref=rest, send_sem=send_sem, recv_sem=recv_sem,
            device_id=(lax.rem(me + 1, n), slab), device_id_type=MESH)

    def multiply(h):
        for k in range(2):
            at = k * (depth // 2)
            part = jnp.concatenate(
                [cells_ref[pl.ds((2 * h + c) * depth + at, depth // 2), :] for c in range(2)], axis=1)
            parts[k] = jnp.dot(
                des_ref[:, at : at + depth // 2], part, preferred_element_type=jnp.float32)

    def spread_out(h):
        def piece(first, count):
            return parts[0, first : first + count] + parts[1, first : first + count]

        for g in range(n):
            q = g // share
            out[h, g, 0:24] = piece(24 * q, 24)
            out[h, g, 24:48] = piece(top + 24 * q, 24)
            out[h, g, 48:56] = piece(2 * top, 8)
        got[h, 0] = out[h, me]
        return exchange(lambda g: out.at[h, g], got.at[h], send.at[h], recv.at[h])

    with jax.named_scope("multiply_first"):
        for chunk in left_over:
            add_product(0, chunk)
    with jax.named_scope("entry_wait"):
        pl.semaphore_wait(barrier, n * m - 1)
    copies_t = [spread_out(0)]
    cross_design(flat_ref, cross_ref)
    out_x[...] = cross_ref[0] + cross_ref[1]
    copies_x = exchange(lambda g: out_x, got_x, xsend.at[0], xrecv.at[0])
    got_x[0] = out_x[...]

    with jax.named_scope("second_load_wait"):
        settle(1)
    with jax.named_scope("squares"):
        step = 256

        def square(k, totals):
            new = []
            for c in range(4):
                at = pl.ds(pl.multiple_of(c * depth + k * step, step), step)
                part = cells_ref[at, :].astype(jnp.float32)
                new.append(totals[c] + jnp.sum((part * part).reshape(step // 32, 4, 8, LANES), axis=0))
            return tuple(new)

        totals = lax.fori_loop(
            0, depth // step, square, tuple(jnp.zeros((4, 8, LANES), jnp.float32) for _ in range(4)))
        sub = lax.broadcasted_iota(jnp.int32, (8, LANES), 0)
        packed = jnp.zeros((8, LANES), jnp.float32)
        for c in range(4):
            total = jnp.sum(totals[c], axis=0)
            total = total + pltpu.roll(total, 4, 0)
            total = total + pltpu.roll(total, 2, 0)
            packed = jnp.where(sub // 2 == c, total, packed)
        out_q[...] = packed
        got_q[0] = packed
    copies_q = exchange(lambda g: out_q, got_q, qsend.at[0], qrecv.at[0])
    with jax.named_scope("multiply_second"):
        multiply(1)
        copies_t.append(spread_out(1))

    cells = mask_ref[...].astype(jnp.float32)

    with jax.named_scope("gram"):
        copies_x.wait()
        total_x = got_x[source(0)]
        for s in range(1, n):
            total_x = total_x + got_x[source(s)]
        gram = [[total_x[j : j + 1, top + i : top + i + 1] for j in range(4)] for i in range(4)]
        turned[...] = total_x.T
        mine_x = turned[pl.ds(pl.multiple_of(24 * (me // share), 8), 24), :]
        low_z = cholesky([row[1:4] for row in gram[1:4]])
        inv_z = [1.0 / low_z[i][i] for i in range(3)]
        low_f = cholesky(gram)
        inv_diag = [1.0 / low_f[i][i] for i in range(4)]
        unit = [jnp.zeros((1, 1), jnp.float32), jnp.ones((1, 1), jnp.float32)]
        columns = [cho_solve(low_f, inv_diag, [unit[int(i == j)] for i in range(4)]) for j in range(4)]
        inverse = [[columns[j][i] for j in range(4)] for i in range(4)]

    up = (me, lax.rem(slab + 1, m))
    down = (me, lax.rem(slab + m - 1, m))

    def halo(src, dst, h, k, to):
        return pltpu.make_async_remote_copy(
            src_ref=src.at[h], dst_ref=dst.at[h], send_sem=hsend.at[h, k], recv_sem=hrecv.at[h, k],
            device_id=to, device_id_type=MESH)

    rise = [halo(own, low, h, 0, up) for h in range(2)]
    fall = [halo(own, high, h, 1, down) for h in range(2)]

    @pl.when(slab == 0)
    def _():
        low[...] = jnp.zeros_like(low)

    @pl.when(slab == m - 1)
    def _():
        high[...] = jnp.zeros_like(high)

    own[...] = jnp.zeros_like(own)
    field[...] = jnp.zeros_like(field)

    for h in range(2):
        with jax.named_scope("take_in"):
            copies_t[h].wait()
            if h == 0:
                copies_q.wait()
                total_q = got_q[source(0)]
                for s in range(1, n):
                    total_q = total_q + got_q[source(s)]
        with jax.named_scope("statistic"):
            total = got[h, source(0)]
            for s in range(1, n):
                total = total + got[h, source(s)]
            for z in range(2):
                obs = total[48 + 4 * z : 52 + 4 * z]
                prod = [obs[k : k + 1] for k in range(4)]
                squares = jnp.concatenate(
                    [total_q[4 * h + 2 * c + z : 4 * h + 2 * c + z + 1] for c in range(2)], axis=1)
                fit = cho_solve(low_z, inv_z, prod[1:4])
                resid = squares - (prod[1] * fit[0] + prod[2] * fit[1] + prod[3] * fit[2])

                def statistic(proj):
                    slope = sum(inverse[0][k] * proj[k] for k in range(4))
                    quad = sum(proj[k] * sum(inverse[k][l] * proj[l] for l in range(4)) for k in range(4))
                    return slope / jnp.sqrt((resid - quad) / freedom * inverse[0][0])

                seen = [prod[k] - sum(gram[k][1 + i] * fit[i] for i in range(3)) for k in range(4)]
                mask_row = cells[z : z + 1, h * half_plane : (h + 1) * half_plane]
                line = statistic(seen) * mask_row
                for c in range(2):
                    own[h, 4, 2 * z + c : 2 * z + c + 1] = line[:, c * LANES : (c + 1) * LANES]
                proj = []
                for c in range(3):
                    first = 24 * z + 8 * c
                    proj.append(total[first : first + 8] - sum(
                        mine_x[8 * c : 8 * c + 8, 1 + i : 2 + i] * fit[i] for i in range(3)))
                block = statistic([proj[0], seen[1], proj[1], proj[2]]) * mask_row
                for c in range(2):
                    own[h, 2 * z + c] = block[:, c * LANES : (c + 1) * LANES]

        @pl.when(slab < m - 1)
        def _():
            rise[h].start()

        @pl.when(slab > 0)
        def _():
            fall[h].start()

    with jax.named_scope("halo_wait"):
        @pl.when(slab > 0)
        def _():
            for copy in rise:
                copy.wait_recv()

        @pl.when(slab < m - 1)
        def _():
            for copy in fall:
                copy.wait_recv()

    with jax.named_scope("blur"):
        def deep(pick):
            slices = []
            for ref in (low, own, high):
                for z in range(2):
                    slices.append(jnp.concatenate(
                        [pick(ref, h, 2 * z + c) for h in range(2) for c in range(2)], axis=1))
            return [
                sum(gauss_taps[position] * slices[position + z] for position in range(5))
                for z in range(2)
            ]

        first, second = deep(lambda ref, h, k: ref[h, k])
        field[0:8, :] = first
        field[8:16, :] = second
        first, second = deep(lambda ref, h, k: ref[h, 4, k : k + 1])
        field[16:17, :] = first
        field[17:18, :] = second

        cell = lax.broadcasted_iota(jnp.int32, (24, plane), 1)
        smooth = blur(field[...], PY, cell // PY, PX)
        smooth = blur(smooth, 1, cell % PY, PY)

        peaks = jnp.maximum(
            jnp.max(jnp.where(cells[0:1] > 0, smooth[0:8] * cells[0:1], -1e30), axis=1, keepdims=True),
            jnp.max(jnp.where(cells[1:2] > 0, smooth[8:16] * cells[1:2], -1e30), axis=1, keepdims=True),
        )
        lane = lax.broadcasted_iota(jnp.int32, (8, LANES), 1)
        line = jnp.sum(jnp.where(lane == sub, peaks, 0.0), axis=0, keepdims=True)
        peak_out[...] = line
        peak_in[0] = line
    side = 2 * slab // m
    targets = []
    for j in range(m):
        line_slab = side * j + (1 - side) * (m - 1 - j)
        targets += [(a, line_slab, lax.rem(line_slab - slab + m, m)) for a in range(n - 1, 0, -1)]
    targets += [(0, lax.rem(slab + o, m), o) for o in range(1, m)]
    for a, line_slab, o in targets:
        pltpu.make_async_remote_copy(
            src_ref=peak_out, dst_ref=peak_in.at[a * m + o], send_sem=psend.at[0], recv_sem=precv.at[0],
            device_id=(lax.rem(me + a, n), line_slab), device_id_type=MESH).start()
    rest = peak_in.at[pl.ds(1, n * m - 1)]
    copies_p = pltpu.make_async_remote_copy(
        src_ref=rest, dst_ref=rest, send_sem=psend.at[0], recv_sem=precv.at[0],
        device_id=(lax.rem(me + 1, n), slab), device_id_type=MESH)
    seen_t = [smooth[16 + z : 17 + z] * cells[z : z + 1] for z in range(2)]
    smooth_ref[...] = jnp.concatenate(seen_t, axis=0)

    with jax.named_scope("peak_wait"):
        copies_p.wait_recv()
    for a in range(n):
        best = peak_in[a * m]
        for o in range(1, m):
            best = jnp.maximum(best, peak_in[a * m + o])
        peak_ref[lax.rem(me - a + n, n)] = best

    with jax.named_scope("send_wait"):
        copies_p.wait_send()

        @pl.when(slab < m - 1)
        def _():
            for copy in rise:
                copy.wait_send()

        @pl.when(slab > 0)
        def _():
            for copy in fall:
                copy.wait_send()


def p_kernel(smooth_ref, peaks_ref, mask_ref, t_ref, pval_ref, line_ref):
    n = peaks_ref.shape[0]
    copies = line_ref.shape[1]
    groups = copies // 8
    share = n // groups
    cells = mask_ref[...].astype(jnp.float32)
    values = smooth_ref[...]
    t_ref[...] = values
    sub = lax.broadcasted_iota(jnp.int32, (8, LANES), 0)
    lane = lax.broadcasted_iota(jnp.int32, (8, LANES), 1)
    line = jnp.zeros((8, LANES), jnp.float32)
    counts = [jnp.zeros((8, values.shape[1]), jnp.float32) for _ in range(2)]
    for q in range(groups):
        best = peaks_ref[q * share]
        for s in range(1, share):
            best = jnp.maximum(best, peaks_ref[q * share + s])
        value = jnp.sum(jnp.where(lane == sub, best, 0.0), axis=1, keepdims=True)
        line = jnp.where(lane == sub + 8 * q, value, line)
        for z in range(2):
            counts[z] = counts[z] + jax.nn.sigmoid((value - values[z : z + 1]) / 0.2)
    total = [jnp.sum(count, axis=0, keepdims=True) for count in counts]
    pval_ref[...] = cells * (1.0 + jnp.concatenate(total, axis=0)) / (copies + 1)
    line_ref[...] = jnp.sum(line, axis=0, keepdims=True)[:, :copies]


def body(n, m, subjects_data, covariates, permutes, brain_mask):
    subj_rows, depth, plane = subjects_data.shape
    copies = permutes.shape[0]
    groups = copies // 8
    nest = 4 * LANES // copies * BLOCK
    assert depth == 2 and plane == PX * PY and n % groups == 0 and subj_rows % nest == 0
    lane_tiles = plane // LANES
    data = subjects_data.reshape(subj_rows, depth, lane_tiles, LANES).transpose(0, 2, 1, 3)
    f32 = jnp.float32
    bf16 = jnp.bfloat16
    vmem = pl.BlockSpec(memory_space=pltpu.VMEM)
    hbm = pl.BlockSpec(memory_space=pltpu.HBM)
    dma = pltpu.SemaphoreType.DMA
    tall = 3 * copies + 16
    data, covariates, permutes = (
        pltpu.with_memory_space_constraint(x, pltpu.HBM) for x in (data, covariates, permutes))
    smooth, peaks = pl.pallas_call(
        functools.partial(maps_kernel, n, m, float(n * subj_rows - 4)),
        in_specs=[hbm] * 4,
        out_specs=[vmem] * 2,
        out_shape=[pltpu.VMEM((depth, plane), f32), pltpu.VMEM((n, 1, LANES), f32)],
        scratch_shapes=[
            pltpu.VMEM((depth, plane), jnp.int32),
            pltpu.VMEM((lane_tiles, subj_rows, depth, LANES), bf16),
            pltpu.VMEM((lane_tiles * subj_rows * depth, LANES), bf16),
            pltpu.VMEM((3, subj_rows), bf16),
            pltpu.VMEM((copies, subj_rows), jnp.int32),
            pltpu.VMEM((subj_rows // nest, 8 * HALF, LANES), f32),
            pltpu.VMEM((subj_rows // nest * 8, HALF, LANES), jnp.int32),
            pltpu.VMEM((6 * copies + 16, 2 * subj_rows), bf16),
            pltpu.VMEM((tall, subj_rows), bf16),
            pltpu.VMEM((2, 8, LANES), f32),
            pltpu.VMEM((8, LANES), f32),
            pltpu.VMEM((n, 8, LANES), f32),
            pltpu.VMEM((8, LANES), f32),
            pltpu.VMEM((n, 8, LANES), f32),
            pltpu.VMEM((2, n, 56, plane // 2), f32),
            pltpu.VMEM((2, n, 56, plane // 2), f32),
            pltpu.VMEM((2, lane_tiles + 1, 8, LANES), f32),
            pltpu.VMEM((2, lane_tiles + 1, 8, LANES), f32),
            pltpu.VMEM((2, lane_tiles + 1, 8, LANES), f32),
            pltpu.VMEM((2, 6 * copies + 16, plane // 2), f32),
            pltpu.VMEM((24, plane), f32),
            pltpu.VMEM((1, LANES), f32),
            pltpu.VMEM((n * m, 1, LANES), f32),
            pltpu.VMEM((LANES, 8), f32),
            dma((2,)), dma((3,)), dma((2,)),
            dma((1,)), dma((1,)), dma((1,)), dma((1,)), dma((2,)), dma((2,)),
            dma((2, 2)), dma((2, 2)), dma((1,)), dma((1,)),
        ],
        compiler_params=pltpu.CompilerParams(
            collective_id=0, has_side_effects=True, vmem_limit_bytes=48 * 2**20
        ),
        name="maps",
    )(data, covariates, permutes, pltpu.with_memory_space_constraint(brain_mask, pltpu.HBM))
    smooth_t, p_values, line = pl.pallas_call(
        p_kernel,
        in_specs=[vmem] * 3,
        out_specs=[vmem] * 3,
        out_shape=[
            jax.ShapeDtypeStruct((depth, plane), f32),
            jax.ShapeDtypeStruct((depth, plane), f32),
            jax.ShapeDtypeStruct((1, copies), f32),
        ],
        compiler_params=pltpu.CompilerParams(vmem_limit_bytes=8 * 2**20),
        name="p_values",
    )(smooth, peaks, brain_mask)
    return smooth_t, p_values, line.reshape(copies)


def solution(mesh):
    return jax.shard_map(
        functools.partial(body, mesh.shape["subj"], mesh.shape["slab"]),
        mesh=mesh,
        in_specs=(P("subj", "slab", None), P(None, "subj"), P(None, "subj"), P("slab", None)),
        out_specs=(P("slab", None), P("slab", None), P()),
        check_vma=False,
    )
```
